32 devices in a mesh: section: 2 (over y), fsdp: 4 (over z), replica: 4 (over x, core).
Axes of the slice: x: 2, y: 2, z: 4, core: 2. Of those that a mesh axis runs over, the one named last changes fastest.
Arguments:
- inputs: bfloat16 [2, 4096, 2048], P(None, ('replica', 'fsdp')), may hold values from -6 to 6
- cotangent: bfloat16 [2, 4096, 2048], P(None, ('replica', 'fsdp')), may hold values from -6 to 6
- norm_gains: bfloat16 [2, 2, 2048], P('section'), may hold values from 0.099609375 to 1.8984375
- norm_biases: bfloat16 [2, 2, 2048], P('section'), may hold values from -1.5 to 1.5
- w_attn: bfloat16 [2, 2048, 2304], P('section', None, 'fsdp'), may hold values from -0.125 to 0.125
- w_out: bfloat16 [2, 2048, 2048], P('section', None, 'fsdp'), may hold values from -2 to 2
- w_up: bfloat16 [2, 2048, 8192], P('section', None, 'fsdp'), may hold values from -0.125 to 0.125
- w_down: bfloat16 [2, 8192, 2048], P('section', 'fsdp'), may hold values from -0.0625 to 0.0625
- down_attn: bfloat16 [2, 8, 16, 2048], P('section', None, None, 'fsdp'), may hold values from -0.125 to 0.125
- up_attn: bfloat16 [2, 8, 16, 2304], P('section', None, None, 'fsdp'), may hold values from -0.375 to 0.375
- down_out: bfloat16 [2, 8, 16, 2048], P('section', None, None, 'fsdp'), may hold values from -2 to 2
- up_out: bfloat16 [2, 8, 16, 2048], P('section', None, None, 'fsdp'), may hold values from -0.375 to 0.375
- down_up: bfloat16 [2, 8, 16, 2048], P('section', None, None, 'fsdp'), may hold values from -0.125 to 0.125
- up_up: bfloat16 [2, 8, 16, 8192], P('section', None, None, 'fsdp'), may hold values from -0.375 to 0.375
- down_down: bfloat16 [2, 8, 16, 8192], P('section', None, None, 'fsdp'), may hold values from -0.0625 to 0.0625
- up_down: bfloat16 [2, 8, 16, 2048], P('section', None, None, 'fsdp'), may hold values from -0.375 to 0.375
- seg_lengths: int32 [2, 4, 5], P(None, 'replica'), may hold values from 1 to 512, 1024 in all within a row
- parent_ids: int32 [2, 4, 5], P(None, 'replica'), may hold values from 0 to 3, as said below
- adapter_ids: int32 [2, 4, 1], P(None, 'replica'), may hold values from 0 to 7
Outputs:
- layer_outputs: bfloat16 [2, 2, 4096, 2048], P('section', None, ('replica', 'fsdp'))
- input_grads: bfloat16 [2, 2, 4096, 2048], P('section', None, ('replica', 'fsdp'))
- grad_down_attn: float32 [2, 8, 16, 2048], P('section', None, None, 'fsdp')
- grad_up_attn: float32 [2, 8, 16, 2304], P('section', None, None, 'fsdp')
- grad_down_out: float32 [2, 8, 16, 2048], P('section', None, None, 'fsdp')
- grad_up_out: float32 [2, 8, 16, 2048], P('section', None, None, 'fsdp')
- grad_down_up: float32 [2, 8, 16, 2048], P('section', None, None, 'fsdp')
- grad_up_up: float32 [2, 8, 16, 8192], P('section', None, None, 'fsdp')
- grad_down_down: float32 [2, 8, 16, 8192], P('section', None, None, 'fsdp')
- grad_up_down: float32 [2, 8, 16, 2048], P('section', None, None, 'fsdp')
The draws below stay inside these ranges and needn't reach their ends.
Inputs may be any that keep to these rules, and one draw needn't show every extreme that they name: `seg_lengths`: for every micro-batch and tree the 5 lengths sum to 1024. parent_ids[m,t,0] is 0; for k > 0, parent_ids[m,t,k] is below k. `adapter_ids`: every adapter index is used by some tree.
All inputs are finite; a program needn't handle non-finite values.
Results may differ from the reference program's by a relative error of at most 0.024.
Values may be sent and summed in bfloat16 or wider, within the bound.
No kernel may reach another device: no remote copies, remote signals or barrier semaphores. Data moves between devices by JAX's collectives and lax.ppermute only.
A program may use at most 448 MiB of HBM per device.

```python
import math
import jax
import jax.numpy as jnp
import numpy as np
from jax import lax

D = 2048
HEADS = 16
HEAD_DIM = 128
FF = 8192
RANK = 16
ADAPTERS = 8
SEGS = 5
MICRO = 2
TREE = 1024
TREES = 4


def draw_parent_ids(key, part):
    raw_bits = jax.random.randint(key, (MICRO, TREES, SEGS), 0, 1 << 20, dtype=jnp.int32)
    order = jnp.arange(SEGS, dtype=jnp.int32)
    parents = jnp.where(order > 0, raw_bits % jnp.maximum(order, 1), 0)
    return parents.at[0, 0, SEGS - 1].set(SEGS - 2).astype(jnp.int32)


def shard_levels(key, dims, cuts, smallest, largest):
    factor_of, own = 1.0, jax.random.fold_in(key, 6)
    for axis_at, parts in cuts:
        steps = jnp.exp(jax.random.uniform(jax.random.fold_in(own, axis_at), (parts,), jnp.float32, smallest / len(cuts), largest / len(cuts)))
        factor_of = factor_of * jnp.repeat(steps, dims[axis_at] // parts).reshape([-1 if axis == axis_at else 1 for axis in range(len(dims))])
    return factor_of


def choose_distinct(rng, rows, number_of, top, lift):
    order = jax.random.permutation(jax.random.fold_in(rng, 1), number_of)
    boost = order
    for power in range(3):
        boost = boost * boost // number_of
    boost = boost * lift // number_of
    tickets = jax.random.randint(jax.random.fold_in(rng, 2), (rows, number_of), 0, 4096) + boost
    fixed_rows = jax.random.permutation(jax.random.fold_in(rng, 3), rows)[jnp.arange(number_of) % rows]
    tickets = jnp.where(jnp.arange(rows)[:, None] == fixed_rows[None, :], 1 << 14, tickets)
    merit = tickets * number_of + jnp.arange(number_of)
    return lax.top_k(merit.astype(jnp.int32), top)[1].astype(jnp.int32)


def profile(number_of, total, limit, lean):
    portions = [(1 << 20) // math.isqrt(grade ** lean) + 1 for grade in range(2, number_of + 1)]
    surplus, holding = total - limit - (number_of - 1), [1] * (number_of - 1)
    while surplus > 0:
        candidates = [i for i in range(number_of - 1) if holding[i] < limit]
        pool, remaining = sum([portions[i] for i in candidates]), surplus
        for i in candidates:
            more = min(limit - holding[i], max(1, remaining * portions[i] // pool), surplus)
            holding[i] = holding[i] + more
            surplus = surplus - more
    return np.array([limit] + holding)


def uneven_parts(own_key, number_of, total, bound, skew):
    if number_of == 2:
        one = jax.random.randint(own_key, (), max(1, total - bound), min(bound, total - 1) + 1)
        return jnp.stack([one, total - one])
    tallies = jnp.asarray(profile(number_of, total, bound, skew), jnp.int32)
    twos = (number_of - 1) // 2
    donor, receiver = tallies[1:1 + 2 * twos:2], tallies[2:2 + 2 * twos:2]
    margin = jnp.minimum(donor - 1, bound - receiver)
    moved = jax.random.randint(jax.random.fold_in(own_key, 1), (twos,), 0, 1 << 20) % (margin + 1)
    tallies = tallies.at[1:1 + 2 * twos:2].set(donor - moved).at[2:2 + 2 * twos:2].set(receiver + moved)
    return tallies[jax.random.permutation(jax.random.fold_in(own_key, 2), number_of)]


def centred(key, extent, deviation, most, cuts=(), held_as=jnp.bfloat16):
    entries = jax.random.normal(key, extent, jnp.float32) * deviation
    if len(cuts) > 0:
        entries = shard_levels(key, extent, cuts, -0.22, 0.18) * entries
    return jnp.clip(entries, min=-most, max=most).astype(held_as)


def setup_inputs(seed: int = 0) -> dict:
    seeds = jax.random.split(jax.random.key(seed), 20)
    return {
        "inputs": centred(seeds[0], (MICRO, TREES * TREE, D), 1.0, 6.0, ((1, 16),)),
        "cotangent": centred(seeds[1], (MICRO, TREES * TREE, D), 1.0, 6.0, ((1, 16),)),
        "norm_gains": jnp.clip(1.0 + 0.18 * jax.random.normal(seeds[2], (2, 2, D), jnp.float32), 0.099609375, 1.8984375).astype(jnp.bfloat16),
        "norm_biases": centred(seeds[3], (2, 2, D), 0.3, 1.5, ((0, 2),)),
        "w_attn": centred(seeds[4], (2, D, D + 2 * HEAD_DIM), D ** -0.5, 0.125, ((0, 2), (2, 4))),
        "w_out": centred(seeds[5], (2, D, D), (max(D // 256, 2)) ** -0.5, 2.0, ((0, 2), (2, 4))),
        "w_up": centred(seeds[6], (2, D, FF), D ** -0.5, 0.125, ((0, 2), (2, 4))),
        "w_down": centred(seeds[7], (2, FF, D), FF ** -0.5, 0.0625, ((0, 2), (1, 4))),
        "down_attn": centred(seeds[8], (2, ADAPTERS, RANK, D), D ** -0.5, 0.125, ((0, 2), (3, 4))),
        "up_attn": centred(seeds[9], (2, ADAPTERS, RANK, D + 2 * HEAD_DIM), (RANK * RANK) ** -0.5, 0.375, ((0, 2), (3, 4))),
        "down_out": centred(seeds[10], (2, ADAPTERS, RANK, D), (max(D // 256, 2)) ** -0.5, 2.0, ((0, 2), (3, 4))),
        "up_out": centred(seeds[11], (2, ADAPTERS, RANK, D), (RANK * RANK) ** -0.5, 0.375, ((0, 2), (3, 4))),
        "down_up": centred(seeds[12], (2, ADAPTERS, RANK, D), D ** -0.5, 0.125, ((0, 2), (3, 4))),
        "up_up": centred(seeds[13], (2, ADAPTERS, RANK, FF), (RANK * RANK) ** -0.5, 0.375, ((0, 2), (3, 4))),
        "down_down": centred(seeds[14], (2, ADAPTERS, RANK, FF), FF ** -0.5, 0.0625, ((0, 2), (3, 4))),
        "up_down": centred(seeds[15], (2, ADAPTERS, RANK, D), (RANK * RANK) ** -0.5, 0.375, ((0, 2), (3, 4))),
        "seg_lengths": jax.vmap(lambda own: uneven_parts(own, SEGS, TREE, TREE // 2, 2))(jax.random.split(seeds[16], MICRO * TREES)).reshape((MICRO, TREES, SEGS)).astype(jnp.int32),
        "parent_ids": draw_parent_ids(jax.random.fold_in(seeds[19], 71), 0),
        "adapter_ids": choose_distinct(seeds[18], MICRO * TREES, ADAPTERS, 1, 0).reshape((MICRO, TREES, 1)),
    }


@jax.custom_vjp
def low(v):
    return lax.optimization_barrier(v.astype(jnp.bfloat16)).astype(jnp.float32)

@jax.custom_vjp
def low_back(v):
    return v

def low_keep(v):
    return (low(v), None)

def low_pass(kept, grad):
    return (grad,)

def back_keep(v):
    return (v, None)

def back_low(kept, grad):
    return (low(grad),)
low.defvjp(low_keep, low_pass)
low_back.defvjp(back_keep, back_low)
HIGH = lax.Precision.HIGHEST
ADAPTER_SCALING = 2.0
NORM_EPS = 1e-05
MASKED = -1e+30

def both_ways(tensor):
    return low(low_back(tensor))

def matrix_product(left_side, right_side):
    return jnp.dot(left_side, right_side, precision=HIGH, preferred_element_type=jnp.float32)

def layer_norm(value_rows, gain_vec, shift_vec):
    centre = value_rows - lax.optimization_barrier(jnp.mean(value_rows, axis=-1, keepdims=True))
    spread = lax.optimization_barrier(jnp.mean(centre * centre, axis=-1, keepdims=True))
    return centre * lax.rsqrt(spread + NORM_EPS) * gain_vec + shift_vec

def project(value_rows, weight_matrix, down_projector, up_projector):
    return matrix_product(value_rows, weight_matrix) + ADAPTER_SCALING * matrix_product(matrix_product(value_rows, down_projector.T), up_projector)

def segment_of(places, lengths):
    ends = jnp.cumsum(lengths, dtype=jnp.int32)
    return lax.optimization_barrier(jnp.sum((places[:, None] >= ends[None, :]).astype(jnp.int32), axis=1, dtype=jnp.int32))

def ancestry(parents):
    seg_ids = jnp.arange(parents.shape[0], dtype=jnp.int32)
    current = seg_ids
    reach = current[:, None] == seg_ids[None, :]
    for sweep in range(parents.shape[0] - 1):
        current = lax.optimization_barrier(jnp.sum(jnp.where(current[:, None] == seg_ids[None, :], parents[None, :], 0), axis=1, dtype=jnp.int32))
        reach = reach | (current[:, None] == seg_ids[None, :])
    return reach.astype(jnp.float32)

def permitted(seg_query, place_query, seg_key, place_key, ancestors):
    seg_ids = jnp.arange(ancestors.shape[0], dtype=jnp.int32)
    anc_rows = jnp.dot((seg_query[:, None] == seg_ids[None, :]).astype(jnp.float32), ancestors)
    reach = jnp.dot(anc_rows, (seg_key[:, None] == seg_ids[None, :]).astype(jnp.float32).T)
    return (reach > 0.5) & (place_key[None, :] <= place_query[:, None])

def attention(queries, key_mat, value_mat, segments, ancestors):
    block_rows = min(512, TREE)
    places = jnp.arange(TREE, dtype=jnp.int32)
    query_blocks = queries.reshape(TREE // block_rows, block_rows, HEADS, HEAD_DIM)
    seg_blocks = segments.reshape(TREE // block_rows, block_rows)
    place_blocks = places.reshape(TREE // block_rows, block_rows)

    def one_block(pieces):
        query_block, seg_block, place_block = pieces
        scores = jnp.einsum('rhd,kd->rhk', query_block, key_mat, precision=HIGH) * HEAD_DIM ** (-0.5)
        scores = low_back(scores)
        visible = permitted(seg_block, place_block, segments, places, ancestors)[:, None, :]
        scores = jnp.where(visible, scores, MASKED)
        attn_probs = jnp.exp(scores - jax.nn.logsumexp(scores, axis=-1, keepdims=True))
        mixed_out = jnp.einsum('rhk,kd->rhd', low(attn_probs), value_mat, precision=HIGH)
        return mixed_out.reshape(block_rows, D)
    return lax.map(jax.checkpoint(one_block), (query_blocks, seg_blocks, place_blocks)).reshape(TREE, D)

def layer(residual, weights, adapters, segments, ancestors):
    gain_one, shift_one, gain_two, shift_two, attn_weight, out_weight, up_weight, down_weight = weights
    attn_down, attn_up, proj_down, proj_up, widen_down, widen_up, narrow_down, narrow_up = adapters
    normed = both_ways(layer_norm(residual, gain_one, shift_one))
    joined_out = project(normed, attn_weight, attn_down, attn_up)
    queries = both_ways(joined_out[:, :D])
    key_mat = both_ways(joined_out[:, D:D + HEAD_DIM])
    value_mat = both_ways(joined_out[:, D + HEAD_DIM:])
    mixed_out = both_ways(attention(queries, key_mat, value_mat, segments, ancestors))
    middle = residual + low_back(project(mixed_out, out_weight, proj_down, proj_up))
    second = both_ways(layer_norm(middle, gain_two, shift_two))
    pre_act = low_back(project(second, up_weight, widen_down, widen_up))
    gelu_out = both_ways(jax.nn.gelu(pre_act, approximate=True))
    return middle + low_back(project(gelu_out, down_weight, narrow_down, narrow_up))

def reference(inputs, cotangent, norm_gains, norm_biases, w_attn, w_out, w_up, w_down, down_attn, up_attn, down_out, up_out, down_up, up_up, down_down, up_down, seg_lengths, parent_ids, adapter_ids):
    gains = norm_gains.astype(jnp.float32)
    shifts = norm_biases.astype(jnp.float32)
    frozen = [arr.astype(jnp.float32) for arr in (w_attn, w_out, w_up, w_down)]
    stacks = [arr.astype(jnp.float32) for arr in (down_attn, up_attn, down_out, up_out, down_up, up_up, down_down, up_down)]
    tree_total = MICRO * TREES
    tree_inputs = inputs.reshape(tree_total, TREE, D).astype(jnp.float32)
    tree_cots = cotangent.reshape(tree_total, TREE, D).astype(jnp.float32)
    lengths_all = seg_lengths.reshape(tree_total, SEGS)
    parents_all = parent_ids.reshape(tree_total, SEGS)
    chosen_all = adapter_ids.reshape(tree_total)

    def section_weights(section_at):
        return (gains[section_at, 0], shifts[section_at, 0], gains[section_at, 1], shifts[section_at, 1]) + tuple((arr[section_at] for arr in frozen))

    def one_tree(totals, pieces):
        tree_in, tree_cot, lengths, parents, chosen = pieces
        segments = segment_of(jnp.arange(TREE, dtype=jnp.int32), lengths)
        ancestors = ancestry(parents)
        picked = [tuple((lax.dynamic_index_in_dim(arr[section_at], chosen, 0, keepdims=False) for arr in stacks)) for section_at in range(2)]
        first_out, back_first = jax.vjp(lambda residual, adapters: layer(residual, section_weights(0), adapters, segments, ancestors), tree_in, picked[0])
        between = low(first_out)
        last_out, back_last = jax.vjp(lambda residual, adapters: layer(residual, section_weights(1), adapters, segments, ancestors), between, picked[1])
        grad_between, grads_last = back_last(tree_cot)
        grad_between = low(grad_between)
        grad_in, grads_first = back_first(grad_between)
        new_totals = []
        for slot_index, running in enumerate(totals):
            for section_at, grad_list in ((0, grads_first), (1, grads_last)):
                slab = lax.dynamic_index_in_dim(running[section_at], chosen, 0, keepdims=False) + grad_list[slot_index]
                running = running.at[section_at].set(lax.dynamic_update_index_in_dim(running[section_at], slab, chosen, 0))
            new_totals.append(running)
        return (tuple(new_totals), (between, low(last_out), grad_in, grad_between))
    start_totals = tuple((jnp.zeros(arr.shape, jnp.float32) for arr in stacks))
    totals, outs = lax.scan(one_tree, start_totals, (tree_inputs, tree_cots, lengths_all, parents_all, chosen_all))
    firsts, lasts, grads_in, grads_between = outs
    layer_outputs = jnp.stack([firsts, lasts]).reshape(2, MICRO, TREES * TREE, D).astype(jnp.bfloat16)
    input_grads = jnp.stack([grads_in, grads_between]).reshape(2, MICRO, TREES * TREE, D).astype(jnp.bfloat16)
    return (layer_outputs, input_grads, totals[0], totals[1], totals[2], totals[3], totals[4], totals[5], totals[6], totals[7])
```

```python
import functools
import math

import jax
import jax.numpy as jnp
from jax import lax
from jax.experimental import pallas as pl
from jax.experimental.pallas import tpu as pltpu
from jax.sharding import PartitionSpec as P

D = 2048
HEADS = 16
HEAD_DIM = 128
RANK = 16

NORM_EPS = 1e-05
MASKED = -1e30
BF = jnp.bfloat16
F32 = jnp.float32
INV_ROOT = HEAD_DIM ** (-0.5)
LOG2E = math.log2(math.e)
LN2 = math.log(2.0)
GELU_C = math.sqrt(2.0 / math.pi)
VMEM_LIMIT = 56 * 1024 * 1024

NN = (((1,), (0,)), ((), ()))
NT = (((1,), (1,)), ((), ()))
TN = (((0,), (0,)), ((), ()))


def dot(left, right, dims=NN):
    return lax.dot_general(left, right, dims, preferred_element_type=F32)


def params(steps=1):
    return pltpu.CompilerParams(
        dimension_semantics=("arbitrary",) * steps, vmem_limit_bytes=VMEM_LIMIT
    )


def layer_norm(rows, gain, shift):
    centre = rows - jnp.mean(rows, axis=-1, keepdims=True)
    spread = jnp.mean(centre * centre, axis=-1, keepdims=True)
    return centre * lax.rsqrt(spread + NORM_EPS) * gain + shift


def layer_norm_back(rows, gain, grad):
    centre = rows - jnp.mean(rows, axis=-1, keepdims=True)
    spread = jnp.mean(centre * centre, axis=-1, keepdims=True)
    scale = lax.rsqrt(spread + NORM_EPS)
    unit = centre * scale
    inner = grad * gain
    return scale * (
        inner
        - jnp.mean(inner, axis=-1, keepdims=True)
        - unit * jnp.mean(inner * unit, axis=-1, keepdims=True)
    )


def tree_mask(rows, per_tree):
    row = lax.broadcasted_iota(jnp.int32, (rows, (rows // per_tree) * RANK), 0)
    col = lax.broadcasted_iota(jnp.int32, (rows, (rows // per_tree) * RANK), 1)
    return (row // per_tree) == (col // RANK)


def masked(value, per_tree):
    return jnp.where(tree_mask(value.shape[0], per_tree), 2.0 * value, 0.0).astype(BF)


def attention_forward_kernel(blocks, heads, q_ref, *refs):
    kv_refs, (bias_ref, o_ref, lse_ref) = refs[:blocks], refs[blocks:]
    keys = jnp.concatenate([r[:, :HEAD_DIM] for r in kv_refs], axis=0)
    vals = jnp.concatenate([r[:, HEAD_DIM:] for r in kv_refs], axis=0).T
    for h in range(heads):
        cols = slice(h * HEAD_DIM, (h + 1) * HEAD_DIM)
        scores = dot(keys, q_ref[:, cols], NT) + bias_ref[...]
        top = jnp.max(scores, axis=0, keepdims=True)
        probs = jnp.exp2(scores - top)
        total = jnp.sum(probs, axis=0, keepdims=True)
        mixed = dot(vals, probs.astype(BF)) * (1.0 / total)
        o_ref[:, cols] = mixed.T.astype(BF)
        lse_ref[0, h : h + 1, :] = top + jnp.log2(total)


def attention_forward(q, kv, bias, heads=4):
    rows = q.shape[0]
    blocks = len(kv)
    wide = heads * HEAD_DIM
    steps = HEADS // heads
    whole = lambda i: (0, 0)
    return pl.pallas_call(
        functools.partial(attention_forward_kernel, blocks, heads),
        grid=(steps,),
        in_specs=[pl.BlockSpec((rows, wide), lambda i: (0, i))]
        + [pl.BlockSpec((rows, 2 * HEAD_DIM), whole)] * blocks
        + [pl.BlockSpec((blocks * rows, rows), whole)],
        out_specs=[
            pl.BlockSpec((rows, wide), lambda i: (0, i)),
            pl.BlockSpec((1, heads, rows), lambda i: (i, 0, 0)),
        ],
        out_shape=[
            jax.ShapeDtypeStruct((rows, D), BF),
            jax.ShapeDtypeStruct((steps, heads, rows), F32),
        ],
        compiler_params=params(),
        cost_estimate=pl.CostEstimate(
            flops=4 * rows * rows * blocks * D,
            transcendentals=rows * rows * blocks * HEADS,
            bytes_accessed=4 * rows * D + 4 * rows * rows * blocks,
        ),
        name="attention_forward",
    )(q, *kv, bias)


def attention_backward_kernel(blocks, heads, q_ref, do_ref, o_ref, *refs):
    kv_refs = refs[:blocks]
    bias_ref, lse_ref, dq_ref, dkv_ref, acc_ref = refs[blocks:]
    rows = q_ref.shape[0]
    step = pl.program_id(0)

    @pl.when(step == 0)
    def _():
        acc_ref[...] = jnp.zeros_like(acc_ref)

    keys = jnp.concatenate([r[:, :HEAD_DIM] for r in kv_refs], axis=0)
    vals = jnp.concatenate([r[:, HEAD_DIM:] for r in kv_refs], axis=0)
    keys_t = keys.T
    for h in range(heads):
        cols = slice(h * HEAD_DIM, (h + 1) * HEAD_DIM)
        q, do = q_ref[:, cols], do_ref[:, cols]
        delta = jnp.sum(
            (do.astype(F32) * o_ref[:, cols].astype(F32)).T, axis=0, keepdims=True
        )
        scores = dot(keys, q, NT) + bias_ref[...]
        probs = jnp.exp2(scores - lse_ref[0, h : h + 1, :])
        dprobs = dot(vals, do, NT)
        dscores = (probs * (dprobs - delta)).astype(BF)
        acc_ref[:, :HEAD_DIM] += dot(dscores, q)
        acc_ref[:, HEAD_DIM:] += dot(probs.astype(BF), do)
        dq_ref[:, cols] = (dot(keys_t, dscores) * INV_ROOT).T.astype(BF)

    @pl.when(step == pl.num_programs(0) - 1)
    def _():
        for s in range(blocks):
            part = slice(s * rows, (s + 1) * rows)
            dkv_ref[s, :, :HEAD_DIM] = (acc_ref[part, :HEAD_DIM] * LN2).astype(BF)
            dkv_ref[s, :, HEAD_DIM:] = acc_ref[part, HEAD_DIM:].astype(BF)


def attention_backward(q, do, o, kv, bias, lse, heads=4):
    rows = q.shape[0]
    blocks = len(kv)
    wide = heads * HEAD_DIM
    steps = HEADS // heads
    whole = lambda i: (0, 0)
    return pl.pallas_call(
        functools.partial(attention_backward_kernel, blocks, heads),
        grid=(steps,),
        in_specs=[pl.BlockSpec((rows, wide), lambda i: (0, i))] * 3
        + [pl.BlockSpec((rows, 2 * HEAD_DIM), whole)] * blocks
        + [
            pl.BlockSpec((blocks * rows, rows), whole),
            pl.BlockSpec((1, heads, rows), lambda i: (i, 0, 0)),
        ],
        out_specs=[
            pl.BlockSpec((rows, wide), lambda i: (0, i)),
            pl.BlockSpec((blocks, rows, 2 * HEAD_DIM), lambda i: (0, 0, 0)),
        ],
        out_shape=[
            jax.ShapeDtypeStruct((rows, D), BF),
            jax.ShapeDtypeStruct((blocks, rows, 2 * HEAD_DIM), BF),
        ],
        scratch_shapes=[pltpu.VMEM((blocks * rows, 2 * HEAD_DIM), F32)],
        compiler_params=params(),
        cost_estimate=pl.CostEstimate(
            flops=10 * rows * rows * blocks * D,
            transcendentals=rows * rows * blocks * HEADS,
            bytes_accessed=8 * rows * D + 4 * rows * rows * blocks,
        ),
        name="attention_backward",
    )(q, do, o, *kv, bias, lse)


def mlp_forward_kernel(
    per_tree, b_ref, x2_ref, wu_ref, wd_ref, upu_ref, dnd_ref, dnu_ref, upd_ref,
    y_ref, g_ref, gp_ref, u3_ref, u4_ref, acc_ref,
):
    step = pl.program_id(0)

    @pl.when(step == 0)
    def _():
        u3_ref[...] = masked(dot(b_ref[...], dnu_ref[...], NT), per_tree)
        y_ref[...] = x2_ref[...]
        acc_ref[...] = jnp.zeros_like(acc_ref)

    f = dot(b_ref[...], wu_ref[0]) + dot(u3_ref[...], upu_ref[...])
    square = f * f
    bend = jnp.tanh(GELU_C * f * (1.0 + 0.044715 * square))
    half = 0.5 * (1.0 + bend)
    g = (f * half).astype(BF)
    g_ref[...] = g
    gp_ref[...] = (
        half
        + 0.5 * f * (1.0 - bend * bend) * (GELU_C * (1.0 + 3 * 0.044715 * square))
    ).astype(BF)
    y_ref[...] += dot(g, wd_ref[...])
    acc_ref[...] += dot(g, dnd_ref[...], NT)

    @pl.when(step == pl.num_programs(0) - 1)
    def _():
        u4 = masked(acc_ref[...], per_tree)
        u4_ref[...] = u4
        y_ref[...] += dot(u4, upd_ref[...])


def mlp_forward(b, x2, w_up, w_down, up_up, down_down, down_up, up_down, block=512):
    rows = b.shape[0]
    shards, _, part = w_up.shape
    hidden = shards * part
    trees = down_up.shape[0] // RANK
    wide = trees * RANK
    block = min(block, part)
    per = part // block
    once = lambda j: (0, 0)
    return pl.pallas_call(
        functools.partial(mlp_forward_kernel, rows // trees),
        grid=(hidden // block,),
        in_specs=[
            pl.BlockSpec((rows, D), once, pipeline_mode=pl.Buffered(1)),
            pl.BlockSpec((rows, D), once, pipeline_mode=pl.Buffered(1)),
            pl.BlockSpec((1, D, block), lambda j: (j // per, 0, j % per)),
            pl.BlockSpec((block, D), lambda j: (j, 0)),
            pl.BlockSpec((wide, block), lambda j: (0, j)),
            pl.BlockSpec((wide, block), lambda j: (0, j)),
            pl.BlockSpec((wide, D), once),
            pl.BlockSpec((wide, D), once),
        ],
        out_specs=[
            pl.BlockSpec((rows, D), once),
            pl.BlockSpec((rows, block), lambda j: (0, j)),
            pl.BlockSpec((rows, block), lambda j: (0, j)),
            pl.BlockSpec((rows, wide), once),
            pl.BlockSpec((rows, wide), once),
        ],
        out_shape=[
            jax.ShapeDtypeStruct((rows, D), F32),
            jax.ShapeDtypeStruct((rows, hidden), BF),
            jax.ShapeDtypeStruct((rows, hidden), BF),
            jax.ShapeDtypeStruct((rows, wide), BF),
            jax.ShapeDtypeStruct((rows, wide), BF),
        ],
        scratch_shapes=[pltpu.VMEM((rows, wide), F32)],
        compiler_params=params(),
        cost_estimate=pl.CostEstimate(
            flops=4 * rows * D * hidden,
            transcendentals=rows * hidden,
            bytes_accessed=4 * D * hidden + 4 * rows * hidden + 10 * rows * D,
        ),
        name="mlp_forward",
    )(b, x2, w_up, w_down, up_up, down_down, down_up, up_down)


def mlp_backward_kernel(
    per_tree, dy_ref, b_ref, x2_ref, gain_ref, wu_ref, wd_ref, g_ref, gp_ref, u3_ref, u4_ref,
    upu_ref, dnd_ref, dnu_ref, upd_ref,
    dx2_ref, gupu_ref, gdnd_ref, gdnu_ref, gupd_ref,
    dm_ref, du4_ref, du3_ref,
):
    step = pl.program_id(0)

    @pl.when(step == 0)
    def _():
        dm = dy_ref[...].astype(BF)
        dm_ref[...] = dm
        du4_ref[...] = masked(dot(dm, upd_ref[...], NT), per_tree)
        gupd_ref[...] = dot(u4_ref[...], dm, TN)
        dx2_ref[...] = jnp.zeros_like(dx2_ref)
        du3_ref[...] = jnp.zeros_like(du3_ref)

    du4 = du4_ref[...]
    dg = dot(dm_ref[...], wd_ref[...], NT) + dot(du4, dnd_ref[...])
    df = (gp_ref[...].astype(F32) * dg).astype(BF)
    gdnd_ref[...] = dot(du4, g_ref[...], TN)
    gupu_ref[...] = dot(u3_ref[...], df, TN)
    du3_ref[...] += dot(df, upu_ref[...], NT)
    dx2_ref[...] += dot(df, wu_ref[0], NT)

    @pl.when(step == pl.num_programs(0) - 1)
    def _():
        du3 = masked(du3_ref[...], per_tree)
        gdnu_ref[...] = dot(du3, b_ref[...], TN)
        db = (dx2_ref[...] + dot(du3, dnu_ref[...])).astype(BF).astype(F32)
        dx2_ref[...] = dy_ref[...] + layer_norm_back(x2_ref[...], gain_ref[...], db)


def mlp_backward(
    dy, b, x2, gain, w_up, w_down, g, gp, u3, u4, up_up, down_down, down_up, up_down, block=512
):
    rows = b.shape[0]
    shards, _, part = w_up.shape
    hidden = shards * part
    trees = down_up.shape[0] // RANK
    wide = trees * RANK
    block = min(block, part)
    per = part // block
    once = lambda j: (0, 0)
    single = pl.Buffered(1)
    return pl.pallas_call(
        functools.partial(mlp_backward_kernel, rows // trees),
        grid=(hidden // block,),
        in_specs=[
            pl.BlockSpec((rows, D), once, pipeline_mode=single),
            pl.BlockSpec((rows, D), once, pipeline_mode=single),
            pl.BlockSpec((rows, D), once, pipeline_mode=single),
            pl.BlockSpec((1, D), once),
            pl.BlockSpec((1, D, block), lambda j: (j // per, 0, j % per)),
            pl.BlockSpec((block, D), lambda j: (j, 0)),
            pl.BlockSpec((rows, block), lambda j: (0, j)),
            pl.BlockSpec((rows, block), lambda j: (0, j)),
            pl.BlockSpec((rows, wide), once),
            pl.BlockSpec((rows, wide), once),
            pl.BlockSpec((wide, block), lambda j: (0, j)),
            pl.BlockSpec((wide, block), lambda j: (0, j)),
            pl.BlockSpec((wide, D), once),
            pl.BlockSpec((wide, D), once),
        ],
        out_specs=[
            pl.BlockSpec((rows, D), once),
            pl.BlockSpec((wide, block), lambda j: (0, j)),
            pl.BlockSpec((wide, block), lambda j: (0, j)),
            pl.BlockSpec((wide, D), once),
            pl.BlockSpec((wide, D), once),
        ],
        out_shape=[
            jax.ShapeDtypeStruct((rows, D), F32),
            jax.ShapeDtypeStruct((wide, hidden), F32),
            jax.ShapeDtypeStruct((wide, hidden), F32),
            jax.ShapeDtypeStruct((wide, D), F32),
            jax.ShapeDtypeStruct((wide, D), F32),
        ],
        scratch_shapes=[
            pltpu.VMEM((rows, D), BF),
            pltpu.VMEM((rows, wide), BF),
            pltpu.VMEM((rows, wide), F32),
        ],
        compiler_params=params(),
        cost_estimate=pl.CostEstimate(
            flops=4 * rows * D * hidden,
            transcendentals=0,
            bytes_accessed=4 * D * hidden + 4 * rows * hidden + 14 * rows * D,
        ),
        name="mlp_backward",
    )(dy, b, x2, gain, w_up, w_down, g, gp, u3, u4, up_up, down_down, down_up, up_down)


def segment_of(places, lengths):
    order = jnp.arange(lengths.shape[0], dtype=jnp.int32)
    ends = jnp.sum(
        jnp.where(order[None, :] <= order[:, None], lengths[None, :], 0), axis=1, dtype=jnp.int32
    )
    return jnp.sum((places[:, None] >= ends[None, :]).astype(jnp.int32), axis=1, dtype=jnp.int32)


def ancestry(parents):
    seg_ids = jnp.arange(parents.shape[0], dtype=jnp.int32)
    current = seg_ids
    reach = current[:, None] == seg_ids[None, :]
    for sweep in range(parents.shape[0] - 1):
        current = jnp.sum(
            jnp.where(current[:, None] == seg_ids[None, :], parents[None, :], 0),
            axis=1,
            dtype=jnp.int32,
        )
        reach = reach | (current[:, None] == seg_ids[None, :])
    return reach.astype(BF)


def key_bias(lengths, parents, query_places, key_places):
    seg_ids = jnp.arange(parents.shape[0], dtype=jnp.int32)
    of_query = (segment_of(query_places, lengths)[:, None] == seg_ids[None, :]).astype(BF)
    of_key = (segment_of(key_places, lengths)[:, None] == seg_ids[None, :]).astype(BF)
    reach = dot(of_key, dot(of_query, ancestry(parents)).astype(BF), NT)
    allowed = (
        (reach > 0.5)
        & (key_places[:, None] <= query_places[None, :])
        & (key_places[:, None] >= 0)
    )
    return jnp.where(allowed, 0.0, MASKED).astype(F32)


def local(
    inputs, cotangent, norm_gains, norm_biases, w_attn, w_out, w_up, w_down,
    down_attn, up_attn, down_out, up_out, down_up, up_up, down_down, up_down,
    seg_lengths, parent_ids, adapter_ids,
):
    section = lax.axis_index("section")
    shard = lax.axis_index("fsdp")
    member = lax.axis_index("replica")
    shards = lax.axis_size("fsdp")
    members = lax.axis_size("replica")
    trees, per_tree = inputs.shape[0], inputs.shape[1]
    rows = trees * per_tree
    gain = norm_gains[0].astype(F32)
    shift = norm_biases[0].astype(F32)

    def gathered(weight):
        part = weight.shape[0] // members
        own = lax.dynamic_slice_in_dim(weight, member * part, part, 0)
        return lax.all_gather(own, ("fsdp", "replica"), axis=0, tiled=True)

    stacks = (down_attn, up_attn, down_out, up_out, down_up, up_up, down_down, up_down)
    widths = [stack.shape[3] for stack in stacks]
    starts = [sum(widths[:i]) for i in range(len(widths))]
    chosen = adapter_ids[:, 0, 0]
    picked = jnp.concatenate(
        [
            jnp.concatenate(
                [lax.dynamic_index_in_dim(stack[0], chosen[m], 0, keepdims=False) for m in range(trees)],
                axis=0,
            )
            for stack in stacks
        ],
        axis=1,
    )
    maps = lax.all_gather(picked, "fsdp", axis=0)
    maps = [
        jnp.moveaxis(maps[:, :, at : at + width], 0, 1).reshape(trees * RANK, shards * width)
        for at, width in zip(starts, widths)
    ]
    dn_attn, up_attn_, dn_out, up_out_, dn_up, up_up_, dn_down, up_down_ = maps

    attn_parts = gathered(w_attn[0]).reshape(shards, D, w_attn.shape[2])
    attn_full = jnp.moveaxis(attn_parts, 0, 1).reshape(D, shards * w_attn.shape[2])
    w_q, w_kv = attn_full[:, :D], attn_full[:, D:]
    out_parts = gathered(w_out[0]).reshape(shards, D, w_out.shape[2])
    out_full = jnp.moveaxis(out_parts, 0, 1).reshape(D, D)
    up_parts = gathered(w_up[0]).reshape(shards, D, w_up.shape[2])
    down_full = gathered(w_down[0])
    owners = lax.all_gather(chosen, "replica", axis=0, tiled=True)

    query_places = shard * per_tree + jnp.arange(per_tree, dtype=jnp.int32)
    key_places = jnp.concatenate(
        [(shard - s) * per_tree + jnp.arange(per_tree, dtype=jnp.int32) for s in range(shards)]
    )
    biases = [
        key_bias(seg_lengths[m, 0], parent_ids[m, 0], query_places, key_places)
        for m in range(trees)
    ]

    def tree(value, m):
        return value[m * per_tree : (m + 1) * per_tree]

    def to_higher(value, steps):
        return lax.ppermute(value, "fsdp", [(i, i + steps) for i in range(shards - steps)])

    def to_lower(value, steps):
        return lax.ppermute(value, "fsdp", [(i + steps, i) for i in range(shards - steps)])

    def forward(x):
        a = layer_norm(x, gain[0], shift[0]).astype(BF)
        u1 = masked(dot(a, dn_attn, NT), per_tree)
        kv = (dot(a, w_kv) + dot(u1, up_attn_[:, D:])).astype(BF)
        kv_blocks = [
            [tree(kv, m)] + [to_higher(tree(kv, m), s) for s in range(1, shards)]
            for m in range(trees)
        ]
        q = ((dot(a, w_q) + dot(u1, up_attn_[:, :D])) * (INV_ROOT * LOG2E)).astype(BF)
        mixed = [attention_forward(tree(q, m), kv_blocks[m], biases[m]) for m in range(trees)]
        o = jnp.concatenate([part[0] for part in mixed], axis=0)
        u2 = masked(dot(o, dn_out, NT), per_tree)
        x2 = x + (dot(o, out_full) + dot(u2, up_out_))
        b = layer_norm(x2, gain[1], shift[1]).astype(BF)
        y, g, gp, u3, u4 = mlp_forward(
            b, x2, up_parts, down_full, up_up_, dn_down, dn_up, up_down_
        )
        kept = (x, a, u1, q, kv_blocks, mixed, o, u2, x2, b, g, gp, u3, u4)
        return y.astype(BF), kept

    def backward(dy, kept):
        x, a, u1, q, kv_blocks, mixed, o, u2, x2, b, g, gp, u3, u4 = kept
        dx2, g_up_up, g_dn_down, g_dn_up, g_up_down = mlp_backward(
            dy, b, x2, gain[1:2], up_parts, down_full, g, gp, u3, u4,
            up_up_, dn_down, dn_up, up_down_,
        )
        dr = dx2.astype(BF)
        du2 = masked(dot(dr, up_out_, NT), per_tree)
        do = (dot(dr, out_full, NT) + dot(du2, dn_out)).astype(BF)
        g_up_out = dot(u2, dr, TN)
        g_dn_out = dot(du2, o, TN)
        joined = []
        for m in range(trees):
            dq, dkv = attention_backward(
                tree(q, m), tree(do, m), tree(o, m), kv_blocks[m], biases[m], mixed[m][1]
            )
            total = dkv[0].astype(F32)
            for s in range(1, shards):
                total = total + to_lower(dkv[s], s).astype(F32)
            joined.append(jnp.concatenate([dq, total.astype(BF)], axis=1))
        joined = jnp.concatenate(joined, axis=0)
        du1 = masked(dot(joined, up_attn_, NT), per_tree)
        da = (dot(joined, attn_full, NT) + dot(du1, dn_attn)).astype(BF).astype(F32)
        g_up_attn = dot(u1, joined, TN)
        g_dn_attn = dot(du1, a, TN)
        dx = dx2 + layer_norm_back(x, gain[0], da)
        grads = (
            g_dn_attn, g_up_attn, g_dn_out, g_up_out, g_dn_up, g_up_up, g_dn_down, g_up_down
        )
        return dx.astype(BF), grads

    own = inputs.reshape(rows, D)
    first, _ = forward(own.astype(F32))
    arrived = lax.ppermute(first, "section", [(0, 1)])
    layer_out, kept = forward(jnp.where(section == 0, own, arrived).astype(F32))

    own_grad = cotangent.reshape(rows, D)
    last, _ = backward(own_grad.astype(F32), kept)
    arrived = lax.ppermute(last, "section", [(1, 0)])
    in_grad, grads = backward(jnp.where(section == 1, own_grad, arrived).astype(F32), kept)

    slabs = jnp.concatenate(
        [
            grad.astype(BF).reshape(trees * RANK, shards, width)
            for grad, width in zip(grads, widths)
        ],
        axis=2,
    )
    slabs = lax.psum_scatter(
        jnp.moveaxis(slabs, 1, 0), "fsdp", scatter_dimension=0, tiled=False
    )
    slabs = lax.all_gather(slabs, "replica", axis=0)
    slabs = slabs.reshape(members * trees, RANK * sum(widths))
    adapters = down_attn.shape[1]
    pick = (jnp.arange(adapters, dtype=jnp.int32)[:, None] == owners[None, :]).astype(BF)
    totals = dot(pick, slabs).reshape(adapters, RANK, sum(widths))
    finals = [
        totals[None, :, :, at : at + width] for at, width in zip(starts, widths)
    ]
    return (
        layer_out.reshape(1, trees, per_tree, D),
        in_grad.reshape(1, trees, per_tree, D),
        *finals,
    )


def solution(mesh):
    rows = P(None, ("replica", "fsdp"), None)
    stack = P("section", None, None, "fsdp")
    placed = (
        (rows, rows)
        + (P("section", None, None),) * 2
        + (P("section", None, "fsdp"),) * 3
        + (P("section", "fsdp", None),)
        + (stack,) * 8
        + (P(None, "replica", None),) * 3
    )
    return jax.shard_map(
        local,
        mesh=mesh,
        in_specs=placed,
        out_specs=(P("section", None, ("replica", "fsdp"), None),) * 2 + (stack,) * 8,
        check_vma=False,
    )
```

```python
import functools
import math

import jax
import jax.numpy as jnp
from jax import lax
from jax.experimental import pallas as pl
from jax.experimental.pallas import tpu as pltpu
from jax.sharding import PartitionSpec as P

D = 2048
HEADS = 16
HEAD_DIM = 128
RANK = 16

NORM_EPS = 1e-05
MASKED = -1e30
BF = jnp.bfloat16
F32 = jnp.float32
INV_ROOT = HEAD_DIM ** (-0.5)
LOG2E = math.log2(math.e)
LN2 = math.log(2.0)
GELU_C = math.sqrt(2.0 / math.pi)
VMEM_LIMIT = 56 * 1024 * 1024

NN = (((1,), (0,)), ((), ()))
NT = (((1,), (1,)), ((), ()))
TN = (((0,), (0,)), ((), ()))


def dot(left, right, dims=NN):
    return lax.dot_general(left, right, dims, preferred_element_type=F32)


def params(steps=1):
    return pltpu.CompilerParams(
        dimension_semantics=("arbitrary",) * steps, vmem_limit_bytes=VMEM_LIMIT
    )


def layer_norm(rows, gain, shift):
    centre = rows - jnp.mean(rows, axis=-1, keepdims=True)
    spread = jnp.mean(centre * centre, axis=-1, keepdims=True)
    return centre * lax.rsqrt(spread + NORM_EPS) * gain + shift


def layer_norm_back(rows, gain, grad):
    centre = rows - jnp.mean(rows, axis=-1, keepdims=True)
    spread = jnp.mean(centre * centre, axis=-1, keepdims=True)
    scale = lax.rsqrt(spread + NORM_EPS)
    unit = centre * scale
    inner = grad * gain
    return scale * (
        inner
        - jnp.mean(inner, axis=-1, keepdims=True)
        - unit * jnp.mean(inner * unit, axis=-1, keepdims=True)
    )


def tree_mask(rows, per_tree):
    row = lax.broadcasted_iota(jnp.int32, (rows, (rows // per_tree) * RANK), 0)
    col = lax.broadcasted_iota(jnp.int32, (rows, (rows // per_tree) * RANK), 1)
    return (row // per_tree) == (col // RANK)


def masked(value, per_tree):
    return jnp.where(tree_mask(value.shape[0], per_tree), 2.0 * value, 0.0).astype(BF)


def attention_forward_kernel(blocks, heads, q_ref, *refs):
    kv_refs, (bias_ref, o_ref, lse_ref) = refs[:blocks], refs[blocks:]
    keys = jnp.concatenate([r[:, :HEAD_DIM] for r in kv_refs], axis=0)
    vals = jnp.concatenate([r[:, HEAD_DIM:] for r in kv_refs], axis=0)
    vals = jnp.concatenate([vals, jnp.ones_like(vals)], axis=1)
    for h in range(heads):
        cols = slice(h * HEAD_DIM, (h + 1) * HEAD_DIM)
        scores = dot(q_ref[:, cols], keys, NT) + bias_ref[...]
        top = jnp.max(scores, axis=1, keepdims=True)
        probs = jnp.exp2(scores - top)
        mixed = dot(probs.astype(BF), vals)
        total = mixed[:, HEAD_DIM:]
        o_ref[:, cols] = (mixed[:, :HEAD_DIM] / total).astype(BF)
        lse_ref[0, h : h + 1, :] = (top + jnp.log2(total)).T[0:1, :]


def attention_forward(q, kv, bias, heads=8):
    rows = q.shape[0]
    blocks = len(kv)
    wide = heads * HEAD_DIM
    steps = HEADS // heads
    whole = lambda i: (0, 0)
    return pl.pallas_call(
        functools.partial(attention_forward_kernel, blocks, heads),
        grid=(steps,),
        in_specs=[pl.BlockSpec((rows, wide), lambda i: (0, i))]
        + [pl.BlockSpec((rows, 2 * HEAD_DIM), whole)] * blocks
        + [pl.BlockSpec((rows, blocks * rows), whole)],
        out_specs=[
            pl.BlockSpec((rows, wide), lambda i: (0, i)),
            pl.BlockSpec((1, heads, rows), lambda i: (i, 0, 0)),
        ],
        out_shape=[
            jax.ShapeDtypeStruct((rows, D), BF),
            jax.ShapeDtypeStruct((steps, heads, rows), F32),
        ],
        compiler_params=params(),
        cost_estimate=pl.CostEstimate(
            flops=8 * rows * rows * blocks * D,
            transcendentals=rows * rows * blocks * HEADS,
            bytes_accessed=4 * rows * D + 4 * rows * rows * blocks,
        ),
        name="attention_forward",
    )(q, *kv, bias)


def attention_backward_kernel(blocks, heads, q_ref, do_ref, o_ref, *refs):
    kv_refs = refs[:blocks]
    bias_ref, lse_ref, dq_ref, dkv_ref, acc_ref = refs[blocks:]
    rows = q_ref.shape[0]
    step = pl.program_id(0)

    @pl.when(step == 0)
    def _():
        acc_ref[...] = jnp.zeros_like(acc_ref)

    keys = jnp.concatenate([r[:, :HEAD_DIM] for r in kv_refs], axis=0)
    vals = jnp.concatenate([r[:, HEAD_DIM:] for r in kv_refs], axis=0)
    keys_t = keys.T
    for h in range(heads):
        cols = slice(h * HEAD_DIM, (h + 1) * HEAD_DIM)
        q, do = q_ref[:, cols], do_ref[:, cols]
        delta = jnp.sum(
            (do.astype(F32) * o_ref[:, cols].astype(F32)).T, axis=0, keepdims=True
        )
        scores = dot(keys, q, NT) + bias_ref[...]
        probs = jnp.exp2(scores - lse_ref[0, h : h + 1, :])
        dprobs = dot(vals, do, NT)
        dscores = (probs * (dprobs - delta)).astype(BF)
        acc_ref[:, :HEAD_DIM] += dot(dscores, q)
        acc_ref[:, HEAD_DIM:] += dot(probs.astype(BF), do)
        dq_ref[:, cols] = (dot(keys_t, dscores) * INV_ROOT).T.astype(BF)

    @pl.when(step == pl.num_programs(0) - 1)
    def _():
        for s in range(blocks):
            part = slice(s * rows, (s + 1) * rows)
            dkv_ref[s, :, :HEAD_DIM] = (acc_ref[part, :HEAD_DIM] * LN2).astype(BF)
            dkv_ref[s, :, HEAD_DIM:] = acc_ref[part, HEAD_DIM:].astype(BF)


def attention_backward(tree, q, do, o, kv, bias, lse, heads=8):
    rows = q.shape[0]
    blocks = len(kv)
    wide = heads * HEAD_DIM
    steps = HEADS // heads
    whole = lambda i: (0, 0)
    return pl.pallas_call(
        functools.partial(attention_backward_kernel, blocks, heads),
        grid=(steps,),
        in_specs=[
            pl.BlockSpec((rows, wide), lambda i: (0, i)),
            pl.BlockSpec((rows, wide), lambda i: (tree, i)),
            pl.BlockSpec((rows, wide), lambda i: (0, i)),
        ]
        + [pl.BlockSpec((rows, 2 * HEAD_DIM), whole)] * blocks
        + [
            pl.BlockSpec((blocks * rows, rows), whole),
            pl.BlockSpec((1, heads, rows), lambda i: (i, 0, 0)),
        ],
        out_specs=[
            pl.BlockSpec((rows, wide), lambda i: (0, i)),
            pl.BlockSpec((blocks, rows, 2 * HEAD_DIM), lambda i: (0, 0, 0)),
        ],
        out_shape=[
            jax.ShapeDtypeStruct((rows, D), BF),
            jax.ShapeDtypeStruct((blocks, rows, 2 * HEAD_DIM), BF),
        ],
        scratch_shapes=[pltpu.VMEM((blocks * rows, 2 * HEAD_DIM), F32)],
        compiler_params=params(),
        cost_estimate=pl.CostEstimate(
            flops=20 * rows * rows * blocks * D,
            transcendentals=rows * rows * blocks * HEADS,
            bytes_accessed=8 * rows * D + 4 * rows * rows * blocks,
        ),
        name="attention_backward",
    )(q, do, o, *kv, bias, lse)


def entry_kernel(x_ref, norm_ref, dn_ref, up_ref, w_ref, a_ref, u_ref, kv_ref):
    a = layer_norm(x_ref[...].astype(F32), norm_ref[0:1, :], norm_ref[1:2, :]).astype(BF)
    a_ref[...] = a
    u = (2.0 * dot(a, dn_ref[...], NT)).astype(BF)
    u_ref[...] = u
    kv_ref[...] = (dot(a, w_ref[...]) + dot(u, up_ref[...])).astype(BF)


def entry(tree, x, norm, dn, up, w):
    rows = x.shape[0]
    wide = 2 * HEAD_DIM
    last = D // wide
    return pl.pallas_call(
        entry_kernel,
        grid=(1,),
        in_specs=[
            pl.BlockSpec((rows, D), lambda i: (0, 0)),
            pl.BlockSpec((2, D), lambda i: (0, 0)),
            pl.BlockSpec((RANK, D), lambda i: (tree, 0)),
            pl.BlockSpec((RANK, wide), lambda i: (tree, last)),
            pl.BlockSpec((D, wide), lambda i: (0, last)),
        ],
        out_specs=[
            pl.BlockSpec((rows, D), lambda i: (0, 0)),
            pl.BlockSpec((rows, RANK), lambda i: (0, 0)),
            pl.BlockSpec((rows, wide), lambda i: (0, 0)),
        ],
        out_shape=[
            jax.ShapeDtypeStruct((rows, D), BF),
            jax.ShapeDtypeStruct((rows, RANK), BF),
            jax.ShapeDtypeStruct((rows, wide), BF),
        ],
        compiler_params=params(),
        cost_estimate=pl.CostEstimate(
            flops=3 * rows * D * wide, transcendentals=0, bytes_accessed=8 * rows * D
        ),
        name="entry",
    )(x, norm, dn, up, w)


def queries_kernel(a_ref, u_ref, up_ref, w_ref, q_ref):
    q = dot(a_ref[...], w_ref[...]) + dot(u_ref[...], up_ref[...])
    q_ref[...] = (q * (INV_ROOT * LOG2E)).astype(BF)


def queries(tree, a, u, up, w, block=1024):
    rows = a.shape[0]
    return pl.pallas_call(
        queries_kernel,
        grid=(D // block,),
        in_specs=[
            pl.BlockSpec((rows, D), lambda i: (0, 0)),
            pl.BlockSpec((rows, RANK), lambda i: (0, 0)),
            pl.BlockSpec((RANK, block), lambda i: (tree, i)),
            pl.BlockSpec((D, block), lambda i: (0, i)),
        ],
        out_specs=pl.BlockSpec((rows, block), lambda i: (0, i)),
        out_shape=jax.ShapeDtypeStruct((rows, D), BF),
        compiler_params=params(),
        cost_estimate=pl.CostEstimate(
            flops=2 * rows * D * D, transcendentals=0, bytes_accessed=2 * D * D
        ),
        name="queries",
    )(a, u, up, w)


def mixing_kernel(trees, *refs):
    o_refs, x_refs = refs[:trees], refs[trees : 2 * trees]
    norm_ref, dn_ref, up_ref, w_ref, u_ref, x2_ref, b_ref, o_all = refs[2 * trees :]
    rows = o_refs[0].shape[0]
    block = w_ref.shape[1]
    step = pl.program_id(0)

    @pl.when(step == 0)
    def _():
        for m in range(trees):
            part = slice(m * rows, (m + 1) * rows)
            o_all[part, :] = o_refs[m][...]
            x2_ref[part, :] = x_refs[m][...].astype(F32)
        u_ref[...] = masked(dot(o_all[...], dn_ref[...], NT), rows)

    cols = pl.ds(pl.multiple_of(step * block, block), block)
    x2_ref[:, cols] += dot(o_all[...], w_ref[...]) + dot(u_ref[...], up_ref[...])

    @pl.when(step == pl.num_programs(0) - 1)
    def _():
        b_ref[...] = layer_norm(x2_ref[...], norm_ref[0:1, :], norm_ref[1:2, :]).astype(BF)


def mixing(o, x, norm, dn, up, w, block=512):
    trees, rows = len(o), o[0].shape[0]
    total, wide = trees * rows, trees * RANK
    whole = lambda i: (0, 0)
    single = pl.Buffered(1)
    return pl.pallas_call(
        functools.partial(mixing_kernel, trees),
        grid=(D // block,),
        in_specs=[pl.BlockSpec((rows, D), whole, pipeline_mode=single)] * (2 * trees)
        + [
            pl.BlockSpec((2, D), whole),
            pl.BlockSpec((wide, D), whole),
            pl.BlockSpec((wide, block), lambda i: (0, i)),
            pl.BlockSpec((D, block), lambda i: (0, i)),
        ],
        out_specs=[
            pl.BlockSpec((total, wide), whole),
            pl.BlockSpec((total, D), whole),
            pl.BlockSpec((total, D), whole),
        ],
        out_shape=[
            jax.ShapeDtypeStruct((total, wide), BF),
            jax.ShapeDtypeStruct((total, D), F32),
            jax.ShapeDtypeStruct((total, D), BF),
        ],
        scratch_shapes=[pltpu.VMEM((total, D), BF)],
        compiler_params=params(),
        cost_estimate=pl.CostEstimate(
            flops=2 * total * D * D, transcendentals=0, bytes_accessed=2 * D * D + 10 * total * D
        ),
        name="mixing",
    )(*o, *x, norm, dn, up, w)


def unmixing_kernel(trees, *refs):
    o_refs = refs[:trees]
    dx2_ref, u_ref, dn_ref, up_ref, w_ref, do_ref, gdn_ref, gup_ref, dr_ref, du_ref = refs[trees:]
    rows = o_refs[0].shape[0]

    @pl.when(pl.program_id(0) == 0)
    def _():
        dr = dx2_ref[...].astype(BF)
        dr_ref[...] = dr
        du_ref[...] = masked(dot(dr, up_ref[...], NT), rows)
        gup_ref[...] = dot(u_ref[...], dr, TN).astype(BF)

    do_ref[...] = (dot(dr_ref[...], w_ref[...], NT) + dot(du_ref[...], dn_ref[...])).astype(BF)
    o = jnp.concatenate([r[...] for r in o_refs], axis=0)
    gdn_ref[...] = dot(du_ref[...], o, TN).astype(BF)


def unmixing(o, dx2, u, dn, up, w, block=512):
    trees, rows = len(o), o[0].shape[0]
    total, wide = trees * rows, trees * RANK
    whole = lambda i: (0, 0)
    return pl.pallas_call(
        functools.partial(unmixing_kernel, trees),
        grid=(D // block,),
        in_specs=[pl.BlockSpec((rows, block), lambda i: (0, i))] * trees
        + [
            pl.BlockSpec((total, D), whole, pipeline_mode=pl.Buffered(1)),
            pl.BlockSpec((total, wide), whole),
            pl.BlockSpec((wide, block), lambda i: (0, i)),
            pl.BlockSpec((wide, D), whole),
            pl.BlockSpec((block, D), lambda i: (i, 0)),
        ],
        out_specs=[
            pl.BlockSpec((total, block), lambda i: (0, i)),
            pl.BlockSpec((wide, block), lambda i: (0, i)),
            pl.BlockSpec((wide, D), whole),
        ],
        out_shape=[
            jax.ShapeDtypeStruct((total, D), BF),
            jax.ShapeDtypeStruct((wide, D), BF),
            jax.ShapeDtypeStruct((wide, D), BF),
        ],
        scratch_shapes=[pltpu.VMEM((total, D), BF), pltpu.VMEM((total, wide), BF)],
        compiler_params=params(),
        cost_estimate=pl.CostEstimate(
            flops=2 * total * D * D, transcendentals=0, bytes_accessed=2 * D * D + 8 * total * D
        ),
        name="unmixing",
    )(*o, dx2, u, dn, up, w)


def leaving_kernel(
    dq_ref, dkv_ref, a_ref, u_ref, x_ref, dx2_ref, gain_ref, dn_ref, up_ref, w_ref,
    dx_ref, gdn_ref, gup_ref, da_ref, du_ref,
):
    step = pl.program_id(0)
    block = w_ref.shape[0]

    @pl.when(step == 0)
    def _():
        joined = jnp.concatenate([dq_ref[...], dkv_ref[...]], axis=1)
        du_ref[...] = (2.0 * dot(joined, up_ref[...], NT)).astype(BF)
        gup_ref[...] = dot(u_ref[...], joined, TN).astype(BF)

    da = dot(dq_ref[...], w_ref[:, :D], NT) + dot(dkv_ref[...], w_ref[:, D:], NT)
    cols = pl.ds(pl.multiple_of(step * block, block), block)
    da_ref[:, cols] = (da + dot(du_ref[...], dn_ref[...])).astype(BF).astype(F32)
    gdn_ref[...] = dot(du_ref[...], a_ref[...], TN).astype(BF)

    @pl.when(step == pl.num_programs(0) - 1)
    def _():
        back = layer_norm_back(x_ref[...].astype(F32), gain_ref[...], da_ref[...])
        dx_ref[...] = (dx2_ref[...] + back).astype(BF)


def leaving(tree, dq, dkv, a, u, x, dx2, gain, dn, up, w, block=512):
    rows = dq.shape[0]
    joined = D + 2 * HEAD_DIM
    whole = lambda i: (0, 0)
    return pl.pallas_call(
        leaving_kernel,
        grid=(D // block,),
        in_specs=[
            pl.BlockSpec((rows, D), whole),
            pl.BlockSpec((rows, 2 * HEAD_DIM), whole),
            pl.BlockSpec((rows, block), lambda i: (0, i)),
            pl.BlockSpec((rows, RANK), whole),
            pl.BlockSpec((rows, D), whole),
            pl.BlockSpec((rows, D), lambda i: (tree, 0)),
            pl.BlockSpec((1, D), whole),
            pl.BlockSpec((RANK, block), lambda i: (tree, i)),
            pl.BlockSpec((RANK, joined), lambda i: (tree, 0)),
            pl.BlockSpec((block, joined), lambda i: (i, 0)),
        ],
        out_specs=[
            pl.BlockSpec((rows, D), whole),
            pl.BlockSpec((RANK, block), lambda i: (0, i)),
            pl.BlockSpec((RANK, joined), whole),
        ],
        out_shape=[
            jax.ShapeDtypeStruct((rows, D), BF),
            jax.ShapeDtypeStruct((RANK, D), BF),
            jax.ShapeDtypeStruct((RANK, joined), BF),
        ],
        scratch_shapes=[pltpu.VMEM((rows, D), F32), pltpu.VMEM((rows, RANK), BF)],
        compiler_params=params(),
        cost_estimate=pl.CostEstimate(
            flops=2 * rows * D * joined, transcendentals=0, bytes_accessed=2 * D * joined
        ),
        name="leaving",
    )(dq, dkv, a, u, x, dx2, gain, dn, up, w)


def gelu_parts(f):
    square = f * f
    half = 0.5 + 0.5 * jnp.tanh(f * (GELU_C + (GELU_C * 0.044715) * square))
    return square, half


def mlp_up_kernel(per_tree, b_ref, wu_ref, upu_ref, dnu_ref, g_ref, u3_ref):
    @pl.when(pl.program_id(0) == 0)
    def _():
        u3_ref[...] = masked(dot(b_ref[...], dnu_ref[...], NT), per_tree)

    f = dot(b_ref[...], wu_ref[0]) + dot(u3_ref[...], upu_ref[...])
    g_ref[...] = (f * gelu_parts(f)[1]).astype(BF)


def mlp_up(b, w_up, up_up, down_up, block=512):
    rows = b.shape[0]
    shards, _, part = w_up.shape
    hidden = shards * part
    wide = down_up.shape[0]
    block = min(block, part)
    per = part // block
    once = lambda j: (0, 0)
    return pl.pallas_call(
        functools.partial(mlp_up_kernel, rows * RANK // wide),
        grid=(hidden // block,),
        in_specs=[
            pl.BlockSpec((rows, D), once),
            pl.BlockSpec((1, D, block), lambda j: (j // per, 0, j % per)),
            pl.BlockSpec((wide, block), lambda j: (0, j)),
            pl.BlockSpec((wide, D), once),
        ],
        out_specs=pl.BlockSpec((rows, block), lambda j: (0, j)),
        out_shape=jax.ShapeDtypeStruct((rows, hidden), BF),
        scratch_shapes=[pltpu.VMEM((rows, wide), BF)],
        compiler_params=params(),
        cost_estimate=pl.CostEstimate(
            flops=2 * rows * D * hidden,
            transcendentals=rows * hidden,
            bytes_accessed=2 * D * hidden + 2 * rows * hidden,
        ),
        name="mlp_up",
    )(b, w_up, up_up, down_up)


def mlp_down_kernel(g_ref, x2_ref, wd_ref, dnd_ref, upd_ref, y_ref, sum_ref, acc_ref):
    step = pl.program_id(0)

    @pl.when(step == 0)
    def _():
        sum_ref[...] = x2_ref[...]
        acc_ref[...] = jnp.zeros_like(acc_ref)

    g = g_ref[...]
    sum_ref[...] += dot(g, wd_ref[...])
    acc_ref[...] += dot(g, dnd_ref[...], NT)

    @pl.when(step == pl.num_programs(0) - 1)
    def _():
        u4 = (2.0 * acc_ref[...]).astype(BF)
        y_ref[...] = (sum_ref[...] + dot(u4, upd_ref[...])).astype(BF)


def mlp_down(tree, trees, g, x2, w_down, down_down, up_down, block=1024):
    rows, hidden = g.shape[0] // trees, g.shape[1]
    once = lambda j: (0, 0)
    return pl.pallas_call(
        mlp_down_kernel,
        grid=(hidden // block,),
        in_specs=[
            pl.BlockSpec((rows, block), lambda j: (tree, j)),
            pl.BlockSpec((rows, D), lambda j: (tree, 0)),
            pl.BlockSpec((block, D), lambda j: (j, 0)),
            pl.BlockSpec((RANK, block), lambda j: (tree, j)),
            pl.BlockSpec((RANK, D), lambda j: (tree, 0)),
        ],
        out_specs=pl.BlockSpec((rows, D), once),
        out_shape=jax.ShapeDtypeStruct((rows, D), BF),
        scratch_shapes=[pltpu.VMEM((rows, D), F32), pltpu.VMEM((rows, RANK), F32)],
        compiler_params=params(),
        cost_estimate=pl.CostEstimate(
            flops=2 * rows * D * hidden,
            transcendentals=0,
            bytes_accessed=2 * D * hidden + 2 * rows * hidden,
        ),
        name="mlp_down",
    )(g, x2, w_down, down_down, up_down)


def mlp_forward_kernel(
    per_tree, b_ref, x2_ref, wu_ref, wd_ref, upu_ref, dnd_ref, dnu_ref, upd_ref,
    y_ref, g_ref, gp_ref, u3_ref, u4_ref, sum_ref, acc_ref,
):
    step = pl.program_id(0)

    @pl.when(step == 0)
    def _():
        u3_ref[...] = masked(dot(b_ref[...], dnu_ref[...], NT), per_tree)
        sum_ref[...] = x2_ref[...]
        acc_ref[...] = jnp.zeros_like(acc_ref)

    f = dot(b_ref[...], wu_ref[0]) + dot(u3_ref[...], upu_ref[...])
    square, half = gelu_parts(f)
    g = (f * half).astype(BF)
    g_ref[...] = g
    slope = f * ((2 * GELU_C) + (6 * GELU_C * 0.044715) * square)
    gp_ref[...] = (half + (half * (1.0 - half)) * slope).astype(BF)
    sum_ref[...] += dot(g, wd_ref[...])
    acc_ref[...] += dot(dnd_ref[...], g, NT)

    @pl.when(step == pl.num_programs(0) - 1)
    def _():
        u4 = masked(acc_ref[...].T, per_tree)
        u4_ref[...] = u4
        y_ref[...] = (sum_ref[...] + dot(u4, upd_ref[...])).astype(BF)


def mlp_forward(b, x2, w_up, w_down, up_up, down_down, down_up, up_down, block=512):
    rows = b.shape[0]
    shards, _, part = w_up.shape
    hidden = shards * part
    trees = down_up.shape[0] // RANK
    wide = trees * RANK
    block = min(block, part)
    per = part // block
    once = lambda j: (0, 0)
    return pl.pallas_call(
        functools.partial(mlp_forward_kernel, rows // trees),
        grid=(hidden // block,),
        in_specs=[
            pl.BlockSpec((rows, D), once, pipeline_mode=pl.Buffered(1)),
            pl.BlockSpec((rows, D), once, pipeline_mode=pl.Buffered(1)),
            pl.BlockSpec((1, D, block), lambda j: (j // per, 0, j % per)),
            pl.BlockSpec((block, D), lambda j: (j, 0)),
            pl.BlockSpec((wide, block), lambda j: (0, j)),
            pl.BlockSpec((wide, block), lambda j: (0, j)),
            pl.BlockSpec((wide, D), once),
            pl.BlockSpec((wide, D), once),
        ],
        out_specs=[
            pl.BlockSpec((rows, D), once),
            pl.BlockSpec((rows, block), lambda j: (0, j)),
            pl.BlockSpec((rows, block), lambda j: (0, j)),
            pl.BlockSpec((rows, wide), once),
            pl.BlockSpec((rows, wide), once),
        ],
        out_shape=[
            jax.ShapeDtypeStruct((rows, D), BF),
            jax.ShapeDtypeStruct((rows, hidden), BF),
            jax.ShapeDtypeStruct((rows, hidden), BF),
            jax.ShapeDtypeStruct((rows, wide), BF),
            jax.ShapeDtypeStruct((rows, wide), BF),
        ],
        scratch_shapes=[pltpu.VMEM((rows, D), F32), pltpu.VMEM((wide, rows), F32)],
        compiler_params=params(),
        cost_estimate=pl.CostEstimate(
            flops=4 * rows * D * hidden,
            transcendentals=rows * hidden,
            bytes_accessed=4 * D * hidden + 4 * rows * hidden + 10 * rows * D,
        ),
        name="mlp_forward",
    )(b, x2, w_up, w_down, up_up, down_down, down_up, up_down)


def mlp_backward_kernel(
    per_tree, dy_ref, b_ref, x2_ref, gain_ref, wu_ref, wd_ref, g_ref, gp_ref, u3_ref, u4_ref,
    upu_ref, dnd_ref, dnu_ref, upd_ref,
    dx2_ref, gupu_ref, gdnd_ref, gdnu_ref, gupd_ref,
    du4_ref, du3_ref,
):
    step = pl.program_id(0)

    @pl.when(step == 0)
    def _():
        dm = dy_ref[...]
        du4_ref[...] = masked(dot(dm, upd_ref[...], NT), per_tree)
        gupd_ref[...] = dot(u4_ref[...], dm, TN).astype(BF)
        dx2_ref[...] = jnp.zeros_like(dx2_ref)
        du3_ref[...] = jnp.zeros_like(du3_ref)

    du4 = du4_ref[...]
    dg = dot(dy_ref[...], wd_ref[...], NT) + dot(du4, dnd_ref[...])
    df = (gp_ref[...].astype(F32) * dg).astype(BF)
    gdnd_ref[...] = dot(du4, g_ref[...], TN).astype(BF)
    gupu_ref[...] = dot(u3_ref[...], df, TN).astype(BF)
    du3_ref[...] += dot(upu_ref[...], df, NT)
    dx2_ref[...] += dot(df, wu_ref[0], NT)

    @pl.when(step == pl.num_programs(0) - 1)
    def _():
        du3 = masked(du3_ref[...].T, per_tree)
        gdnu_ref[...] = dot(du3, b_ref[...], TN).astype(BF)
        db = (dx2_ref[...] + dot(du3, dnu_ref[...])).astype(BF).astype(F32)
        dx2_ref[...] = dy_ref[...].astype(F32) + layer_norm_back(x2_ref[...], gain_ref[...], db)


def mlp_backward(
    dy, b, x2, gain, w_up, w_down, g, gp, u3, u4, up_up, down_down, down_up, up_down, block=512
):
    rows = b.shape[0]
    shards, _, part = w_up.shape
    hidden = shards * part
    trees = down_up.shape[0] // RANK
    wide = trees * RANK
    block = min(block, part)
    per = part // block
    once = lambda j: (0, 0)
    single = pl.Buffered(1)
    return pl.pallas_call(
        functools.partial(mlp_backward_kernel, rows // trees),
        grid=(hidden // block,),
        in_specs=[
            pl.BlockSpec((rows, D), once, pipeline_mode=single),
            pl.BlockSpec((rows, D), once, pipeline_mode=single),
            pl.BlockSpec((rows, D), once, pipeline_mode=single),
            pl.BlockSpec((1, D), once),
            pl.BlockSpec((1, D, block), lambda j: (j // per, 0, j % per)),
            pl.BlockSpec((block, D), lambda j: (j, 0)),
            pl.BlockSpec((rows, block), lambda j: (0, j)),
            pl.BlockSpec((rows, block), lambda j: (0, j)),
            pl.BlockSpec((rows, wide), once),
            pl.BlockSpec((rows, wide), once),
            pl.BlockSpec((wide, block), lambda j: (0, j)),
            pl.BlockSpec((wide, block), lambda j: (0, j)),
            pl.BlockSpec((wide, D), once),
            pl.BlockSpec((wide, D), once),
        ],
        out_specs=[
            pl.BlockSpec((rows, D), once),
            pl.BlockSpec((wide, block), lambda j: (0, j)),
            pl.BlockSpec((wide, block), lambda j: (0, j)),
            pl.BlockSpec((wide, D), once),
            pl.BlockSpec((wide, D), once),
        ],
        out_shape=[
            jax.ShapeDtypeStruct((rows, D), F32),
            jax.ShapeDtypeStruct((wide, hidden), BF),
            jax.ShapeDtypeStruct((wide, hidden), BF),
            jax.ShapeDtypeStruct((wide, D), BF),
            jax.ShapeDtypeStruct((wide, D), BF),
        ],
        scratch_shapes=[
            pltpu.VMEM((rows, wide), BF),
            pltpu.VMEM((wide, rows), F32),
        ],
        compiler_params=params(),
        cost_estimate=pl.CostEstimate(
            flops=4 * rows * D * hidden,
            transcendentals=0,
            bytes_accessed=4 * D * hidden + 4 * rows * hidden + 14 * rows * D,
        ),
        name="mlp_backward",
    )(dy, b, x2, gain, w_up, w_down, g, gp, u3, u4, up_up, down_down, down_up, up_down)


def segment_of(places, lengths):
    order = jnp.arange(lengths.shape[0], dtype=jnp.int32)
    ends = jnp.sum(
        jnp.where(order[None, :] <= order[:, None], lengths[None, :], 0), axis=1, dtype=jnp.int32
    )
    return jnp.sum((places[:, None] >= ends[None, :]).astype(jnp.int32), axis=1, dtype=jnp.int32)


def ancestry(parents):
    seg_ids = jnp.arange(parents.shape[0], dtype=jnp.int32)
    current = seg_ids
    reach = current[:, None] == seg_ids[None, :]
    for sweep in range(parents.shape[0] - 1):
        current = jnp.sum(
            jnp.where(current[:, None] == seg_ids[None, :], parents[None, :], 0),
            axis=1,
            dtype=jnp.int32,
        )
        reach = reach | (current[:, None] == seg_ids[None, :])
    return reach.astype(BF)


def key_bias(lengths, parents, query_places, key_places):
    seg_ids = jnp.arange(parents.shape[0], dtype=jnp.int32)
    of_query = (segment_of(query_places, lengths)[:, None] == seg_ids[None, :]).astype(BF)
    of_key = (segment_of(key_places, lengths)[:, None] == seg_ids[None, :]).astype(BF)
    known = ancestry(parents)

    def bias(rows_in, rows_out, place_query, place_key):
        reach = dot(rows_in, rows_out, NT)
        allowed = (reach > 0.5) & (place_key <= place_query) & (place_key >= 0)
        return jnp.where(allowed, 0.0, MASKED).astype(F32)

    anc = dot(of_query, known).astype(BF)
    return (
        bias(anc, of_key, query_places[:, None], key_places[None, :]),
        bias(of_key, anc, query_places[None, :], key_places[:, None]),
    )


def shifted(value, axis, steps):
    count = lax.axis_size(axis)
    return lax.ppermute(value, axis, [(i, (i + steps) % count) for i in range(count)])


def local(
    inputs, cotangent, norm_gains, norm_biases, w_attn, w_out, w_up, w_down,
    down_attn, up_attn, down_out, up_out, down_up, up_up, down_down, up_down,
    seg_lengths, parent_ids, adapter_ids,
):
    section = lax.axis_index("section")
    shard = lax.axis_index("fsdp")
    member = lax.axis_index("replica")
    shards = lax.axis_size("fsdp")
    members = lax.axis_size("replica")
    trees, per_tree = inputs.shape[0], inputs.shape[1]
    gain = norm_gains[0].astype(F32)
    shift = norm_biases[0].astype(F32)
    norms = [jnp.stack([gain[i], shift[i]]) for i in range(2)]

    def quarter(weight):
        part = weight.shape[0] // members
        return lax.dynamic_slice_in_dim(weight, member * part, part, 0)

    def gathered(weight):
        return lax.all_gather(quarter(weight), ("fsdp", "replica"), axis=0, tiled=True)

    up_parts = gathered(w_up[0]).reshape(shards, D, w_up.shape[2])
    down_full = gathered(w_down[0])

    def stacked(pieces):
        buffer = jnp.zeros((shards, *pieces[0].shape), pieces[0].dtype)
        for k, piece in enumerate(pieces):
            at = (lax.rem(shard - k + shards, shards),) + (0,) * piece.ndim
            buffer = lax.dynamic_update_slice(buffer, piece[None], at)
        return buffer

    stacks = (down_attn, up_attn, down_out, up_out, down_up, up_up, down_down, up_down)
    widths = [stack.shape[3] for stack in stacks]
    starts = [sum(widths[:i]) for i in range(len(widths))]
    chosen = adapter_ids[:, 0, 0]
    picked = jnp.concatenate(
        [
            jnp.concatenate(
                [lax.dynamic_index_in_dim(stack[0], chosen[m], 0, keepdims=False) for m in range(trees)],
                axis=0,
            )
            for stack in stacks
        ],
        axis=1,
    )
    owners = lax.all_gather(chosen, "replica", axis=0, tiled=True)
    owners, picked = lax.optimization_barrier((owners, picked))
    maps = stacked([picked] + [shifted(picked, "fsdp", k) for k in range(1, shards)])
    maps = [
        jnp.moveaxis(maps[:, :, at : at + width], 0, 1).reshape(trees * RANK, shards * width)
        for at, width in zip(starts, widths)
    ]
    dn_attn, up_attn_, dn_out, up_out_, dn_up, up_up_, dn_down, up_down_ = maps

    both = jnp.concatenate([w_out[0], w_attn[0]], axis=1)
    own = quarter(both)
    rows_each, wide = own.shape
    cores = 2 if members % 2 == 0 else 1
    held = jnp.zeros((shards, members, rows_each, wide), BF)
    held = lax.dynamic_update_slice(
        held, both.reshape(1, members, rows_each, wide), (shard, 0, 0, 0)
    )
    for k in range(1, shards):
        piece = shifted(own, "fsdp", k)
        column = [(piece, member)]
        for i in range(1, members // cores):
            column.append(
                (shifted(piece, "replica", cores * i), lax.rem(member - cores * i + members, members))
            )
        if cores == 2:
            swap = [(i, i ^ 1) for i in range(members)]
            column += [
                (lax.ppermute(value, "replica", swap), place ^ 1) for value, place in column
            ]
        source = lax.rem(shard - k + shards, shards)
        for value, place in column:
            held = lax.dynamic_update_slice(held, value[None, None], (source, place, 0, 0))
    held = held.reshape(shards, D, wide)
    out_wide = w_out.shape[2]
    out_full = jnp.moveaxis(held[:, :, :out_wide], 0, 1).reshape(D, D)
    attn_full = jnp.moveaxis(held[:, :, out_wide:], 0, 1).reshape(D, shards * w_attn.shape[2])

    query_places = shard * per_tree + jnp.arange(per_tree, dtype=jnp.int32)
    key_places = jnp.concatenate(
        [(shard - s) * per_tree + jnp.arange(per_tree, dtype=jnp.int32) for s in range(shards)]
    )
    biases = [
        key_bias(seg_lengths[m, 0], parent_ids[m, 0], query_places, key_places)
        for m in range(trees)
    ]

    def to_higher(value, steps):
        return lax.ppermute(value, "fsdp", [(i, i + steps) for i in range(shards - steps)])

    def to_lower(value, steps):
        return lax.ppermute(value, "fsdp", [(i + steps, i) for i in range(shards - steps)])

    def attend(x):
        kept = []
        for m in range(trees):
            a, u1, kv = entry(m, x[m], norms[0], dn_attn, up_attn_, attn_full)
            blocks = [kv] + [to_higher(kv, s) for s in range(1, shards)]
            q = queries(m, a, u1, up_attn_, attn_full)
            o, lse = attention_forward(q, blocks, biases[m][0])
            kept.append((a, u1, q, blocks, o, lse))
        o = [part[4] for part in kept]
        u2, x2, b = mixing(o, x, norms[1], dn_out, up_out_, out_full)
        return kept, o, u2, x2, b

    def backward(dy, x, state, mlp_state):
        kept, o, u2, x2, b = state
        g, gp, u3, u4 = mlp_state
        dx2, g_up_up, g_dn_down, g_dn_up, g_up_down = mlp_backward(
            dy, b, x2, gain[1:2], up_parts, down_full, g, gp, u3, u4,
            up_up_, dn_down, dn_up, up_down_,
        )
        do, g_dn_out, g_up_out = unmixing(o, dx2, u2, dn_out, up_out_, out_full)
        partial = []
        for m in range(trees):
            a, u1, q, blocks, o_m, lse = kept[m]
            dq, dkv = attention_backward(m, q, do, o_m, blocks, biases[m][1], lse)
            arrived = [to_lower(dkv[s], s) for s in range(1, shards)]
            partial.append((dq, dkv[0], arrived))
        dx, g_attn = [], []
        for m in range(trees):
            a, u1 = kept[m][:2]
            dq, total, arrived = partial[m]
            total = total.astype(F32)
            for part in arrived:
                total = total + part.astype(F32)
            dx_m, g_dn, g_up = leaving(
                m, dq, total.astype(BF), a, u1, x[m], dx2, gain[0:1], dn_attn, up_attn_, attn_full
            )
            dx.append(dx_m)
            g_attn.append((g_dn, g_up))
        g_dn_attn = jnp.concatenate([g[0] for g in g_attn], axis=0)
        g_up_attn = jnp.concatenate([g[1] for g in g_attn], axis=0)
        early = (g_dn_out, g_up_out, g_dn_up, g_up_up, g_dn_down, g_up_down)
        return dx, early, (g_dn_attn, g_up_attn)

    own_rows = [inputs[m] for m in range(trees)]
    _, _, _, x2, b = attend(own_rows)
    g = mlp_up(b, up_parts, up_up_, dn_up)
    arrived = [
        lax.ppermute(
            mlp_down(m, trees, g, x2, down_full, dn_down, up_down_), "section", [(0, 1)]
        )
        for m in range(trees)
    ]
    x = [jnp.where(section == 0, own_rows[m], arrived[m]) for m in range(trees)]
    state = attend(x)
    layer_out, *mlp_state = mlp_forward(
        state[4], state[3], up_parts, down_full, up_up_, dn_down, dn_up, up_down_
    )

    own_grad = cotangent.reshape(trees * per_tree, D)
    first, _, _ = backward(own_grad, x, state, mlp_state)
    arrived = jnp.concatenate([lax.ppermute(part, "section", [(1, 0)]) for part in first], axis=0)
    in_grad, early, late = backward(
        jnp.where(section == 1, own_grad, arrived), x, state, mlp_state
    )

    adapters = down_attn.shape[1]

    def by_shard(grads, parts):
        return jnp.concatenate(
            [g.reshape(trees * RANK, shards, width) for g, width in zip(grads, parts)], axis=2
        )

    def placed(slabs, ids, parts):
        pick = jnp.arange(adapters, dtype=jnp.int32)[:, None] == ids[None, :]
        total = jnp.zeros((adapters, *slabs.shape[1:]), F32)
        for t in range(slabs.shape[0]):
            total = total + jnp.where(pick[:, t, None, None], slabs[t].astype(F32)[None], 0.0)
        offsets = [sum(parts[:i]) for i in range(len(parts))]
        return [total[None, :, :, at : at + width] for at, width in zip(offsets, parts)]

    early_widths = widths[2:]
    slabs = jnp.moveaxis(by_shard(early, early_widths), 1, 0)
    slabs = lax.psum_scatter(slabs, "fsdp", scatter_dimension=0, tiled=False)
    slabs = lax.all_gather(slabs, "replica", axis=0)
    early = placed(
        slabs.reshape(members * trees, RANK, sum(early_widths)), owners, early_widths
    )

    late_widths = widths[:2]
    slabs = jnp.moveaxis(by_shard(late, late_widths), 1, 0)
    total = lax.dynamic_index_in_dim(slabs, shard, 0, keepdims=False).astype(F32)
    for k in range(1, shards):
        goal = lax.rem(shard + k, shards)
        part = lax.dynamic_index_in_dim(slabs, goal, 0, keepdims=False)
        total = total + shifted(part, "fsdp", k).astype(F32)
    total = total.astype(BF)
    slabs = jnp.stack([total] + [shifted(total, "replica", i) for i in range(1, members)])
    order = lax.rem(member - jnp.arange(members, dtype=jnp.int32) + members, members)
    ids = owners.reshape(members, trees)[order].reshape(-1)
    late = placed(slabs.reshape(members * trees, RANK, sum(late_widths)), ids, late_widths)
    return (
        layer_out.reshape(1, trees, per_tree, D),
        jnp.stack(in_grad)[None],
        *late,
        *early,
    )


def solution(mesh):
    rows = P(None, ("replica", "fsdp"), None)
    stack = P("section", None, None, "fsdp")
    placed = (
        (rows, rows)
        + (P("section", None, None),) * 2
        + (P("section", None, "fsdp"),) * 3
        + (P("section", "fsdp", None),)
        + (stack,) * 8
        + (P(None, "replica", None),) * 3
    )
    return jax.shard_map(
        local,
        mesh=mesh,
        in_specs=placed,
        out_specs=(P("section", None, ("replica", "fsdp"), None),) * 2 + (stack,) * 8,
        check_vma=False,
    )
```

```python
import functools
import math

import jax
import jax.numpy as jnp
from jax import lax
from jax.experimental import pallas as pl
from jax.experimental.pallas import tpu as pltpu
from jax.sharding import PartitionSpec as P

D = 2048
HEADS = 16
HEAD_DIM = 128
RANK = 16

NORM_EPS = 1e-05
MASKED = -1e30
BF = jnp.bfloat16
F32 = jnp.float32
INV_ROOT = HEAD_DIM ** (-0.5)
LOG2E = math.log2(math.e)
LN2 = math.log(2.0)
GELU_C = math.sqrt(2.0 / math.pi)
VMEM_LIMIT = 56 * 1024 * 1024

NN = (((1,), (0,)), ((), ()))
NT = (((1,), (1,)), ((), ()))
TN = (((0,), (0,)), ((), ()))


def dot(left, right, dims=NN):
    return lax.dot_general(left, right, dims, preferred_element_type=F32)


def params(steps=1):
    return pltpu.CompilerParams(
        dimension_semantics=("arbitrary",) * steps, vmem_limit_bytes=VMEM_LIMIT
    )


def layer_norm(rows, gain, shift):
    centre = rows - jnp.mean(rows, axis=-1, keepdims=True)
    spread = jnp.mean(centre * centre, axis=-1, keepdims=True)
    return centre * lax.rsqrt(spread + NORM_EPS) * gain + shift


def layer_norm_back(rows, gain, grad):
    centre = rows - jnp.mean(rows, axis=-1, keepdims=True)
    spread = jnp.mean(centre * centre, axis=-1, keepdims=True)
    scale = lax.rsqrt(spread + NORM_EPS)
    unit = centre * scale
    inner = grad * gain
    return scale * (
        inner
        - jnp.mean(inner, axis=-1, keepdims=True)
        - unit * jnp.mean(inner * unit, axis=-1, keepdims=True)
    )


def tree_mask(rows, per_tree):
    row = lax.broadcasted_iota(jnp.int32, (rows, (rows // per_tree) * RANK), 0)
    col = lax.broadcasted_iota(jnp.int32, (rows, (rows // per_tree) * RANK), 1)
    return (row // per_tree) == (col // RANK)


def masked(value, per_tree):
    return jnp.where(tree_mask(value.shape[0], per_tree), 2.0 * value, 0.0).astype(BF)


def attention_forward_kernel(blocks, heads, before, keep, q_ref, *refs):
    kv_refs, (bias_ref, *refs) = refs[:blocks], refs[blocks:]
    o_ref, lse_ref, *kept_refs = refs[before:]
    keys = jnp.concatenate([r[:, :HEAD_DIM] for r in kv_refs], axis=0)
    vals = jnp.concatenate([r[:, HEAD_DIM:] for r in kv_refs], axis=0)
    vals = jnp.concatenate([vals, jnp.ones_like(vals)], axis=1)
    if keep:
        for kept, given in zip(kept_refs, (q_ref, *kv_refs)):
            kept[...] = given[...]
    for h in range(heads):
        cols = slice(h * HEAD_DIM, (h + 1) * HEAD_DIM)
        scores = dot(q_ref[:, cols], keys, NT) + bias_ref[...]
        top = jnp.max(scores, axis=1, keepdims=True)
        probs = jnp.exp2(scores - top)
        mixed = dot(probs.astype(BF), vals)
        total = mixed[:, HEAD_DIM:]
        o_ref[:, cols] = (mixed[:, :HEAD_DIM] / total).astype(BF)
        lse_ref[0, h : h + 1, :] = (top + jnp.log2(total)).T[0:1, :]


def attention_forward(tree, trees, q, kv, bias, before, keep, heads=8):
    rows = q.shape[0]
    blocks = len(kv)
    wide = heads * HEAD_DIM
    steps = HEADS // heads
    whole = lambda i: (0, 0)
    mine = pl.BlockSpec((rows, wide), lambda i: (tree, i))
    pair = pl.BlockSpec((rows, 2 * HEAD_DIM), lambda i: (tree, 0))
    tall = jax.ShapeDtypeStruct((trees * rows, D), BF)
    outs = [tall, jax.ShapeDtypeStruct((trees * steps, heads, rows), F32)]
    out_specs = [mine, pl.BlockSpec((1, heads, rows), lambda i: (tree * steps + i, 0, 0))]
    if keep:
        outs += [tall] + [jax.ShapeDtypeStruct((trees * rows, 2 * HEAD_DIM), BF)] * blocks
        out_specs += [mine] + [pair] * blocks
    return pl.pallas_call(
        functools.partial(attention_forward_kernel, blocks, heads, len(before), keep),
        grid=(steps,),
        in_specs=[pl.BlockSpec((rows, wide), lambda i: (0, i))]
        + [pl.BlockSpec((rows, 2 * HEAD_DIM), whole)] * blocks
        + [pl.BlockSpec((rows, blocks * rows), whole)]
        + [pl.BlockSpec(memory_space=pl.ANY)] * len(before),
        out_specs=out_specs,
        out_shape=outs,
        input_output_aliases={blocks + 2 + i: i for i in range(len(before))},
        compiler_params=params(),
        cost_estimate=pl.CostEstimate(
            flops=8 * rows * rows * blocks * D,
            transcendentals=rows * rows * blocks * HEADS,
            bytes_accessed=4 * rows * D + 4 * rows * rows * blocks,
        ),
        name="attention_forward",
    )(q, *kv, bias, *before)


def attention_backward_kernel(blocks, heads, _, q_ref, do_ref, o_ref, *refs):
    kv_refs = refs[:blocks]
    bias_ref, lse_ref, dq_ref, *dkv_refs, acc_ref = refs[blocks:]
    rows = q_ref.shape[0]
    step = pl.program_id(0)

    @pl.when(step == 0)
    def _():
        acc_ref[...] = jnp.zeros_like(acc_ref)

    keys = jnp.concatenate([r[:, :HEAD_DIM] for r in kv_refs], axis=0)
    vals = jnp.concatenate([r[:, HEAD_DIM:] for r in kv_refs], axis=0)
    keys_t = keys.T
    for h in range(heads):
        cols = slice(h * HEAD_DIM, (h + 1) * HEAD_DIM)
        q, do = q_ref[:, cols], do_ref[:, cols]
        delta = jnp.sum(
            (do.astype(F32) * o_ref[:, cols].astype(F32)).T, axis=0, keepdims=True
        )
        scores = dot(keys, q, NT) + bias_ref[...]
        probs = jnp.exp2(scores - lse_ref[0, h : h + 1, :])
        dprobs = dot(vals, do, NT)
        dscores = (probs * (dprobs - delta)).astype(BF)
        acc_ref[:, :HEAD_DIM] += dot(dscores, q)
        acc_ref[:, HEAD_DIM:] += dot(probs.astype(BF), do)
        dq_ref[:, cols] = (dot(keys_t, dscores) * INV_ROOT).T.astype(BF)

    @pl.when(step == pl.num_programs(0) - 1)
    def _():
        for s in range(blocks):
            part = slice(s * rows, (s + 1) * rows)
            dkv_refs[s][:, :HEAD_DIM] = (acc_ref[part, :HEAD_DIM] * LN2).astype(BF)
            dkv_refs[s][:, HEAD_DIM:] = acc_ref[part, HEAD_DIM:].astype(BF)


def attention_backward(which, q, do, o, kv, bias, lse):
    rows = do.shape[0]
    blocks = len(kv)
    trees = q.shape[0] // rows
    heads = lse.shape[1]
    steps = lse.shape[0] // trees
    wide = heads * HEAD_DIM
    mine = lambda i, w: (w[1], i)
    pair = pl.BlockSpec((rows, 2 * HEAD_DIM), lambda i, w: (0, 0))
    dq, *dkv = pl.pallas_call(
        functools.partial(attention_backward_kernel, blocks, heads),
        grid_spec=pltpu.PrefetchScalarGridSpec(
            num_scalar_prefetch=1,
            grid=(steps,),
            in_specs=[
                pl.BlockSpec((rows, wide), mine),
                pl.BlockSpec((rows, wide), lambda i, w: (0, i)),
                pl.BlockSpec((rows, wide), mine),
            ]
            + [pl.BlockSpec((rows, 2 * HEAD_DIM), lambda i, w: (w[1], 0))] * blocks
            + [
                pl.BlockSpec((blocks * rows, rows), lambda i, w: (w[1], 0)),
                pl.BlockSpec((1, heads, rows), lambda i, w: (w[1] * steps + i, 0, 0)),
            ],
            out_specs=[pl.BlockSpec((rows, wide), lambda i, w: (0, i))] + [pair] * blocks,
            scratch_shapes=[pltpu.VMEM((blocks * rows, 2 * HEAD_DIM), F32)],
        ),
        out_shape=[jax.ShapeDtypeStruct((rows, D), BF)]
        + [jax.ShapeDtypeStruct((rows, 2 * HEAD_DIM), BF)] * blocks,
        compiler_params=params(),
        cost_estimate=pl.CostEstimate(
            flops=20 * rows * rows * blocks * D,
            transcendentals=rows * rows * blocks * HEADS,
            bytes_accessed=8 * rows * D + 4 * rows * rows * blocks,
        ),
        name="attention_backward",
    )(which, q, do, o, *kv, bias, lse)
    return dq, dkv


def assemble_kernel(wide, held_ref, full_ref):
    full_ref[...] = jnp.concatenate(
        [held_ref[z][:, :wide] for z in range(held_ref.shape[0])], axis=1
    )


def assemble(held, start, wide, block=256):
    shards, depth, _ = held.shape
    padded = -(-wide // 128) * 128
    return pl.pallas_call(
        functools.partial(assemble_kernel, wide),
        grid=(depth // block,),
        in_specs=[pl.BlockSpec((shards, block, padded), lambda i: (0, i, start // padded))],
        out_specs=pl.BlockSpec((block, shards * wide), lambda i: (i, 0)),
        out_shape=jax.ShapeDtypeStruct((depth, shards * wide), BF),
        compiler_params=params(),
        cost_estimate=pl.CostEstimate(
            flops=0, transcendentals=0, bytes_accessed=4 * shards * depth * padded
        ),
        name="assemble",
    )(held)


def entry_body(x, norm_ref, dn_ref, up_ref, w_ref, a_ref, u_ref, kv_ref):
    a = layer_norm(x.astype(F32), norm_ref[0:1, :], norm_ref[1:2, :]).astype(BF)
    a_ref[...] = a
    u = (2.0 * dot(a, dn_ref[...], NT)).astype(BF)
    u_ref[...] = u
    kv_ref[...] = (dot(a, w_ref[...]) + dot(u, up_ref[...])).astype(BF)


def entry_own_kernel(own_ref, *refs):
    entry_body(own_ref[...], *refs)


def entry_arrived_kernel(before, flag_ref, own_ref, arrived_ref, *refs):
    given, (a_ref, u_ref, kv_ref, x_all, a_all, u_all) = refs[:4], refs[4 + before :]
    x = jnp.where(flag_ref[0] == 1, own_ref[...], arrived_ref[...])
    x_all[...] = x
    entry_body(x, *given, a_ref, u_ref, kv_ref)
    a_all[...] = a_ref[...]
    u_all[0] = u_ref[...]


def entry(tree, trees, own, norm, dn, up, w, arrived=None, flag=None, before=()):
    rows = own.shape[0] // trees
    wide = 2 * HEAD_DIM
    last = D // wide
    whole = lambda i, *_: (0, 0)
    mine = pl.BlockSpec((rows, D), lambda i, *_: (tree, 0))
    row = pl.BlockSpec((rows, D), whole)
    ins, ins_specs = ([own], [mine]) if arrived is None else ([own, arrived], [mine, row])
    outs = [
        jax.ShapeDtypeStruct((rows, D), BF),
        jax.ShapeDtypeStruct((rows, RANK), BF),
        jax.ShapeDtypeStruct((rows, wide), BF),
    ]
    out_specs = [row, pl.BlockSpec((rows, RANK), whole), pl.BlockSpec((rows, wide), whole)]
    kernel = entry_own_kernel
    if arrived is not None:
        kernel = functools.partial(entry_arrived_kernel, len(before))
        outs += [jax.ShapeDtypeStruct((trees * rows, D), BF)] * 2
        outs += [jax.ShapeDtypeStruct((trees, rows, RANK), BF)]
        out_specs += [mine, mine, pl.BlockSpec((1, rows, RANK), lambda i, *_: (tree, 0, 0))]
    return pl.pallas_call(
        kernel,
        grid_spec=pltpu.PrefetchScalarGridSpec(
            num_scalar_prefetch=0 if arrived is None else 1,
            grid=(1,),
            in_specs=ins_specs
            + [
                pl.BlockSpec((2, D), whole),
                pl.BlockSpec((RANK, D), lambda i, *_: (tree, 0)),
                pl.BlockSpec((RANK, wide), lambda i, *_: (tree, last)),
                pl.BlockSpec((D, wide), lambda i, *_: (0, last)),
            ]
            + [pl.BlockSpec(memory_space=pl.ANY)] * len(before),
            out_specs=out_specs,
        ),
        out_shape=outs,
        input_output_aliases={7 + i: 3 + i for i in range(len(before))},
        compiler_params=params(),
        cost_estimate=pl.CostEstimate(
            flops=3 * rows * D * wide, transcendentals=0, bytes_accessed=8 * rows * D
        ),
        name="entry",
    )(*([] if arrived is None else [flag]), *ins, norm, dn, up, w, *before)


def queries_kernel(a_ref, u_ref, up_ref, w_ref, q_ref):
    q = dot(a_ref[...], w_ref[...]) + dot(u_ref[...], up_ref[...])
    q_ref[...] = (q * (INV_ROOT * LOG2E)).astype(BF)


def queries(tree, a, u, up, w, block=1024):
    rows = a.shape[0]
    return pl.pallas_call(
        queries_kernel,
        grid=(D // block,),
        in_specs=[
            pl.BlockSpec((rows, D), lambda i: (0, 0)),
            pl.BlockSpec((rows, RANK), lambda i: (0, 0)),
            pl.BlockSpec((RANK, block), lambda i: (tree, i)),
            pl.BlockSpec((D, block), lambda i: (0, i)),
        ],
        out_specs=pl.BlockSpec((rows, block), lambda i: (0, i)),
        out_shape=jax.ShapeDtypeStruct((rows, D), BF),
        compiler_params=params(),
        cost_estimate=pl.CostEstimate(
            flops=2 * rows * D * D, transcendentals=0, bytes_accessed=2 * D * D
        ),
        name="queries",
    )(a, u, up, w)


def mix(step, rows, o_ref, x_ref, dn_ref, up_ref, w_ref, u_ref, sum_ref):
    @pl.when(step == 0)
    def _():
        sum_ref[...] = x_ref[...].astype(F32)
        u_ref[...] = masked(dot(o_ref[...], dn_ref[...], NT), rows)

    block = w_ref.shape[2]
    cols = pl.ds(pl.multiple_of(step * block, block), block)
    sum_ref[:, cols] += dot(o_ref[...], w_ref[0]) + dot(u_ref[...], up_ref[...])


def normed(sum_ref, norm_ref):
    return layer_norm(sum_ref[...], norm_ref[0:1, :], norm_ref[1:2, :]).astype(BF)


def mixing_kernel(rows, o_ref, x_ref, norm_ref, dn_ref, up_ref, w_ref, x2_ref, b_ref, u_ref):
    step = pl.program_id(0)
    mix(step, rows, o_ref, x_ref, dn_ref, up_ref, w_ref, u_ref, x2_ref)

    @pl.when(step == pl.num_programs(0) - 1)
    def _():
        b_ref[...] = normed(x2_ref, norm_ref)


def mixing(o, x, norm, dn, up, held, part):
    total, wide = o.shape[0], dn.shape[0]
    shards = held.shape[0]
    block = D // shards
    at = part // block
    whole = lambda i: (0, 0)
    single = pl.Buffered(1)
    return pl.pallas_call(
        functools.partial(mixing_kernel, total * RANK // wide),
        grid=(shards,),
        in_specs=[pl.BlockSpec((total, D), whole, pipeline_mode=single)] * 2
        + [
            pl.BlockSpec((2, D), whole),
            pl.BlockSpec((wide, D), whole),
            pl.BlockSpec((wide, block), lambda i: (0, i)),
            pl.BlockSpec((1, D, block), lambda i: (i, 0, at)),
        ],
        out_specs=[pl.BlockSpec((total, D), whole), pl.BlockSpec((total, D), whole)],
        out_shape=[
            jax.ShapeDtypeStruct((total, D), F32),
            jax.ShapeDtypeStruct((total, D), BF),
        ],
        scratch_shapes=[pltpu.VMEM((total, wide), BF)],
        compiler_params=params(),
        cost_estimate=pl.CostEstimate(
            flops=2 * total * D * D, transcendentals=0, bytes_accessed=2 * D * D + 10 * total * D
        ),
        name="mixing",
    )(o, x, norm, dn, up, held)


def query_leaving_kernel(_, dq_ref, u_ref, up_ref, w_ref, da_ref, du_ref, gup_ref):
    @pl.when(pl.program_id(0) == 0)
    def _():
        du_ref[...] = dot(dq_ref[...], up_ref[...], NT)
        gup_ref[...] = dot(u_ref[0], dq_ref[...], TN).astype(BF)

    da_ref[...] = dot(dq_ref[...], w_ref[...], NT)


def query_leaving(which, dq, u, up, w, block=1024):
    rows = dq.shape[0]
    whole = lambda i, w: (0, 0)
    return pl.pallas_call(
        query_leaving_kernel,
        grid_spec=pltpu.PrefetchScalarGridSpec(
            num_scalar_prefetch=1,
            grid=(D // block,),
            in_specs=[
                pl.BlockSpec((rows, D), whole),
                pl.BlockSpec((1, rows, RANK), lambda i, w: (w[1], 0, 0)),
                pl.BlockSpec((RANK, D), lambda i, w: (w[1], 0)),
                pl.BlockSpec((block, D), lambda i, w: (i, 0)),
            ],
            out_specs=[
                pl.BlockSpec((rows, block), lambda i, w: (0, i)),
                pl.BlockSpec((rows, RANK), whole),
                pl.BlockSpec((RANK, D), whole),
            ],
        ),
        out_shape=[
            jax.ShapeDtypeStruct((rows, D), F32),
            jax.ShapeDtypeStruct((rows, RANK), F32),
            jax.ShapeDtypeStruct((RANK, D), BF),
        ],
        compiler_params=params(),
        cost_estimate=pl.CostEstimate(
            flops=2 * rows * D * D, transcendentals=0, bytes_accessed=2 * D * D
        ),
        name="query_leaving",
    )(which, dq, u, up, w)


def leaving_kernel(blocks, _, da_ref, du_ref, *refs):
    dkv_refs = refs[:blocks]
    (a_ref, u_ref, x_ref, dr_ref, gain_ref, dn_ref, up_ref, w_ref,
     dx_ref, gdn_ref, gup_ref) = refs[blocks:]
    total = dkv_refs[0][...].astype(F32)
    for ref in dkv_refs[1:]:
        total = total + ref[...].astype(F32)
    dkv = total.astype(BF)
    du = (2.0 * (du_ref[...] + dot(dkv, up_ref[...], NT))).astype(BF)
    gup_ref[...] = dot(u_ref[0], dkv, TN).astype(BF)
    gdn_ref[...] = dot(du, a_ref[...], TN).astype(BF)
    da = da_ref[...] + dot(dkv, w_ref[...], NT) + dot(du, dn_ref[...])
    back = layer_norm_back(
        x_ref[...].astype(F32), gain_ref[...], da.astype(BF).astype(F32)
    )
    dx_ref[...] = (dr_ref[...].astype(F32) + back).astype(BF)


def leaving(which, da, du, dkv, a, u, x, dr, gain, dn, up, w):
    rows = da.shape[0]
    wide = 2 * HEAD_DIM
    last = D // wide
    whole = lambda i, w: (0, 0)
    mine = lambda i, w: (w[1], 0)
    return pl.pallas_call(
        functools.partial(leaving_kernel, len(dkv)),
        grid_spec=pltpu.PrefetchScalarGridSpec(
            num_scalar_prefetch=1,
            grid=(1,),
            in_specs=[pl.BlockSpec((rows, D), whole), pl.BlockSpec((rows, RANK), whole)]
            + [pl.BlockSpec((rows, wide), whole)] * len(dkv)
            + [
                pl.BlockSpec((rows, D), mine),
                pl.BlockSpec((1, rows, RANK), lambda i, w: (w[1], 0, 0)),
                pl.BlockSpec((rows, D), mine),
                pl.BlockSpec((rows, D), whole),
                pl.BlockSpec((1, D), whole),
                pl.BlockSpec((RANK, D), mine),
                pl.BlockSpec((RANK, wide), lambda i, w: (w[1], last)),
                pl.BlockSpec((D, wide), lambda i, w: (0, last)),
            ],
            out_specs=[
                pl.BlockSpec((rows, D), whole),
                pl.BlockSpec((RANK, D), whole),
                pl.BlockSpec((RANK, wide), whole),
            ],
        ),
        out_shape=[
            jax.ShapeDtypeStruct((rows, D), BF),
            jax.ShapeDtypeStruct((RANK, D), BF),
            jax.ShapeDtypeStruct((RANK, wide), BF),
        ],
        compiler_params=params(),
        cost_estimate=pl.CostEstimate(
            flops=4 * rows * D * wide, transcendentals=0, bytes_accessed=14 * rows * D
        ),
        name="leaving",
    )(which, da, du, *dkv, a, u, x, dr, gain, dn, up, w)


def gelu_parts(f):
    square = f * f
    half = 0.5 + 0.5 * jnp.tanh(f * (GELU_C + (GELU_C * 0.044715) * square))
    return square, half


def mlp_up_kernel(per_tree, b_ref, wu_ref, upu_ref, dnu_ref, g_ref, u3_ref):
    @pl.when(pl.program_id(0) == 0)
    def _():
        u3_ref[...] = masked(dot(b_ref[...], dnu_ref[...], NT), per_tree)

    f = dot(b_ref[...], wu_ref[0]) + dot(u3_ref[...], upu_ref[...])
    g_ref[...] = (f * gelu_parts(f)[1]).astype(BF)


def mlp_up(b, held, part, up_up, down_up, block=1024):
    rows = b.shape[0]
    shards = held.shape[0]
    hidden = shards * part
    wide = down_up.shape[0]
    block = min(block, part)
    per = part // block
    once = lambda j: (0, 0)
    return pl.pallas_call(
        functools.partial(mlp_up_kernel, rows * RANK // wide),
        grid=(hidden // block,),
        in_specs=[
            pl.BlockSpec((rows, D), once),
            pl.BlockSpec((1, D, block), lambda j: (j // per, 0, j % per)),
            pl.BlockSpec((wide, block), lambda j: (0, j)),
            pl.BlockSpec((wide, D), once),
        ],
        out_specs=pl.BlockSpec((rows, block), lambda j: (0, j)),
        out_shape=jax.ShapeDtypeStruct((rows, hidden), BF),
        scratch_shapes=[pltpu.VMEM((rows, wide), BF)],
        compiler_params=params(),
        cost_estimate=pl.CostEstimate(
            flops=2 * rows * D * hidden,
            transcendentals=rows * hidden,
            bytes_accessed=2 * D * hidden + 2 * rows * hidden,
        ),
        name="mlp_up",
    )(b, held, up_up, down_up)


def mlp_down_kernel(trees, g_ref, x2_ref, wd_ref, dnd_ref, upd_ref, *refs):
    y_refs, (sum_ref, acc_ref) = refs[:trees], refs[trees:]
    step = pl.program_id(0)
    rows = g_ref.shape[0] // trees

    @pl.when(step == 0)
    def _():
        sum_ref[...] = x2_ref[...]
        acc_ref[...] = jnp.zeros_like(acc_ref)

    g = g_ref[...]
    sum_ref[...] += dot(g, wd_ref[...])
    acc_ref[...] += dot(dnd_ref[...], g, NT)

    @pl.when(step == pl.num_programs(0) - 1)
    def _():
        u4 = masked(acc_ref[...].T, rows)
        y = (sum_ref[...] + dot(u4, upd_ref[...])).astype(BF)
        for m in range(trees):
            y_refs[m][...] = y[m * rows : (m + 1) * rows]


def mlp_down(trees, g, x2, w_down, down_down, up_down, block=1024):
    total, hidden = g.shape
    rows, wide = total // trees, trees * RANK
    once = lambda j: (0, 0)
    return pl.pallas_call(
        functools.partial(mlp_down_kernel, trees),
        grid=(hidden // block,),
        in_specs=[
            pl.BlockSpec((total, block), lambda j: (0, j)),
            pl.BlockSpec((total, D), once, pipeline_mode=pl.Buffered(1)),
            pl.BlockSpec((block, D), lambda j: (j, 0)),
            pl.BlockSpec((wide, block), lambda j: (0, j)),
            pl.BlockSpec((wide, D), once),
        ],
        out_specs=[pl.BlockSpec((rows, D), once)] * trees,
        out_shape=[jax.ShapeDtypeStruct((rows, D), BF)] * trees,
        scratch_shapes=[pltpu.VMEM((total, D), F32), pltpu.VMEM((wide, total), F32)],
        compiler_params=params(),
        cost_estimate=pl.CostEstimate(
            flops=2 * total * D * hidden,
            transcendentals=0,
            bytes_accessed=2 * D * hidden + 2 * total * hidden,
        ),
        name="mlp_down",
    )(g, x2, w_down, down_down, up_down)


def by_tree(u_ref, u, rows):
    for m in range(u_ref.shape[0]):
        u_ref[m] = u[m * rows : (m + 1) * rows, m * RANK : (m + 1) * RANK]


def forward_kernel(trees, first, *refs):
    (o_ref, x_ref, norm_ref, dno_ref, upo_ref, wo_ref, wu_ref, wd_ref, upu_ref, dnd_ref, dnu_ref,
     upd_ref, y_ref, x2_ref, b_ref, g_ref, gp_ref, u2_ref, u3_ref, u4_ref,
     sum_ref, acc_ref, mixed_ref, inner_ref) = refs
    step = pl.program_id(0)
    rows = o_ref.shape[0] // trees

    @pl.when(step < first)
    def _():
        mix(step, rows, o_ref, x_ref, dno_ref, upo_ref, wo_ref, mixed_ref, sum_ref)

    @pl.when(step == first - 1)
    def _():
        by_tree(u2_ref, mixed_ref[...], rows)
        x2_ref[...] = sum_ref[...].astype(BF)
        b = normed(sum_ref, norm_ref)
        b_ref[...] = b
        inner = masked(dot(b, dnu_ref[...], NT), rows)
        inner_ref[...] = inner
        by_tree(u3_ref, inner, rows)
        acc_ref[...] = jnp.zeros_like(acc_ref)

    @pl.when(step >= first)
    def _():
        f = dot(b_ref[...], wu_ref[0]) + dot(inner_ref[...], upu_ref[...])
        square, half = gelu_parts(f)
        g = (f * half).astype(BF)
        g_ref[...] = g
        slope = f * ((2 * GELU_C) + (6 * GELU_C * 0.044715) * square)
        gp_ref[...] = (half + (half * (1.0 - half)) * slope).astype(BF)
        sum_ref[...] += dot(g, wd_ref[...])
        acc_ref[...] += dot(dnd_ref[...], g, NT)

    @pl.when(step == pl.num_programs(0) - 1)
    def _():
        u4 = masked(acc_ref[...].T, rows)
        by_tree(u4_ref, u4, rows)
        y_ref[...] = (sum_ref[...] + dot(u4, upd_ref[...])).astype(BF)


def forward_rest(trees, o, x, norm, held, part, w_down, maps, block=512):
    _, _, dn_out, up_out, dn_up, up_up, dn_down, up_down = maps
    total, wide = o.shape[0], trees * RANK
    rows = total // trees
    shards = held.shape[0]
    hidden = shards * part
    block = min(block, part)
    per = part // block
    at = part // (D // shards)
    once = lambda i: (0, 0)
    early = lambda i: jnp.minimum(i, shards - 1)
    late = lambda i: jnp.maximum(i - shards, 0)
    single = pl.Buffered(1)
    full = pl.BlockSpec((total, D), once)
    ranks = pl.BlockSpec((trees, rows, RANK), lambda i: (0, 0, 0))
    return pl.pallas_call(
        functools.partial(forward_kernel, trees, shards),
        grid=(shards + hidden // block,),
        in_specs=[pl.BlockSpec((total, D), once, pipeline_mode=single)] * 2
        + [
            pl.BlockSpec((2, D), once),
            pl.BlockSpec((wide, D), once),
            pl.BlockSpec((wide, D // shards), lambda i: (0, early(i))),
            pl.BlockSpec((1, D, D // shards), lambda i: (early(i), 0, at)),
            pl.BlockSpec((1, D, block), lambda i: (late(i) // per, 0, late(i) % per)),
            pl.BlockSpec((block, D), lambda i: (late(i), 0)),
            pl.BlockSpec((wide, block), lambda i: (0, late(i))),
            pl.BlockSpec((wide, block), lambda i: (0, late(i))),
            pl.BlockSpec((wide, D), once),
            pl.BlockSpec((wide, D), once),
        ],
        out_specs=[
            full,
            full,
            full,
            pl.BlockSpec((total, block), lambda i: (0, late(i))),
            pl.BlockSpec((total, block), lambda i: (0, late(i))),
            ranks,
            ranks,
            ranks,
        ],
        out_shape=[jax.ShapeDtypeStruct((total, D), BF)] * 3
        + [jax.ShapeDtypeStruct((total, hidden), BF)] * 2
        + [jax.ShapeDtypeStruct((trees, rows, RANK), BF)] * 3,
        scratch_shapes=[
            pltpu.VMEM((total, D), F32),
            pltpu.VMEM((wide, total), F32),
            pltpu.VMEM((total, wide), BF),
            pltpu.VMEM((total, wide), BF),
        ],
        compiler_params=params(),
        cost_estimate=pl.CostEstimate(
            flops=4 * total * D * hidden + 2 * total * D * D,
            transcendentals=total * hidden,
            bytes_accessed=4 * D * hidden + 4 * total * hidden + 2 * D * D,
        ),
        name="forward_rest",
    )(o, x, norm, dn_out, up_out, held, held, w_down, up_up, dn_down, dn_up, up_down)


def backward_kernel(given, first, *refs):
    flag_ref, own_ref, *refs = refs
    if given == 2:
        arrived_ref, *refs = refs
    (b_ref, x2_ref, gain_ref, wu_ref, wd_ref, g_ref, gp_ref, u3_ref, u4_ref, upu_ref, dnd_ref,
     dnu_ref, upd_ref, o_ref, u2_ref, dno_ref, upo_ref, wo_ref,
     dr_ref, do_ref, gdno_ref, gupo_ref, gdnu_ref, gupu_ref, gdnd_ref, gupd_ref,
     dy_ref, sum_ref, du4_ref, du3_ref, du2_ref) = refs
    step = pl.program_id(0)

    @pl.when(step == 0)
    def _():
        dy = own_ref[...]
        if given == 2:
            dy = jnp.where(flag_ref[0] == 1, dy, arrived_ref[...])
        dy_ref[...] = dy
        du4_ref[...] = (2.0 * dot(dy, upd_ref[...], NT)).astype(BF)
        gupd_ref[...] = dot(u4_ref[0], dy, TN).astype(BF)
        sum_ref[...] = jnp.zeros_like(sum_ref)
        du3_ref[...] = jnp.zeros_like(du3_ref)

    @pl.when(step < first)
    def _():
        du4 = du4_ref[...]
        dg = dot(dy_ref[...], wd_ref[...], NT) + dot(du4, dnd_ref[...])
        df = (gp_ref[...].astype(F32) * dg).astype(BF)
        gdnd_ref[...] = dot(du4, g_ref[...], TN).astype(BF)
        gupu_ref[...] = dot(u3_ref[0], df, TN).astype(BF)
        du3_ref[...] += dot(upu_ref[...], df, NT)
        sum_ref[...] += dot(df, wu_ref[0], NT)

    @pl.when(step == first - 1)
    def _():
        du3 = (2.0 * du3_ref[...].T).astype(BF)
        gdnu_ref[...] = dot(du3, b_ref[...], TN).astype(BF)
        db = (sum_ref[...] + dot(du3, dnu_ref[...])).astype(BF).astype(F32)
        back = layer_norm_back(x2_ref[...].astype(F32), gain_ref[...], db)
        dr = (dy_ref[...].astype(F32) + back).astype(BF)
        dr_ref[...] = dr
        du2_ref[...] = (2.0 * dot(dr, upo_ref[...], NT)).astype(BF)
        gupo_ref[...] = dot(u2_ref[0], dr, TN).astype(BF)

    @pl.when(step >= first)
    def _():
        wide = wo_ref.shape[2]
        du2 = du2_ref[...]
        do = dot(du2, dno_ref[...])
        for z in range(wo_ref.shape[0]):
            do = do + dot(dr_ref[:, z * wide : (z + 1) * wide], wo_ref[z], NT)
        do_ref[...] = do.astype(BF)
        gdno_ref[...] = dot(du2, o_ref[...], TN).astype(BF)


def backward_rest(
    which, own, b, x2, gain, held, part, w_down, g, gp, u2, u3, u4, o, maps, arrived=None,
    block=1024,
):
    _, _, dn_out, up_out, dn_up, up_up, dn_down, up_down = maps
    rows = u2.shape[1]
    shards = held.shape[0]
    hidden = shards * part
    block = min(block, part)
    per = part // block
    at = part // (D // shards)
    first = hidden // block
    deep = 512
    once = lambda i, w: (0, 0)
    mine = lambda i, w: (w[1], 0)
    early = lambda i: jnp.minimum(i, first - 1)
    late = lambda i: jnp.maximum(i - first, 0)
    single = pl.Buffered(1)
    row = pl.BlockSpec((rows, D), mine, pipeline_mode=single)
    given = 1 if arrived is None else 2
    hid = pl.BlockSpec((rows, block), lambda i, w: (w[1], early(i)))
    thin = pl.BlockSpec((RANK, block), lambda i, w: (w[1], early(i)))
    ranks = pl.BlockSpec((1, rows, RANK), lambda i, w: (w[1], 0, 0))
    across = pl.BlockSpec((RANK, D), mine)
    shape = jax.ShapeDtypeStruct
    dr, do, *grads = pl.pallas_call(
        functools.partial(backward_kernel, given, first),
        grid_spec=pltpu.PrefetchScalarGridSpec(
            num_scalar_prefetch=1,
            grid=(first + D // deep,),
            in_specs=[row]
            + [pl.BlockSpec((rows, D), once, pipeline_mode=single)] * (given - 1)
            + [
                row,
                row,
                pl.BlockSpec((1, D), once),
                pl.BlockSpec((1, D, block), lambda i, w: (early(i) // per, 0, early(i) % per)),
                pl.BlockSpec((block, D), lambda i, w: (early(i), 0)),
                hid,
                hid,
                ranks,
                ranks,
                thin,
                thin,
                across,
                across,
                pl.BlockSpec((rows, deep), lambda i, w: (w[1], late(i))),
                ranks,
                pl.BlockSpec((RANK, deep), lambda i, w: (w[1], late(i))),
                across,
                pl.BlockSpec((shards, deep, D // shards), lambda i, w: (0, late(i), at)),
            ],
            out_specs=[
                pl.BlockSpec((rows, D), once),
                pl.BlockSpec((rows, deep), lambda i, w: (0, late(i))),
                pl.BlockSpec((RANK, deep), lambda i, w: (0, late(i))),
                pl.BlockSpec((RANK, D), once),
                pl.BlockSpec((RANK, D), once),
                pl.BlockSpec((RANK, block), lambda i, w: (0, early(i))),
                pl.BlockSpec((RANK, block), lambda i, w: (0, early(i))),
                pl.BlockSpec((RANK, D), once),
            ],
            scratch_shapes=[
                pltpu.VMEM((rows, D), BF),
                pltpu.VMEM((rows, D), F32),
                pltpu.VMEM((rows, RANK), BF),
                pltpu.VMEM((RANK, rows), F32),
                pltpu.VMEM((rows, RANK), BF),
            ],
        ),
        out_shape=[shape((rows, D), BF)] * 2
        + [shape((RANK, D), BF)] * 3
        + [shape((RANK, hidden), BF)] * 2
        + [shape((RANK, D), BF)],
        compiler_params=params(),
        cost_estimate=pl.CostEstimate(
            flops=4 * rows * D * hidden + 2 * rows * D * D,
            transcendentals=0,
            bytes_accessed=4 * D * hidden + 4 * rows * hidden + 2 * D * D,
        ),
        name="backward_rest",
    )(
        which, own, *([] if arrived is None else [arrived]),
        b, x2, gain, held, w_down, g, gp, u3, u4, up_up, dn_down, dn_up, up_down,
        o, u2, dn_out, up_out, held,
    )
    return dr, do, grads


def segment_of(places, lengths):
    order = jnp.arange(lengths.shape[0], dtype=jnp.int32)
    ends = jnp.sum(
        jnp.where(order[None, :] <= order[:, None], lengths[None, :], 0), axis=1, dtype=jnp.int32
    )
    return jnp.sum((places[:, None] >= ends[None, :]).astype(jnp.int32), axis=1, dtype=jnp.int32)


def ancestry(parents):
    seg_ids = jnp.arange(parents.shape[0], dtype=jnp.int32)
    current = seg_ids
    reach = current[:, None] == seg_ids[None, :]
    for sweep in range(parents.shape[0] - 1):
        current = jnp.sum(
            jnp.where(current[:, None] == seg_ids[None, :], parents[None, :], 0),
            axis=1,
            dtype=jnp.int32,
        )
        reach = reach | (current[:, None] == seg_ids[None, :])
    return reach.astype(BF)


def key_bias(lengths, parents, query_places, key_places):
    seg_ids = jnp.arange(parents.shape[0], dtype=jnp.int32)
    of_query = (segment_of(query_places, lengths)[:, None] == seg_ids[None, :]).astype(BF)
    of_key = (segment_of(key_places, lengths)[:, None] == seg_ids[None, :]).astype(BF)
    known = ancestry(parents)

    def bias(rows_in, rows_out, place_query, place_key):
        reach = dot(rows_in, rows_out, NT)
        allowed = (reach > 0.5) & (place_key <= place_query) & (place_key >= 0)
        return jnp.where(allowed, 0.0, MASKED).astype(F32)

    anc = dot(of_query, known).astype(BF)
    return (
        bias(anc, of_key, query_places[:, None], key_places[None, :]),
        bias(of_key, anc, query_places[None, :], key_places[:, None]),
    )


def shifted(value, axis, steps):
    count = lax.axis_size(axis)
    return lax.ppermute(value, axis, [(i, (i + steps) % count) for i in range(count)])


def local(
    inputs, cotangent, norm_gains, norm_biases, w_attn, w_out, w_up, w_down,
    down_attn, up_attn, down_out, up_out, down_up, up_up, down_down, up_down,
    seg_lengths, parent_ids, adapter_ids,
):
    section = lax.axis_index("section")
    shard = lax.axis_index("fsdp")
    member = lax.axis_index("replica")
    shards = lax.axis_size("fsdp")
    members = lax.axis_size("replica")
    trees, per_tree = inputs.shape[0], inputs.shape[1]
    gain = norm_gains[0].astype(F32)
    shift = norm_biases[0].astype(F32)
    norms = [jnp.stack([gain[i], shift[i]]) for i in range(2)]
    is_first = (section == 0).astype(jnp.int32).reshape(1)

    def quarter(weight):
        part = weight.shape[0] // members
        return lax.dynamic_slice_in_dim(weight, member * part, part, 0)

    def gathered(own):
        return lax.all_gather(own[None], ("fsdp", "replica"), axis=1, tiled=True)[0]

    part, out_wide, attn_wide = w_up.shape[2], w_out.shape[2], w_attn.shape[2]
    padded = -(-attn_wide // 128) * 128
    attn_at = -(-(part + out_wide) // padded) * padded
    each = D // members
    own = jnp.concatenate(
        [
            quarter(w_up[0]),
            quarter(w_out[0]),
            jnp.zeros((each, attn_at - part - out_wide), BF),
            quarter(w_attn[0]),
            jnp.zeros((each, padded - attn_wide), BF),
        ],
        axis=1,
    )
    held = gathered(own).reshape(shards, D, own.shape[1])
    down_full = gathered(quarter(w_down[0]))
    attn_full = assemble(held, attn_at, attn_wide)

    stacks = (down_attn, up_attn, down_out, up_out, down_up, up_up, down_down, up_down)
    widths = [stack.shape[3] for stack in stacks]
    starts = [sum(widths[:i]) for i in range(len(widths))]
    chosen = adapter_ids[:, 0, 0]
    picked = jnp.concatenate(
        [
            jnp.concatenate(
                [lax.dynamic_index_in_dim(stack[0], chosen[m], 0, keepdims=False) for m in range(trees)],
                axis=0,
            )
            for stack in stacks
        ],
        axis=1,
    )
    owners = lax.all_gather(chosen, "replica", axis=0, tiled=True)
    owners, picked = lax.optimization_barrier((owners, picked))
    behind = jnp.stack([picked] + [shifted(picked, "fsdp", k) for k in range(1, shards)])
    ordered = [
        lax.dynamic_index_in_dim(behind, lax.rem(shard - z + shards, shards), 0, keepdims=False)
        for z in range(shards)
    ]
    maps = [
        jnp.concatenate([piece[:, at : at + width] for piece in ordered], axis=1)
        for at, width in zip(starts, widths)
    ]
    dn_attn, up_attn_, dn_out, up_out_, dn_up, up_up_, dn_down, up_down_ = maps

    query_places = shard * per_tree + jnp.arange(per_tree, dtype=jnp.int32)
    key_places = jnp.concatenate(
        [(shard - s) * per_tree + jnp.arange(per_tree, dtype=jnp.int32) for s in range(shards)]
    )
    biases = [
        key_bias(seg_lengths[m, 0], parent_ids[m, 0], query_places, key_places)
        for m in range(trees)
    ]

    def to_higher(value, steps):
        return lax.ppermute(value, "fsdp", [(i, i + steps) for i in range(shards - steps)])

    def to_lower(value, steps):
        return lax.ppermute(value, "fsdp", [(i + steps, i) for i in range(shards - steps)])

    def with_lower(kv):
        return [kv] + [to_higher(kv, s) for s in range(1, shards)]

    own_rows = inputs.reshape(trees * per_tree, D)
    before = ()
    for m in range(trees):
        a, u1, kv = entry(m, trees, own_rows, norms[0], dn_attn, up_attn_, attn_full)
        blocks = with_lower(kv)
        before = attention_forward(
            m, trees, queries(m, a, u1, up_attn_, attn_full), blocks, biases[m][0], before, False
        )
    x2, b = mixing(before[0], own_rows, norms[1], dn_out, up_out_, held, part)
    g = mlp_up(b, held, part, up_up_, dn_up)
    sent = mlp_down(trees, g, x2, down_full, dn_down, up_down_)
    arrived = [lax.ppermute(rows, "section", [(0, 1)]) for rows in sent]
    entered, attended = (), ()
    for m in range(trees):
        rows = arrived[m]
        if m:
            rows, attended = lax.optimization_barrier((rows, attended))
        a, u1, kv, *entered = entry(
            m, trees, own_rows, norms[0], dn_attn, up_attn_, attn_full, rows, is_first, entered
        )
        blocks = with_lower(kv)
        attended = attention_forward(
            m, trees, queries(m, a, u1, up_attn_, attn_full), blocks, biases[m][0], attended, True
        )
    x, a, u1 = entered
    o, lse, q, *blocks = attended
    layer_out, x2, b, g, gp, u2, u3, u4 = forward_rest(
        trees, o, x, norms[1], held, part, down_full, maps
    )
    bias = jnp.concatenate([pair[1] for pair in biases], axis=0)

    def by_shard(grads, parts):
        return jnp.stack(
            [
                jnp.concatenate(
                    [g[:, z * part : (z + 1) * part] for g, part in zip(grads, parts)], axis=1
                )
                for z in range(shards)
            ]
        )

    def scattered(slabs):
        return lax.psum_scatter(slabs, "fsdp", scatter_dimension=0)

    def permuted(slabs):
        total = lax.dynamic_index_in_dim(slabs, shard, 0, keepdims=False).astype(F32)
        for k in range(1, shards):
            part = lax.dynamic_index_in_dim(slabs, lax.rem(shard + k, shards), 0, keepdims=False)
            total = total + shifted(part, "fsdp", k).astype(F32)
        return total.astype(BF)

    def all_replicas(total):
        return jnp.stack([total] + [shifted(total, "replica", i) for i in range(1, members)])

    own_grads = cotangent.reshape(trees * per_tree, D)
    order = lax.rem(member - jnp.arange(members, dtype=jnp.int32) + members, members)
    cyclic = owners.reshape(members, trees)[order].reshape(-1)
    in_grads, sums, arrived, before, total, ready = [], [], None, None, None, None
    for step in range(trees + 1):
        tree = jnp.clip(step - 1 + section, 0, trees - 1)
        which = jnp.stack([section, tree]).astype(jnp.int32)
        if arrived is None:
            which = jnp.array([1, 0], jnp.int32)
        total = None
        if ready is not None:
            arrived, ready = lax.optimization_barrier((arrived, ready))
            in_grads.append(ready[0])
            total = scattered(ready[1])
        dr, do, early = backward_rest(
            which, own_grads, b, x2, gain[1:2], held, part, down_full, g, gp, u2, u3, u4,
            o, maps, arrived,
        )
        if total is not None:
            do, total = lax.optimization_barrier((do, total))
            total = all_replicas(total)
        if step == trees:
            slabs = by_shard(early, widths[2:])
            do, slabs = lax.optimization_barrier((do, slabs))
            early_sum = scattered(slabs)
        dq, dkv = attention_backward(which, q, do, o, blocks, bias, lse)
        dkv = [dkv[0]] + [to_lower(dkv[s], s) for s in range(1, shards)]
        da, du, g_up_q = query_leaving(which, dq, u1, up_attn_, attn_full)
        if total is not None:
            da, total = lax.optimization_barrier((da, total))
            sums.append((step - 2, total))
        dx, g_dn, g_up_kv = leaving(
            which, da, du, dkv, a, u1, x, dr, gain[0:1], dn_attn, up_attn_, attn_full
        )
        if step < trees:
            arrived = lax.ppermute(dx, "section", [(1, 0)])
        late = (g_dn, jnp.concatenate([g_up_q, g_up_kv], axis=1))
        now = (dx, *late, *early)
        ready = None
        if 0 < step < trees:
            dx_ready, *grads = (
                jnp.where(section == 1, was, new) for was, new in zip(before, now)
            )
            ready = (dx_ready, by_shard(grads, widths))
        before = now
    in_grads.append(dx)
    late_sum = permuted(by_shard(late, widths[:2]))
    sums.append((trees - 1, all_replicas(jnp.concatenate([late_sum, early_sum], axis=1))))

    finals = []
    names = jnp.arange(down_attn.shape[1], dtype=jnp.int32)[:, None, None]
    for at, width in zip(starts, widths):
        total = jnp.zeros((down_attn.shape[1], RANK, width), F32)
        for m, slabs in sums:
            for r in range(members):
                addend = slabs[r, :, at : at + width].astype(F32)[None]
                total = total + jnp.where(names == cyclic[r * trees + m], addend, 0.0)
        finals.append(total[None])
    return (
        layer_out.reshape(1, trees, per_tree, D),
        jnp.stack(in_grads)[None],
        *finals,
    )


def solution(mesh):
    rows = P(None, ("replica", "fsdp"), None)
    stack = P("section", None, None, "fsdp")
    placed = (
        (rows, rows)
        + (P("section", None, None),) * 2
        + (P("section", None, "fsdp"),) * 3
        + (P("section", "fsdp", None),)
        + (stack,) * 8
        + (P(None, "replica", None),) * 3
    )
    return jax.shard_map(
        local,
        mesh=mesh,
        in_specs=placed,
        out_specs=(P("section", None, ("replica", "fsdp"), None),) * 2 + (stack,) * 8,
        check_vma=False,
    )
```

```python
import functools
import math

import jax
import jax.numpy as jnp
from jax import lax
from jax.experimental import pallas as pl
from jax.experimental.pallas import tpu as pltpu
from jax.sharding import PartitionSpec as P

D = 2048
HEADS = 16
HEAD_DIM = 128
RANK = 16

NORM_EPS = 1e-05
MASKED = -1e30
BF = jnp.bfloat16
F32 = jnp.float32
INV_ROOT = HEAD_DIM ** (-0.5)
LOG2E = math.log2(math.e)
LN2 = math.log(2.0)
GELU_C = math.sqrt(2.0 / math.pi)
VMEM_LIMIT = 56 * 1024 * 1024

NN = (((1,), (0,)), ((), ()))
NT = (((1,), (1,)), ((), ()))
TN = (((0,), (0,)), ((), ()))


def dot(left, right, dims=NN):
    return lax.dot_general(left, right, dims, preferred_element_type=F32)


def params(steps=1):
    return pltpu.CompilerParams(
        dimension_semantics=("arbitrary",) * steps, vmem_limit_bytes=VMEM_LIMIT
    )


def layer_norm(rows, gain, shift):
    centre = rows - jnp.mean(rows, axis=-1, keepdims=True)
    spread = jnp.mean(centre * centre, axis=-1, keepdims=True)
    return centre * lax.rsqrt(spread + NORM_EPS) * gain + shift


def layer_norm_back(rows, gain, grad):
    centre = rows - jnp.mean(rows, axis=-1, keepdims=True)
    spread = jnp.mean(centre * centre, axis=-1, keepdims=True)
    scale = lax.rsqrt(spread + NORM_EPS)
    unit = centre * scale
    inner = grad * gain
    return scale * (
        inner
        - jnp.mean(inner, axis=-1, keepdims=True)
        - unit * jnp.mean(inner * unit, axis=-1, keepdims=True)
    )


def tree_mask(rows, per_tree):
    row = lax.broadcasted_iota(jnp.int32, (rows, (rows // per_tree) * RANK), 0)
    col = lax.broadcasted_iota(jnp.int32, (rows, (rows // per_tree) * RANK), 1)
    return (row // per_tree) == (col // RANK)


def masked(value, per_tree):
    return jnp.where(tree_mask(value.shape[0], per_tree), 2.0 * value, 0.0).astype(BF)


def attention_forward_kernel(blocks, heads, before, keep, q_ref, *refs):
    kv_refs, (bias_ref, *refs) = refs[:blocks], refs[blocks:]
    o_ref, lse_ref, *kept_refs = refs[before:]
    keys = jnp.concatenate([r[:, :HEAD_DIM] for r in kv_refs], axis=0)
    vals = jnp.concatenate([r[:, HEAD_DIM:] for r in kv_refs], axis=0)
    vals = jnp.concatenate([vals, jnp.ones_like(vals)], axis=1)
    if keep:
        kept_refs[0][...] = q_ref[...]
    for h in range(heads):
        cols = slice(h * HEAD_DIM, (h + 1) * HEAD_DIM)
        scores = dot(q_ref[:, cols], keys, NT) + bias_ref[...]
        top = jnp.max(scores, axis=1, keepdims=True)
        probs = jnp.exp2(scores - top)
        mixed = dot(probs.astype(BF), vals)
        total = mixed[:, HEAD_DIM:]
        o_ref[:, cols] = (mixed[:, :HEAD_DIM] / total).astype(BF)
        lse_ref[0, h : h + 1, :] = (top + jnp.log2(total)).T[0:1, :]


def attention_forward(tree, trees, q, kv, bias, before, keep, heads=8):
    rows = q.shape[0]
    blocks = len(kv)
    wide = heads * HEAD_DIM
    steps = HEADS // heads
    mine = pl.BlockSpec((rows, wide), lambda i: (tree, i))
    tall = jax.ShapeDtypeStruct((trees * rows, D), BF)
    outs = [tall, jax.ShapeDtypeStruct((trees * steps, heads, rows), F32)]
    out_specs = [mine, pl.BlockSpec((1, heads, rows), lambda i: (tree * steps + i, 0, 0))]
    if keep:
        outs.append(tall)
        out_specs.append(mine)
    return pl.pallas_call(
        functools.partial(attention_forward_kernel, blocks, heads, len(before), keep),
        grid=(steps,),
        in_specs=[pl.BlockSpec((rows, wide), lambda i: (0, i))]
        + [pl.BlockSpec((rows, 2 * HEAD_DIM), lambda i: (tree, 0))] * blocks
        + [pl.BlockSpec((rows, blocks * rows), lambda i: (0, 0))]
        + [pl.BlockSpec(memory_space=pl.ANY)] * len(before),
        out_specs=out_specs,
        out_shape=outs,
        input_output_aliases={blocks + 2 + i: i for i in range(len(before))},
        compiler_params=params(),
        cost_estimate=pl.CostEstimate(
            flops=8 * rows * rows * blocks * D,
            transcendentals=rows * rows * blocks * HEADS,
            bytes_accessed=4 * rows * D + 4 * rows * rows * blocks,
        ),
        name="attention_forward",
    )(q, *kv, bias, *before)


def attention_backward_kernel(blocks, heads, _, q_ref, do_ref, o_ref, *refs):
    kv_refs = refs[:blocks]
    bias_ref, lse_ref, dq_ref, *dkv_refs, acc_ref = refs[blocks:]
    rows = q_ref.shape[0]
    step = pl.program_id(0)

    @pl.when(step == 0)
    def _():
        acc_ref[...] = jnp.zeros_like(acc_ref)

    keys = jnp.concatenate([r[:, :HEAD_DIM] for r in kv_refs], axis=0)
    vals = jnp.concatenate([r[:, HEAD_DIM:] for r in kv_refs], axis=0)
    keys_t = keys.T
    for h in range(heads):
        cols = slice(h * HEAD_DIM, (h + 1) * HEAD_DIM)
        q, do = q_ref[:, cols], do_ref[:, cols]
        delta = jnp.sum(
            (do.astype(F32) * o_ref[:, cols].astype(F32)).T, axis=0, keepdims=True
        )
        scores = dot(keys, q, NT) + bias_ref[...]
        probs = jnp.exp2(scores - lse_ref[0, h : h + 1, :])
        dprobs = dot(vals, do, NT)
        dscores = (probs * (dprobs - delta)).astype(BF)
        acc_ref[:, :HEAD_DIM] += dot(dscores, q)
        acc_ref[:, HEAD_DIM:] += dot(probs.astype(BF), do)
        dq_ref[:, cols] = (dot(keys_t, dscores) * INV_ROOT).T.astype(BF)

    @pl.when(step == pl.num_programs(0) - 1)
    def _():
        for s in range(blocks):
            part = slice(s * rows, (s + 1) * rows)
            dkv_refs[s][:, :HEAD_DIM] = (acc_ref[part, :HEAD_DIM] * LN2).astype(BF)
            dkv_refs[s][:, HEAD_DIM:] = acc_ref[part, HEAD_DIM:].astype(BF)


def attention_backward(which, q, do, o, kv, bias, lse):
    rows = do.shape[0]
    blocks = len(kv)
    trees = q.shape[0] // rows
    heads = lse.shape[1]
    steps = lse.shape[0] // trees
    wide = heads * HEAD_DIM
    mine = lambda i, w: (w[1], i)
    pair = pl.BlockSpec((rows, 2 * HEAD_DIM), lambda i, w: (0, 0))
    dq, *dkv = pl.pallas_call(
        functools.partial(attention_backward_kernel, blocks, heads),
        grid_spec=pltpu.PrefetchScalarGridSpec(
            num_scalar_prefetch=1,
            grid=(steps,),
            in_specs=[
                pl.BlockSpec((rows, wide), mine),
                pl.BlockSpec((rows, wide), lambda i, w: (0, i)),
                pl.BlockSpec((rows, wide), mine),
            ]
            + [pl.BlockSpec((rows, 2 * HEAD_DIM), lambda i, w: (w[1], 0))] * blocks
            + [
                pl.BlockSpec((blocks * rows, rows), lambda i, w: (w[1], 0)),
                pl.BlockSpec((1, heads, rows), lambda i, w: (w[1] * steps + i, 0, 0)),
            ],
            out_specs=[pl.BlockSpec((rows, wide), lambda i, w: (0, i))] + [pair] * blocks,
            scratch_shapes=[pltpu.VMEM((blocks * rows, 2 * HEAD_DIM), F32)],
        ),
        out_shape=[jax.ShapeDtypeStruct((rows, D), BF)]
        + [jax.ShapeDtypeStruct((rows, 2 * HEAD_DIM), BF)] * blocks,
        compiler_params=params(),
        cost_estimate=pl.CostEstimate(
            flops=20 * rows * rows * blocks * D,
            transcendentals=rows * rows * blocks * HEADS,
            bytes_accessed=8 * rows * D + 4 * rows * rows * blocks,
        ),
        name="attention_backward",
    )(which, q, do, o, *kv, bias, lse)
    return dq, dkv


def pack_kernel(at, _, up_ref, out_ref, attn_ref, all_ref):
    part, wide = up_ref.shape[1], attn_ref.shape[0]
    after = part + out_ref.shape[1]
    all_ref[:, :part] = up_ref[...]
    all_ref[:, part:after] = out_ref[...]
    if at > after:
        all_ref[:, after:at] = jnp.zeros((all_ref.shape[0], at - after), BF)
    attn = attn_ref[...].T
    spare = all_ref.shape[1] - at - wide
    if spare:
        attn = jnp.concatenate([attn, jnp.zeros((attn.shape[0], spare), BF)], axis=1)
    all_ref[:, at:] = attn


def pack(member, each, up, out, attn_t, at, total):
    return pl.pallas_call(
        functools.partial(pack_kernel, at),
        grid_spec=pltpu.PrefetchScalarGridSpec(
            num_scalar_prefetch=1,
            grid=(1,),
            in_specs=[
                pl.BlockSpec((each, up.shape[1]), lambda i, w: (w[0], 0)),
                pl.BlockSpec((each, out.shape[1]), lambda i, w: (w[0], 0)),
                pl.BlockSpec((attn_t.shape[0], each), lambda i, w: (0, w[0])),
            ],
            out_specs=pl.BlockSpec((each, total), lambda i, w: (0, 0)),
        ),
        out_shape=jax.ShapeDtypeStruct((each, total), BF),
        compiler_params=params(),
        cost_estimate=pl.CostEstimate(
            flops=0, transcendentals=0, bytes_accessed=4 * each * total
        ),
        name="pack",
    )(member.astype(jnp.int32).reshape(1), up, out, attn_t)


def assemble_kernel(wide, held_ref, full_ref):
    full_ref[...] = jnp.concatenate(
        [held_ref[z][:, :wide] for z in range(held_ref.shape[0])], axis=1
    )


def assemble(held, start, wide, block=256):
    shards, depth, _ = held.shape
    padded = -(-wide // 128) * 128
    return pl.pallas_call(
        functools.partial(assemble_kernel, wide),
        grid=(depth // block,),
        in_specs=[pl.BlockSpec((shards, block, padded), lambda i: (0, i, start // padded))],
        out_specs=pl.BlockSpec((block, shards * wide), lambda i: (i, 0)),
        out_shape=jax.ShapeDtypeStruct((depth, shards * wide), BF),
        compiler_params=params(),
        cost_estimate=pl.CostEstimate(
            flops=0, transcendentals=0, bytes_accessed=4 * shards * depth * padded
        ),
        name="assemble",
    )(held)


def ranks_of(rows, norm_ref, dn_ref):
    a = layer_norm(rows.astype(F32), norm_ref[0:1, :], norm_ref[1:2, :]).astype(BF)
    return a, dot(a, dn_ref[...], NT)


def entry_kernel(x_ref, norm_ref, dn_ref, up_ref, w_ref, a_ref, u_ref, kv_ref):
    a, u = ranks_of(x_ref[...], norm_ref, dn_ref)
    a_ref[...] = a
    u = (2.0 * u).astype(BF)
    u_ref[...] = u
    kv_ref[...] = (dot(a, w_ref[...]) + dot(u, up_ref[...])).astype(BF)


def entry(tree, trees, x, norm, dn, up, w):
    rows = x.shape[0] // trees
    wide = 2 * HEAD_DIM
    last = D // wide
    whole = lambda i: (0, 0)
    return pl.pallas_call(
        entry_kernel,
        grid=(1,),
        in_specs=[
            pl.BlockSpec((rows, D), lambda i: (tree, 0)),
            pl.BlockSpec((2, D), whole),
            pl.BlockSpec((RANK, D), lambda i: (tree, 0)),
            pl.BlockSpec((RANK, wide), lambda i: (tree, last)),
            pl.BlockSpec((D, wide), lambda i: (0, last)),
        ],
        out_specs=[
            pl.BlockSpec((rows, D), whole),
            pl.BlockSpec((rows, RANK), whole),
            pl.BlockSpec((rows, wide), whole),
        ],
        out_shape=[
            jax.ShapeDtypeStruct((rows, D), BF),
            jax.ShapeDtypeStruct((rows, RANK), BF),
            jax.ShapeDtypeStruct((rows, wide), BF),
        ],
        compiler_params=params(),
        cost_estimate=pl.CostEstimate(
            flops=3 * rows * D * wide, transcendentals=0, bytes_accessed=8 * rows * D
        ),
        name="entry",
    )(x, norm, dn, up, w)


def enter_kernel(before, flag_ref, own_ref, arrived_ref, norm_ref, dn_ref, *refs):
    a_ref, u_ref, x_all, a_all, u_all = refs[before:]
    x = jnp.where(flag_ref[0] == 1, own_ref[...], arrived_ref[...])
    x_all[...] = x
    a, u = ranks_of(x, norm_ref, dn_ref)
    a_ref[...] = a
    a_all[...] = a
    u = (2.0 * u).astype(BF)
    u_ref[...] = u
    u_all[0] = u


def enter(tree, trees, own, arrived, flag, norm, dn, before):
    rows = own.shape[0] // trees
    whole = lambda i, f: (0, 0)
    mine = pl.BlockSpec((rows, D), lambda i, f: (tree, 0))
    row = pl.BlockSpec((rows, D), whole)
    return pl.pallas_call(
        functools.partial(enter_kernel, len(before)),
        grid_spec=pltpu.PrefetchScalarGridSpec(
            num_scalar_prefetch=1,
            grid=(1,),
            in_specs=[
                mine,
                row,
                pl.BlockSpec((2, D), whole),
                pl.BlockSpec((RANK, D), lambda i, f: (tree, 0)),
            ]
            + [pl.BlockSpec(memory_space=pl.ANY)] * len(before),
            out_specs=[
                row,
                pl.BlockSpec((rows, RANK), whole),
                mine,
                mine,
                pl.BlockSpec((1, rows, RANK), lambda i, f: (tree, 0, 0)),
            ],
        ),
        out_shape=[
            jax.ShapeDtypeStruct((rows, D), BF),
            jax.ShapeDtypeStruct((rows, RANK), BF),
            jax.ShapeDtypeStruct((trees * rows, D), BF),
            jax.ShapeDtypeStruct((trees * rows, D), BF),
            jax.ShapeDtypeStruct((trees, rows, RANK), BF),
        ],
        input_output_aliases={5 + i: 2 + i for i in range(len(before))},
        compiler_params=params(),
        cost_estimate=pl.CostEstimate(
            flops=2 * rows * D * 256, transcendentals=0, bytes_accessed=10 * rows * D
        ),
        name="enter",
    )(flag, own, arrived, norm, dn, *before)


def queries_kernel(a_ref, u_ref, up_ref, w_ref, q_ref):
    q = dot(a_ref[...], w_ref[...]) + dot(u_ref[...], up_ref[...])
    q_ref[...] = (q * (INV_ROOT * LOG2E)).astype(BF)


def queries(tree, a, u, up, w, block=1024):
    rows = a.shape[0]
    return pl.pallas_call(
        queries_kernel,
        grid=(D // block,),
        in_specs=[
            pl.BlockSpec((rows, D), lambda i: (0, 0)),
            pl.BlockSpec((rows, RANK), lambda i: (0, 0)),
            pl.BlockSpec((RANK, block), lambda i: (tree, i)),
            pl.BlockSpec((D, block), lambda i: (0, i)),
        ],
        out_specs=pl.BlockSpec((rows, block), lambda i: (0, i)),
        out_shape=jax.ShapeDtypeStruct((rows, D), BF),
        compiler_params=params(),
        cost_estimate=pl.CostEstimate(
            flops=2 * rows * D * D, transcendentals=0, bytes_accessed=2 * D * D
        ),
        name="queries",
    )(a, u, up, w)


def mix(step, rows, o_ref, x_ref, dn_ref, up_ref, w_ref, u_ref, sum_ref):
    @pl.when(step == 0)
    def _():
        sum_ref[...] = x_ref[...].astype(F32)
        u_ref[...] = masked(dot(o_ref[...], dn_ref[...], NT), rows)

    block = w_ref.shape[2]
    cols = pl.ds(pl.multiple_of(step * block, block), block)
    sum_ref[:, cols] += dot(o_ref[...], w_ref[0]) + dot(u_ref[...], up_ref[...])


def normed(sum_ref, norm_ref):
    return layer_norm(sum_ref[...], norm_ref[0:1, :], norm_ref[1:2, :]).astype(BF)


def mixing_kernel(rows, o_ref, x_ref, norm_ref, dn_ref, up_ref, w_ref, x2_ref, b_ref, u_ref):
    step = pl.program_id(0)
    mix(step, rows, o_ref, x_ref, dn_ref, up_ref, w_ref, u_ref, x2_ref)

    @pl.when(step == pl.num_programs(0) - 1)
    def _():
        b_ref[...] = normed(x2_ref, norm_ref)


def mixing(o, x, norm, dn, up, held, part):
    total, wide = o.shape[0], dn.shape[0]
    shards = held.shape[0]
    block = D // shards
    at = part // block
    whole = lambda i: (0, 0)
    single = pl.Buffered(1)
    return pl.pallas_call(
        functools.partial(mixing_kernel, total * RANK // wide),
        grid=(shards,),
        in_specs=[pl.BlockSpec((total, D), whole, pipeline_mode=single)] * 2
        + [
            pl.BlockSpec((2, D), whole),
            pl.BlockSpec((wide, D), whole),
            pl.BlockSpec((wide, block), lambda i: (0, i)),
            pl.BlockSpec((1, D, block), lambda i: (i, 0, at)),
        ],
        out_specs=[pl.BlockSpec((total, D), whole), pl.BlockSpec((total, D), whole)],
        out_shape=[
            jax.ShapeDtypeStruct((total, D), F32),
            jax.ShapeDtypeStruct((total, D), BF),
        ],
        scratch_shapes=[pltpu.VMEM((total, wide), BF)],
        compiler_params=params(),
        cost_estimate=pl.CostEstimate(
            flops=2 * total * D * D, transcendentals=0, bytes_accessed=2 * D * D + 10 * total * D
        ),
        name="mixing",
    )(o, x, norm, dn, up, held)


def query_leaving_kernel(_, dq_ref, up_ref, w_ref, da_ref, du_ref):
    @pl.when(pl.program_id(0) == 0)
    def _():
        du_ref[...] = dot(dq_ref[...], up_ref[...], NT)

    da_ref[...] = dot(dq_ref[...], w_ref[...], NT)


def query_leaving(which, dq, up, w, block=1024):
    rows = dq.shape[0]
    whole = lambda i, w: (0, 0)
    return pl.pallas_call(
        query_leaving_kernel,
        grid_spec=pltpu.PrefetchScalarGridSpec(
            num_scalar_prefetch=1,
            grid=(D // block,),
            in_specs=[
                pl.BlockSpec((rows, D), whole),
                pl.BlockSpec((RANK, D), lambda i, w: (w[1], 0)),
                pl.BlockSpec((block, D), lambda i, w: (i, 0)),
            ],
            out_specs=[
                pl.BlockSpec((rows, block), lambda i, w: (0, i)),
                pl.BlockSpec((rows, RANK), whole),
            ],
        ),
        out_shape=[
            jax.ShapeDtypeStruct((rows, D), F32),
            jax.ShapeDtypeStruct((rows, RANK), F32),
        ],
        compiler_params=params(),
        cost_estimate=pl.CostEstimate(
            flops=2 * rows * D * D, transcendentals=0, bytes_accessed=2 * D * D
        ),
        name="query_leaving",
    )(which, dq, up, w)


def leaving_kernel(blocks, _, dq_ref, da_ref, du_ref, *refs):
    dkv_refs = refs[:blocks]
    (a_ref, u_ref, x_ref, dr_ref, gain_ref, dn_ref, up_ref, w_ref,
     dx_ref, gdn_ref, gup_ref) = refs[blocks:]
    total = dkv_refs[0][...].astype(F32)
    for ref in dkv_refs[1:]:
        total = total + ref[...].astype(F32)
    dkv = total.astype(BF)
    du = (2.0 * (du_ref[...] + dot(dkv, up_ref[...], NT))).astype(BF)
    gup_ref[:, :D] = dot(u_ref[0], dq_ref[...], TN).astype(BF)
    gup_ref[:, D:] = dot(u_ref[0], dkv, TN).astype(BF)
    gdn_ref[...] = dot(du, a_ref[...], TN).astype(BF)
    da = da_ref[...] + dot(dkv, w_ref[...], NT) + dot(du, dn_ref[...])
    back = layer_norm_back(
        x_ref[...].astype(F32), gain_ref[...], da.astype(BF).astype(F32)
    )
    dx_ref[...] = (dr_ref[...].astype(F32) + back).astype(BF)


def leaving(which, dq, da, du, dkv, a, u, x, dr, gain, dn, up, w):
    rows = da.shape[0]
    wide = 2 * HEAD_DIM
    last = D // wide
    whole = lambda i, w: (0, 0)
    mine = lambda i, w: (w[1], 0)
    return pl.pallas_call(
        functools.partial(leaving_kernel, len(dkv)),
        grid_spec=pltpu.PrefetchScalarGridSpec(
            num_scalar_prefetch=1,
            grid=(1,),
            in_specs=[pl.BlockSpec((rows, D), whole)] * 2
            + [pl.BlockSpec((rows, RANK), whole)]
            + [pl.BlockSpec((rows, wide), whole)] * len(dkv)
            + [
                pl.BlockSpec((rows, D), mine),
                pl.BlockSpec((1, rows, RANK), lambda i, w: (w[1], 0, 0)),
                pl.BlockSpec((rows, D), mine),
                pl.BlockSpec((rows, D), whole),
                pl.BlockSpec((1, D), whole),
                pl.BlockSpec((RANK, D), mine),
                pl.BlockSpec((RANK, wide), lambda i, w: (w[1], last)),
                pl.BlockSpec((D, wide), lambda i, w: (0, last)),
            ],
            out_specs=[
                pl.BlockSpec((rows, D), whole),
                pl.BlockSpec((RANK, D), whole),
                pl.BlockSpec((RANK, D + wide), whole),
            ],
        ),
        out_shape=[
            jax.ShapeDtypeStruct((rows, D), BF),
            jax.ShapeDtypeStruct((RANK, D), BF),
            jax.ShapeDtypeStruct((RANK, D + wide), BF),
        ],
        compiler_params=params(),
        cost_estimate=pl.CostEstimate(
            flops=4 * rows * D * wide, transcendentals=0, bytes_accessed=14 * rows * D
        ),
        name="leaving",
    )(which, dq, da, du, *dkv, a, u, x, dr, gain, dn, up, w)


def gelu_parts(f):
    square = f * f
    half = 0.5 + 0.5 * jnp.tanh(f * (GELU_C + (GELU_C * 0.044715) * square))
    return square, half


def mlp_up_kernel(per_tree, b_ref, wu_ref, upu_ref, dnu_ref, g_ref, u3_ref):
    @pl.when(pl.program_id(0) == 0)
    def _():
        u3_ref[...] = masked(dot(b_ref[...], dnu_ref[...], NT), per_tree)

    f = dot(b_ref[...], wu_ref[0]) + dot(u3_ref[...], upu_ref[...])
    g_ref[...] = (f * gelu_parts(f)[1]).astype(BF)


def mlp_up(b, held, part, up_up, down_up, block=1024):
    rows = b.shape[0]
    shards = held.shape[0]
    hidden = shards * part
    wide = down_up.shape[0]
    block = min(block, part)
    per = part // block
    once = lambda j: (0, 0)
    return pl.pallas_call(
        functools.partial(mlp_up_kernel, rows * RANK // wide),
        grid=(hidden // block,),
        in_specs=[
            pl.BlockSpec((rows, D), once),
            pl.BlockSpec((1, D, block), lambda j: (j // per, 0, j % per)),
            pl.BlockSpec((wide, block), lambda j: (0, j)),
            pl.BlockSpec((wide, D), once),
        ],
        out_specs=pl.BlockSpec((rows, block), lambda j: (0, j)),
        out_shape=jax.ShapeDtypeStruct((rows, hidden), BF),
        scratch_shapes=[pltpu.VMEM((rows, wide), BF)],
        compiler_params=params(),
        cost_estimate=pl.CostEstimate(
            flops=2 * rows * D * hidden,
            transcendentals=rows * hidden,
            bytes_accessed=2 * D * hidden + 2 * rows * hidden,
        ),
        name="mlp_up",
    )(b, held, up_up, down_up)


def mlp_down_kernel(
    trees, g_ref, x2_ref, wd_ref, dnd_ref, upd_ref, norm_ref, dn_ref, up_ref, w_ref, *refs
):
    y_refs, (kv_ref, sum_ref, acc_ref) = refs[:trees], refs[trees:]
    step = pl.program_id(0)
    rows = g_ref.shape[0] // trees

    @pl.when(step == 0)
    def _():
        sum_ref[...] = x2_ref[...]
        acc_ref[...] = jnp.zeros_like(acc_ref)

    g = g_ref[...]
    sum_ref[...] += dot(g, wd_ref[...])
    acc_ref[...] += dot(dnd_ref[...], g, NT)

    @pl.when(step == pl.num_programs(0) - 1)
    def _():
        u4 = masked(acc_ref[...].T, rows)
        y = (sum_ref[...] + dot(u4, upd_ref[...])).astype(BF)
        for m in range(trees):
            y_refs[m][...] = y[m * rows : (m + 1) * rows]
        a, u = ranks_of(y, norm_ref, dn_ref)
        kv_ref[...] = (dot(a, w_ref[...]) + dot(masked(u, rows), up_ref[...])).astype(BF)


def mlp_down(trees, g, x2, w_down, down_down, up_down, of_next, block=1024):
    total, hidden = g.shape
    rows, wide = total // trees, trees * RANK
    pair = 2 * HEAD_DIM
    once = lambda j: (0, 0)
    return pl.pallas_call(
        functools.partial(mlp_down_kernel, trees),
        grid=(hidden // block,),
        in_specs=[
            pl.BlockSpec((total, block), lambda j: (0, j)),
            pl.BlockSpec((total, D), once, pipeline_mode=pl.Buffered(1)),
            pl.BlockSpec((block, D), lambda j: (j, 0)),
            pl.BlockSpec((wide, block), lambda j: (0, j)),
            pl.BlockSpec((wide, D), once),
            pl.BlockSpec((2, D), once),
            pl.BlockSpec((wide, D), once),
            pl.BlockSpec((wide, pair), once),
            pl.BlockSpec((D, pair), once),
        ],
        out_specs=[pl.BlockSpec((rows, D), once)] * trees + [pl.BlockSpec((total, pair), once)],
        out_shape=[jax.ShapeDtypeStruct((rows, D), BF)] * trees
        + [jax.ShapeDtypeStruct((total, pair), BF)],
        scratch_shapes=[pltpu.VMEM((total, D), F32), pltpu.VMEM((wide, total), F32)],
        compiler_params=params(),
        cost_estimate=pl.CostEstimate(
            flops=2 * total * D * hidden,
            transcendentals=0,
            bytes_accessed=2 * D * hidden + 2 * total * hidden,
        ),
        name="mlp_down",
    )(g, x2, w_down, down_down, up_down, *of_next)


def by_tree(u_ref, u, rows):
    for m in range(u_ref.shape[0]):
        u_ref[m] = u[m * rows : (m + 1) * rows, m * RANK : (m + 1) * RANK]


def forward_kernel(trees, first, *refs):
    (o_ref, x_ref, norm_ref, dno_ref, upo_ref, wo_ref, wu_ref, wd_ref, upu_ref, dnd_ref, dnu_ref,
     upd_ref, y_ref, x2_ref, b_ref, g_ref, gp_ref, u2_ref, u3_ref, u4_ref,
     sum_ref, acc_ref, mixed_ref, inner_ref) = refs
    step = pl.program_id(0)
    rows = o_ref.shape[0] // trees

    @pl.when(step < first)
    def _():
        mix(step, rows, o_ref, x_ref, dno_ref, upo_ref, wo_ref, mixed_ref, sum_ref)

    @pl.when(step == first - 1)
    def _():
        by_tree(u2_ref, mixed_ref[...], rows)
        x2_ref[...] = sum_ref[...].astype(BF)
        b = normed(sum_ref, norm_ref)
        b_ref[...] = b
        inner = masked(dot(b, dnu_ref[...], NT), rows)
        inner_ref[...] = inner
        by_tree(u3_ref, inner, rows)
        acc_ref[...] = jnp.zeros_like(acc_ref)

    @pl.when(step >= first)
    def _():
        f = dot(b_ref[...], wu_ref[0]) + dot(inner_ref[...], upu_ref[...])
        square, half = gelu_parts(f)
        g = (f * half).astype(BF)
        g_ref[...] = g
        slope = f * ((2 * GELU_C) + (6 * GELU_C * 0.044715) * square)
        gp_ref[...] = (half + (half * (1.0 - half)) * slope).astype(BF)
        sum_ref[...] += dot(g, wd_ref[...])
        acc_ref[...] += dot(dnd_ref[...], g, NT)

    @pl.when(step == pl.num_programs(0) - 1)
    def _():
        u4 = masked(acc_ref[...].T, rows)
        by_tree(u4_ref, u4, rows)
        y_ref[...] = (sum_ref[...] + dot(u4, upd_ref[...])).astype(BF)


def forward_rest(trees, o, x, norm, held, part, w_down, maps, block=512):
    _, _, dn_out, up_out, dn_up, up_up, dn_down, up_down = maps
    total, wide = o.shape[0], trees * RANK
    rows = total // trees
    shards = held.shape[0]
    hidden = shards * part
    block = min(block, part)
    per = part // block
    at = part // (D // shards)
    once = lambda i: (0, 0)
    early = lambda i: jnp.minimum(i, shards - 1)
    late = lambda i: jnp.maximum(i - shards, 0)
    single = pl.Buffered(1)
    full = pl.BlockSpec((total, D), once)
    ranks = pl.BlockSpec((trees, rows, RANK), lambda i: (0, 0, 0))
    return pl.pallas_call(
        functools.partial(forward_kernel, trees, shards),
        grid=(shards + hidden // block,),
        in_specs=[pl.BlockSpec((total, D), once, pipeline_mode=single)] * 2
        + [
            pl.BlockSpec((2, D), once),
            pl.BlockSpec((wide, D), once),
            pl.BlockSpec((wide, D // shards), lambda i: (0, early(i))),
            pl.BlockSpec((1, D, D // shards), lambda i: (early(i), 0, at)),
            pl.BlockSpec((1, D, block), lambda i: (late(i) // per, 0, late(i) % per)),
            pl.BlockSpec((block, D), lambda i: (late(i), 0)),
            pl.BlockSpec((wide, block), lambda i: (0, late(i))),
            pl.BlockSpec((wide, block), lambda i: (0, late(i))),
            pl.BlockSpec((wide, D), once),
            pl.BlockSpec((wide, D), once),
        ],
        out_specs=[
            full,
            full,
            full,
            pl.BlockSpec((total, block), lambda i: (0, late(i))),
            pl.BlockSpec((total, block), lambda i: (0, late(i))),
            ranks,
            ranks,
            ranks,
        ],
        out_shape=[jax.ShapeDtypeStruct((total, D), BF)] * 3
        + [jax.ShapeDtypeStruct((total, hidden), BF)] * 2
        + [jax.ShapeDtypeStruct((trees, rows, RANK), BF)] * 3,
        scratch_shapes=[
            pltpu.VMEM((total, D), F32),
            pltpu.VMEM((wide, total), F32),
            pltpu.VMEM((total, wide), BF),
            pltpu.VMEM((total, wide), BF),
        ],
        compiler_params=params(),
        cost_estimate=pl.CostEstimate(
            flops=4 * total * D * hidden + 2 * total * D * D,
            transcendentals=total * hidden,
            bytes_accessed=4 * D * hidden + 4 * total * hidden + 2 * D * D,
        ),
        name="forward_rest",
    )(o, x, norm, dn_out, up_out, held, held, w_down, up_up, dn_down, dn_up, up_down)


def backward_kernel(given, first, *refs):
    flag_ref, own_ref, *refs = refs
    if given == 2:
        arrived_ref, *refs = refs
    (b_ref, x2_ref, gain_ref, wu_ref, wd_ref, g_ref, gp_ref, u3_ref, u4_ref, upu_ref, dnd_ref,
     dnu_ref, upd_ref, o_ref, u2_ref, dno_ref, upo_ref, wo_ref,
     dr_ref, do_ref, slab_ref,
     dy_ref, sum_ref, du4_ref, du3_ref, du2_ref) = refs
    shards = slab_ref.shape[0]
    small = D // shards
    large = (slab_ref.shape[2] - 4 * small) // 2
    at = [0, small, 2 * small, 3 * small, 3 * small + large, 3 * small + 2 * large]

    def put(which, grad):
        for z in range(shards):
            part = grad[:, z * small : (z + 1) * small].astype(BF)
            slab_ref[z, :, at[which] : at[which] + small] = part

    def put_block(which, index, grad):
        block = grad.shape[1]
        per = large // block
        cols = pl.ds(pl.multiple_of(at[which] + lax.rem(index, per) * block, 128), block)
        slab_ref[index // per, :, cols] = grad.astype(BF)

    step = pl.program_id(0)

    @pl.when(step == 0)
    def _():
        dy = own_ref[...]
        if given == 2:
            dy = jnp.where(flag_ref[0] == 1, dy, arrived_ref[...])
        dy_ref[...] = dy
        du4_ref[...] = (2.0 * dot(dy, upd_ref[...], NT)).astype(BF)
        put(5, dot(u4_ref[0], dy, TN))
        sum_ref[...] = jnp.zeros_like(sum_ref)
        du3_ref[...] = jnp.zeros_like(du3_ref)

    @pl.when(step < first)
    def _():
        du4 = du4_ref[...]
        dg = dot(dy_ref[...], wd_ref[...], NT) + dot(du4, dnd_ref[...])
        df = (gp_ref[...].astype(F32) * dg).astype(BF)
        put_block(4, step, dot(du4, g_ref[...], TN))
        put_block(3, step, dot(u3_ref[0], df, TN))
        du3_ref[...] += dot(upu_ref[...], df, NT)
        sum_ref[...] += dot(df, wu_ref[0], NT)

    @pl.when(step == first - 1)
    def _():
        du3 = (2.0 * du3_ref[...].T).astype(BF)
        put(2, dot(du3, b_ref[...], TN))
        db = (sum_ref[...] + dot(du3, dnu_ref[...])).astype(BF).astype(F32)
        back = layer_norm_back(x2_ref[...].astype(F32), gain_ref[...], db)
        dr = (dy_ref[...].astype(F32) + back).astype(BF)
        dr_ref[...] = dr
        du2_ref[...] = (2.0 * dot(dr, upo_ref[...], NT)).astype(BF)
        put(1, dot(u2_ref[0], dr, TN))

    @pl.when(step >= first)
    def _():
        wide = wo_ref.shape[2]
        du2 = du2_ref[...]
        do = dot(du2, dno_ref[...])
        for z in range(wo_ref.shape[0]):
            do = do + dot(dr_ref[:, z * wide : (z + 1) * wide], wo_ref[z], NT)
        do_ref[...] = do.astype(BF)
        grad = dot(du2, o_ref[...], TN).astype(BF)
        deep = grad.shape[1]
        for z in range(deep // small):
            slab_ref[(step - first) * (deep // small) + z, :, :small] = grad[:, z * small : (z + 1) * small]


def backward_rest(
    which, own, b, x2, gain, held, part, w_down, g, gp, u2, u3, u4, o, maps, arrived=None,
    block=1024,
):
    _, _, dn_out, up_out, dn_up, up_up, dn_down, up_down = maps
    rows = u2.shape[1]
    shards = held.shape[0]
    hidden = shards * part
    block = min(block, part)
    per = part // block
    at = part // (D // shards)
    first = hidden // block
    deep = 512
    once = lambda i, w: (0, 0)
    mine = lambda i, w: (w[1], 0)
    early = lambda i: jnp.minimum(i, first - 1)
    late = lambda i: jnp.maximum(i - first, 0)
    single = pl.Buffered(1)
    row = pl.BlockSpec((rows, D), mine, pipeline_mode=single)
    given = 1 if arrived is None else 2
    hid = pl.BlockSpec((rows, block), lambda i, w: (w[1], early(i)))
    thin = pl.BlockSpec((RANK, block), lambda i, w: (w[1], early(i)))
    ranks = pl.BlockSpec((1, rows, RANK), lambda i, w: (w[1], 0, 0))
    across = pl.BlockSpec((RANK, D), mine)
    shape = jax.ShapeDtypeStruct
    columns = 4 * (D // shards) + 2 * part
    return pl.pallas_call(
        functools.partial(backward_kernel, given, first),
        grid_spec=pltpu.PrefetchScalarGridSpec(
            num_scalar_prefetch=1,
            grid=(first + D // deep,),
            in_specs=[row]
            + [pl.BlockSpec((rows, D), once, pipeline_mode=single)] * (given - 1)
            + [
                row,
                row,
                pl.BlockSpec((1, D), once),
                pl.BlockSpec((1, D, block), lambda i, w: (early(i) // per, 0, early(i) % per)),
                pl.BlockSpec((block, D), lambda i, w: (early(i), 0)),
                hid,
                hid,
                ranks,
                ranks,
                thin,
                thin,
                across,
                across,
                pl.BlockSpec((rows, deep), lambda i, w: (w[1], late(i))),
                ranks,
                pl.BlockSpec((RANK, deep), lambda i, w: (w[1], late(i))),
                across,
                pl.BlockSpec((shards, deep, D // shards), lambda i, w: (0, late(i), at)),
            ],
            out_specs=[
                pl.BlockSpec((rows, D), once),
                pl.BlockSpec((rows, deep), lambda i, w: (0, late(i))),
                pl.BlockSpec((shards, RANK, columns), lambda i, w: (0, 0, 0)),
            ],
            scratch_shapes=[
                pltpu.VMEM((rows, D), BF),
                pltpu.VMEM((rows, D), F32),
                pltpu.VMEM((rows, RANK), BF),
                pltpu.VMEM((RANK, rows), F32),
                pltpu.VMEM((rows, RANK), BF),
            ],
        ),
        out_shape=[shape((rows, D), BF)] * 2 + [shape((shards, RANK, columns), BF)],
        compiler_params=params(),
        cost_estimate=pl.CostEstimate(
            flops=4 * rows * D * hidden + 2 * rows * D * D,
            transcendentals=0,
            bytes_accessed=4 * D * hidden + 4 * rows * hidden + 2 * D * D,
        ),
        name="backward_rest",
    )(
        which, own, *([] if arrived is None else [arrived]),
        b, x2, gain, held, w_down, g, gp, u3, u4, up_up, dn_down, dn_up, up_down,
        o, u2, dn_out, up_out, held,
    )


def place_kernel(parts, ids_ref, *refs):
    slab_refs, grad_refs = refs[: -len(parts)], refs[-len(parts) :]
    for ref in grad_refs:
        ref[...] = jnp.zeros_like(ref)
    for m, slab_ref in enumerate(slab_refs):
        for r in range(slab_ref.shape[0]):
            name = ids_ref[r * len(slab_refs) + m]
            for ref, (at, width) in zip(grad_refs, parts):
                ref[name] += slab_ref[r, :, at : at + width].astype(F32)


def place(ids, slabs, parts, adapters):
    every = lambda i, ids: (0, 0, 0)
    return pl.pallas_call(
        functools.partial(place_kernel, parts),
        grid_spec=pltpu.PrefetchScalarGridSpec(
            num_scalar_prefetch=1,
            grid=(1,),
            in_specs=[pl.BlockSpec(slab.shape, every) for slab in slabs],
            out_specs=[pl.BlockSpec((adapters, RANK, width), every) for _, width in parts],
        ),
        out_shape=[jax.ShapeDtypeStruct((adapters, RANK, width), F32) for _, width in parts],
        compiler_params=params(),
        cost_estimate=pl.CostEstimate(
            flops=0, transcendentals=0, bytes_accessed=6 * slabs[0].size * len(slabs)
        ),
        name="place",
    )(ids, *slabs)


def segment_of(places, lengths):
    order = jnp.arange(lengths.shape[0], dtype=jnp.int32)
    ends = jnp.sum(
        jnp.where(order[None, :] <= order[:, None], lengths[None, :], 0), axis=1, dtype=jnp.int32
    )
    return jnp.sum((places[:, None] >= ends[None, :]).astype(jnp.int32), axis=1, dtype=jnp.int32)


def ancestry(parents):
    seg_ids = jnp.arange(parents.shape[0], dtype=jnp.int32)
    current = seg_ids
    reach = current[:, None] == seg_ids[None, :]
    for sweep in range(parents.shape[0] - 1):
        current = jnp.sum(
            jnp.where(current[:, None] == seg_ids[None, :], parents[None, :], 0),
            axis=1,
            dtype=jnp.int32,
        )
        reach = reach | (current[:, None] == seg_ids[None, :])
    return reach.astype(BF)


def key_bias(lengths, parents, query_places, key_places):
    seg_ids = jnp.arange(parents.shape[0], dtype=jnp.int32)
    of_query = (segment_of(query_places, lengths)[:, None] == seg_ids[None, :]).astype(BF)
    of_key = (segment_of(key_places, lengths)[:, None] == seg_ids[None, :]).astype(BF)
    known = ancestry(parents)

    def bias(rows_in, rows_out, place_query, place_key):
        reach = dot(rows_in, rows_out, NT)
        allowed = (reach > 0.5) & (place_key <= place_query) & (place_key >= 0)
        return jnp.where(allowed, 0.0, MASKED).astype(F32)

    anc = dot(of_query, known).astype(BF)
    return (
        bias(anc, of_key, query_places[:, None], key_places[None, :]),
        bias(of_key, anc, query_places[None, :], key_places[:, None]),
    )


def shifted(value, axis, steps):
    count = lax.axis_size(axis)
    return lax.ppermute(value, axis, [(i, (i + steps) % count) for i in range(count)])


def local(
    inputs, cotangent, norm_gains, norm_biases, w_attn, w_out, w_up, w_down,
    down_attn, up_attn, down_out, up_out, down_up, up_up, down_down, up_down,
    seg_lengths, parent_ids, adapter_ids,
):
    section = lax.axis_index("section")
    shard = lax.axis_index("fsdp")
    member = lax.axis_index("replica")
    shards = lax.axis_size("fsdp")
    members = lax.axis_size("replica")
    trees, per_tree = inputs.shape[0], inputs.shape[1]
    gain = norm_gains[0].astype(F32)
    shift = norm_biases[0].astype(F32)
    norms = [jnp.stack([gain[i], shift[i]]) for i in range(2)]
    is_first = (section == 0).astype(jnp.int32).reshape(1)

    def quarter(weight):
        part = weight.shape[0] // members
        return lax.dynamic_slice_in_dim(weight, member * part, part, 0)

    def gathered(own):
        return lax.all_gather(own[None], ("fsdp", "replica"), axis=1, tiled=True)[0]

    part, out_wide, attn_wide = w_up.shape[2], w_out.shape[2], w_attn.shape[2]
    padded = -(-attn_wide // 128) * 128
    attn_at = -(-(part + out_wide) // padded) * padded
    each = D // members
    own = pack(member, each, w_up[0], w_out[0], w_attn[0].T, attn_at, attn_at + padded)
    held = gathered(own).reshape(shards, D, own.shape[1])
    down_full = gathered(quarter(w_down[0]))
    attn_full = assemble(held, attn_at, attn_wide)

    stacks = (down_attn, up_attn, down_out, up_out, down_up, up_up, down_down, up_down)
    widths = [stack.shape[3] for stack in stacks]
    starts = [sum(widths[:i]) for i in range(len(widths))]
    chosen = adapter_ids[:, 0, 0]
    picked = jnp.concatenate(
        [
            jnp.concatenate(
                [lax.dynamic_index_in_dim(stack[0], chosen[m], 0, keepdims=False) for m in range(trees)],
                axis=0,
            )
            for stack in stacks
        ],
        axis=1,
    )
    owners = lax.all_gather(chosen, "replica", axis=0, tiled=True)
    owners, picked = lax.optimization_barrier((owners, picked))
    ups, downs = [picked], [picked]
    for k in range(1, shards):
        ups.append(lax.ppermute(ups[-1], "fsdp", [(i, i + 1) for i in range(shards - 1)]))
        downs.append(lax.ppermute(downs[-1], "fsdp", [(i + 1, i) for i in range(shards - 1)]))
    behind = jnp.stack(
        [picked] + [jnp.where(shard >= k, ups[k], downs[shards - k]) for k in range(1, shards)]
    )
    ordered = [
        lax.dynamic_index_in_dim(behind, lax.rem(shard - z + shards, shards), 0, keepdims=False)
        for z in range(shards)
    ]
    maps = [
        jnp.concatenate([piece[:, at : at + width] for piece in ordered], axis=1)
        for at, width in zip(starts, widths)
    ]
    dn_attn, up_attn_, dn_out, up_out_, dn_up, up_up_, dn_down, up_down_ = maps

    query_places = shard * per_tree + jnp.arange(per_tree, dtype=jnp.int32)
    key_places = jnp.concatenate(
        [(shard - s) * per_tree + jnp.arange(per_tree, dtype=jnp.int32) for s in range(shards)]
    )
    biases = [
        key_bias(seg_lengths[m, 0], parent_ids[m, 0], query_places, key_places)
        for m in range(trees)
    ]

    def to_higher(value, steps):
        return lax.ppermute(value, "fsdp", [(i, i + steps) for i in range(shards - steps)])

    def to_lower(value, steps):
        return lax.ppermute(value, "fsdp", [(i + steps, i) for i in range(shards - steps)])

    def with_lower(kv):
        return [kv] + [to_higher(kv, s) for s in range(1, shards)]

    own_rows = inputs.reshape(trees * per_tree, D)
    entered = [
        entry(m, trees, own_rows, norms[0], dn_attn, up_attn_, attn_full) for m in range(trees)
    ]
    own_kv = jnp.concatenate([part[2] for part in entered], axis=0)
    blocks = with_lower(own_kv)
    attended = ()
    for m, (a, u1, _) in enumerate(entered):
        q = queries(m, a, u1, up_attn_, attn_full)
        attended = attention_forward(m, trees, q, blocks, biases[m][0], attended, False)
    x2, b = mixing(attended[0], own_rows, norms[1], dn_out, up_out_, held, part)
    g = mlp_up(b, held, part, up_up_, dn_up)
    of_last = [
        lax.ppermute(value, "section", [(1, 0)])
        for value in (norms[0], dn_attn, up_attn_[:, D:], attn_full[:, D:])
    ]
    bias = jnp.concatenate([pair[1] for pair in biases], axis=0)
    g, of_last, bias = lax.optimization_barrier((g, of_last, bias))
    *sent, sent_kv = mlp_down(trees, g, x2, down_full, dn_down, up_down_, of_last)
    arrived_kv = lax.ppermute(sent_kv, "section", [(0, 1)])
    sent, arrived_kv = lax.optimization_barrier((sent, arrived_kv))
    arrived = [lax.ppermute(rows, "section", [(0, 1)]) for rows in sent]
    blocks = with_lower(jnp.where(section == 0, own_kv, arrived_kv))
    entered, attended = (), ()
    for m in range(trees):
        rows = arrived[m]
        if m:
            rows, attended = lax.optimization_barrier((rows, attended))
        a, u1, *entered = enter(
            m, trees, own_rows, rows, is_first, norms[0], dn_attn, entered
        )
        q = queries(m, a, u1, up_attn_, attn_full)
        attended = attention_forward(m, trees, q, blocks, biases[m][0], attended, True)
    x, a, u1 = entered
    o, lse, q = attended
    layer_out, x2, b, g, gp, u2, u3, u4 = forward_rest(
        trees, o, x, norms[1], held, part, down_full, maps
    )
    def by_shard(grads, parts):
        return jnp.stack(
            [
                jnp.concatenate(
                    [g[:, z * part : (z + 1) * part] for g, part in zip(grads, parts)], axis=1
                )
                for z in range(shards)
            ]
        )

    def scattered(slabs):
        return lax.psum_scatter(slabs, "fsdp", scatter_dimension=0)

    def permuted(slabs):
        total = lax.dynamic_index_in_dim(slabs, shard, 0, keepdims=False).astype(F32)
        for k in range(1, shards):
            part = lax.dynamic_index_in_dim(slabs, lax.rem(shard + k, shards), 0, keepdims=False)
            total = total + shifted(part, "fsdp", k).astype(F32)
        return total.astype(BF)

    def all_replicas(total):
        return jnp.stack([total] + [shifted(total, "replica", i) for i in range(1, members)])

    own_grads = cotangent.reshape(trees * per_tree, D)
    order = lax.rem(member - jnp.arange(members, dtype=jnp.int32) + members, members)
    cyclic = owners.reshape(members, trees)[order].reshape(-1)
    in_grads, sums, arrived, before, total, ready = [], [], None, None, None, None
    for step in range(trees + 1):
        tree = jnp.clip(step - 1 + section, 0, trees - 1)
        which = jnp.stack([section, tree]).astype(jnp.int32)
        if arrived is None:
            which = jnp.array([1, 0], jnp.int32)
        total = None
        if ready is not None:
            arrived, ready = lax.optimization_barrier((arrived, ready))
            in_grads.append(ready[0])
            total = scattered(ready[1])
        dr, do, slab = backward_rest(
            which, own_grads, b, x2, gain[1:2], held, part, down_full, g, gp, u2, u3, u4,
            o, maps, arrived,
        )
        if total is not None:
            do, total = lax.optimization_barrier((do, total))
            total = all_replicas(total)
        early_sum = scattered(slab) if step == trees else None
        dq, dkv = attention_backward(which, q, do, o, blocks, bias, lse)
        dkv = [dkv[0]] + [to_lower(dkv[s], s) for s in range(1, shards)]
        if total is not None:
            dq, total = lax.optimization_barrier((dq, total))
            sums.append(total)
        da, du = query_leaving(which, dq, up_attn_, attn_full)
        if early_sum is not None:
            da, early_sum = lax.optimization_barrier((da, early_sum))
        dx, *late = leaving(
            which, dq, da, du, dkv, a, u1, x, dr, gain[0:1], dn_attn, up_attn_, attn_full
        )
        if step < trees:
            arrived = lax.ppermute(dx, "section", [(1, 0)])
        late = by_shard(late, widths[:2])
        now = (dx, slab, late)
        ready = None
        if 0 < step < trees:
            dx_ready, *grads = (
                jnp.where(section == 1, was, new) for was, new in zip(before, now)
            )
            ready = (dx_ready, jnp.concatenate(grads, axis=2))
        before = now
    in_grads.append(dx)
    sums.append(all_replicas(jnp.concatenate([early_sum, permuted(late)], axis=1)))
    order = [2, 3, 4, 5, 6, 7, 0, 1]
    parts = [(sum(widths[i] for i in order[:at]), widths[i]) for at, i in enumerate(order)]
    placed = place(cyclic, sums, parts, down_attn.shape[1])
    finals = [placed[order.index(i)][None] for i in range(len(stacks))]
    return (
        layer_out.reshape(1, trees, per_tree, D),
        jnp.stack(in_grads)[None],
        *finals,
    )


def solution(mesh):
    rows = P(None, ("replica", "fsdp"), None)
    stack = P("section", None, None, "fsdp")
    placed = (
        (rows, rows)
        + (P("section", None, None),) * 2
        + (P("section", None, "fsdp"),) * 3
        + (P("section", "fsdp", None),)
        + (stack,) * 8
        + (P(None, "replica", None),) * 3
    )
    return jax.shard_map(
        local,
        mesh=mesh,
        in_specs=placed,
        out_specs=(P("section", None, ("replica", "fsdp"), None),) * 2 + (stack,) * 8,
        check_vma=False,
    )
```

```python
import functools
import math

import jax
import jax.numpy as jnp
from jax import lax
from jax.experimental import pallas as pl
from jax.experimental.pallas import tpu as pltpu
from jax.sharding import PartitionSpec as P

D = 2048
HEADS = 16
HEAD_DIM = 128
RANK = 16

NORM_EPS = 1e-05
MASKED = -1e30
BF = jnp.bfloat16
F32 = jnp.float32
INV_ROOT = HEAD_DIM ** (-0.5)
LOG2E = math.log2(math.e)
LN2 = math.log(2.0)
GELU_C = math.sqrt(2.0 / math.pi)
VMEM_LIMIT = 52 * 1024 * 1024
SLICE = 512

NN = (((1,), (0,)), ((), ()))
NT = (((1,), (1,)), ((), ()))
TN = (((0,), (0,)), ((), ()))


def dot(left, right, dims=NN):
    return lax.dot_general(left, right, dims, preferred_element_type=F32)


def params(steps=1):
    return pltpu.CompilerParams(
        dimension_semantics=("arbitrary",) * steps, vmem_limit_bytes=VMEM_LIMIT
    )


def layer_norm(rows, gain, shift):
    centre = rows - jnp.mean(rows, axis=-1, keepdims=True)
    spread = jnp.mean(centre * centre, axis=-1, keepdims=True)
    return centre * lax.rsqrt(spread + NORM_EPS) * gain + shift


def layer_norm_back(rows, gain, grad):
    centre = rows - jnp.mean(rows, axis=-1, keepdims=True)
    spread = jnp.mean(centre * centre, axis=-1, keepdims=True)
    scale = lax.rsqrt(spread + NORM_EPS)
    unit = centre * scale
    inner = grad * gain
    return scale * (
        inner
        - jnp.mean(inner, axis=-1, keepdims=True)
        - unit * jnp.mean(inner * unit, axis=-1, keepdims=True)
    )


def tree_mask(rows, per_tree):
    row = lax.broadcasted_iota(jnp.int32, (rows, (rows // per_tree) * RANK), 0)
    col = lax.broadcasted_iota(jnp.int32, (rows, (rows // per_tree) * RANK), 1)
    return (row // per_tree) == (col // RANK)


def masked(value, per_tree):
    return jnp.where(tree_mask(value.shape[0], per_tree), 2.0 * value, 0.0).astype(BF)


def attend(heads, q_ref, kv_refs, bias_ref, o_ref, lse_ref):
    keys = jnp.concatenate([r[:, :HEAD_DIM] for r in kv_refs], axis=0)
    vals = jnp.concatenate([r[:, HEAD_DIM:] for r in kv_refs], axis=0)
    vals = jnp.concatenate([vals, jnp.ones_like(vals)], axis=1)
    for h in range(heads):
        cols = slice(h * HEAD_DIM, (h + 1) * HEAD_DIM)
        scores = dot(q_ref[:, cols], keys, NT) + bias_ref[...]
        top = jnp.max(scores, axis=1, keepdims=True)
        probs = jnp.exp2(scores - top)
        mixed = dot(probs.astype(BF), vals)
        total = mixed[:, HEAD_DIM:]
        o_ref[:, cols] = (mixed[:, :HEAD_DIM] / total).astype(BF)
        lse_ref[0, h : h + 1, :] = (top + jnp.log2(total)).T[0:1, :]


def attention_forward_kernel(blocks, heads, before, q_ref, *refs):
    kv_refs, (bias_ref, *refs) = refs[:blocks], refs[blocks:]
    attend(heads, q_ref, kv_refs, bias_ref, *refs[before:])


def attention_forward(tree, trees, q, kv, bias, before, heads=8):
    rows = q.shape[0]
    blocks = len(kv)
    wide = heads * HEAD_DIM
    steps = HEADS // heads
    return pl.pallas_call(
        functools.partial(attention_forward_kernel, blocks, heads, len(before)),
        grid=(steps,),
        in_specs=[pl.BlockSpec((rows, wide), lambda i: (0, i))]
        + [pl.BlockSpec((rows, 2 * HEAD_DIM), lambda i: (tree, 0))] * blocks
        + [pl.BlockSpec((rows, blocks * rows), lambda i: (0, 0))]
        + [pl.BlockSpec(memory_space=pl.ANY)] * len(before),
        out_specs=[
            pl.BlockSpec((rows, wide), lambda i: (tree, i)),
            pl.BlockSpec((1, heads, rows), lambda i: (tree * steps + i, 0, 0)),
        ],
        out_shape=[
            jax.ShapeDtypeStruct((trees * rows, D), BF),
            jax.ShapeDtypeStruct((trees * steps, heads, rows), F32),
        ],
        input_output_aliases={blocks + 2 + i: i for i in range(len(before))},
        compiler_params=params(),
        cost_estimate=pl.CostEstimate(
            flops=8 * rows * rows * blocks * D,
            transcendentals=rows * rows * blocks * HEADS,
            bytes_accessed=4 * rows * D + 4 * rows * rows * blocks,
        ),
        name="attention_forward",
    )(q, *kv, bias, *before)


def attention_backward_kernel(blocks, heads, _, q_ref, do_ref, o_ref, *refs):
    kv_refs = refs[:blocks]
    bias_ref, lse_ref, dq_ref, *dkv_refs, acc_ref = refs[blocks:]
    rows = q_ref.shape[0]
    step = pl.program_id(0)

    @pl.when(step == 0)
    def _():
        acc_ref[...] = jnp.zeros_like(acc_ref)

    keys = jnp.concatenate([r[:, :HEAD_DIM] for r in kv_refs], axis=0)
    vals = jnp.concatenate([r[:, HEAD_DIM:] for r in kv_refs], axis=0)
    keys_t = keys.T
    for h in range(heads):
        cols = slice(h * HEAD_DIM, (h + 1) * HEAD_DIM)
        q, do = q_ref[:, cols], do_ref[:, cols]
        delta = jnp.sum(
            (do.astype(F32) * o_ref[:, cols].astype(F32)).T, axis=0, keepdims=True
        )
        scores = dot(keys, q, NT) + bias_ref[...]
        probs = jnp.exp2(scores - lse_ref[0, h : h + 1, :])
        dprobs = dot(vals, do, NT)
        dscores = (probs * (dprobs - delta)).astype(BF)
        acc_ref[:, :HEAD_DIM] += dot(dscores, q)
        acc_ref[:, HEAD_DIM:] += dot(probs.astype(BF), do)
        dq_ref[:, cols] = (dot(keys_t, dscores) * INV_ROOT).T.astype(BF)

    @pl.when(step == pl.num_programs(0) - 1)
    def _():
        for s in range(blocks):
            part = slice(s * rows, (s + 1) * rows)
            dkv_refs[s][:, :HEAD_DIM] = (acc_ref[part, :HEAD_DIM] * LN2).astype(BF)
            dkv_refs[s][:, HEAD_DIM:] = acc_ref[part, HEAD_DIM:].astype(BF)


def attention_backward(which, q, do, o, kv, bias, lse):
    rows = do.shape[0]
    blocks = len(kv)
    trees = q.shape[0] // rows
    heads = lse.shape[1]
    steps = lse.shape[0] // trees
    wide = heads * HEAD_DIM
    mine = lambda i, w: (w[1], i)
    pair = pl.BlockSpec((rows, 2 * HEAD_DIM), lambda i, w: (0, 0))
    dq, *dkv = pl.pallas_call(
        functools.partial(attention_backward_kernel, blocks, heads),
        grid_spec=pltpu.PrefetchScalarGridSpec(
            num_scalar_prefetch=1,
            grid=(steps,),
            in_specs=[
                pl.BlockSpec((rows, wide), mine),
                pl.BlockSpec((rows, wide), lambda i, w: (0, i)),
                pl.BlockSpec((rows, wide), mine),
            ]
            + [pl.BlockSpec((rows, 2 * HEAD_DIM), lambda i, w: (w[1], 0))] * blocks
            + [
                pl.BlockSpec((blocks * rows, rows), lambda i, w: (w[1], 0)),
                pl.BlockSpec((1, heads, rows), lambda i, w: (w[1] * steps + i, 0, 0)),
            ],
            out_specs=[pl.BlockSpec((rows, wide), lambda i, w: (0, i))] + [pair] * blocks,
            scratch_shapes=[pltpu.VMEM((blocks * rows, 2 * HEAD_DIM), F32)],
        ),
        out_shape=[jax.ShapeDtypeStruct((rows, D), BF)]
        + [jax.ShapeDtypeStruct((rows, 2 * HEAD_DIM), BF)] * blocks,
        compiler_params=params(),
        cost_estimate=pl.CostEstimate(
            flops=20 * rows * rows * blocks * D,
            transcendentals=rows * rows * blocks * HEADS,
            bytes_accessed=8 * rows * D + 4 * rows * rows * blocks,
        ),
        name="attention_backward",
    )(which, q, do, o, *kv, bias, lse)
    return dq, dkv


def pack_kernel(at, _, up_ref, out_ref, attn_ref, all_ref):
    part, wide = up_ref.shape[1], attn_ref.shape[0]
    after = part + out_ref.shape[1]
    all_ref[:, :part] = up_ref[...]
    all_ref[:, part:after] = out_ref[...]
    if at > after:
        all_ref[:, after:at] = jnp.zeros((all_ref.shape[0], at - after), BF)
    attn = attn_ref[...].T
    spare = all_ref.shape[1] - at - wide
    if spare:
        attn = jnp.concatenate([attn, jnp.zeros((attn.shape[0], spare), BF)], axis=1)
    all_ref[:, at:] = attn


def pack(member, each, up, out, attn_t, at, total):
    return pl.pallas_call(
        functools.partial(pack_kernel, at),
        grid_spec=pltpu.PrefetchScalarGridSpec(
            num_scalar_prefetch=1,
            grid=(1,),
            in_specs=[
                pl.BlockSpec((each, up.shape[1]), lambda i, w: (w[0], 0)),
                pl.BlockSpec((each, out.shape[1]), lambda i, w: (w[0], 0)),
                pl.BlockSpec((attn_t.shape[0], each), lambda i, w: (0, w[0])),
            ],
            out_specs=pl.BlockSpec((each, total), lambda i, w: (0, 0)),
        ),
        out_shape=jax.ShapeDtypeStruct((each, total), BF),
        compiler_params=params(),
        cost_estimate=pl.CostEstimate(
            flops=0, transcendentals=0, bytes_accessed=4 * each * total
        ),
        name="pack",
    )(member.astype(jnp.int32).reshape(1), up, out, attn_t)


def assemble_kernel(wide, held_ref, full_ref):
    full_ref[...] = jnp.concatenate(
        [held_ref[z][:, :wide] for z in range(held_ref.shape[0])], axis=1
    )


def assemble(held, start, wide, block=256):
    shards, depth, _ = held.shape
    padded = -(-wide // 128) * 128
    return pl.pallas_call(
        functools.partial(assemble_kernel, wide),
        grid=(depth // block,),
        in_specs=[pl.BlockSpec((shards, block, padded), lambda i: (0, i, start // padded))],
        out_specs=pl.BlockSpec((block, shards * wide), lambda i: (i, 0)),
        out_shape=jax.ShapeDtypeStruct((depth, shards * wide), BF),
        compiler_params=params(),
        cost_estimate=pl.CostEstimate(
            flops=0, transcendentals=0, bytes_accessed=4 * shards * depth * padded
        ),
        name="assemble",
    )(held)


def ranks_of(rows, norm_ref, dn_ref):
    a = layer_norm(rows.astype(F32), norm_ref[0:1, :], norm_ref[1:2, :]).astype(BF)
    return a, dot(a, dn_ref[...], NT)


def entry_kernel(x_ref, norm_ref, dn_ref, up_ref, w_ref, a_ref, u_ref, kv_ref):
    a, u = ranks_of(x_ref[...], norm_ref, dn_ref)
    a_ref[...] = a
    u = (2.0 * u).astype(BF)
    u_ref[...] = u
    kv_ref[...] = (dot(a, w_ref[...]) + dot(u, up_ref[...])).astype(BF)


def entry(tree, trees, x, norm, dn, up, w):
    rows = x.shape[0] // trees
    wide = 2 * HEAD_DIM
    last = D // wide
    whole = lambda i: (0, 0)
    return pl.pallas_call(
        entry_kernel,
        grid=(1,),
        in_specs=[
            pl.BlockSpec((rows, D), lambda i: (tree, 0)),
            pl.BlockSpec((2, D), whole),
            pl.BlockSpec((RANK, D), lambda i: (tree, 0)),
            pl.BlockSpec((RANK, wide), lambda i: (tree, last)),
            pl.BlockSpec((D, wide), lambda i: (0, last)),
        ],
        out_specs=[
            pl.BlockSpec((rows, D), whole),
            pl.BlockSpec((rows, RANK), whole),
            pl.BlockSpec((rows, wide), whole),
        ],
        out_shape=[
            jax.ShapeDtypeStruct((rows, D), BF),
            jax.ShapeDtypeStruct((rows, RANK), BF),
            jax.ShapeDtypeStruct((rows, wide), BF),
        ],
        compiler_params=params(),
        cost_estimate=pl.CostEstimate(
            flops=3 * rows * D * wide, transcendentals=0, bytes_accessed=8 * rows * D
        ),
        name="entry",
    )(x, norm, dn, up, w)


def enter_kernel(
    blocks, heads, before, flag_ref, own_ref, arrived_ref, norm_ref, dn_ref, up_ref, w_ref, *refs
):
    kv_refs, (bias_ref, *refs) = refs[:blocks], refs[blocks:]
    o_ref, lse_ref, q_ref, x_all, a_ref, u_ref = refs[before:]

    @pl.when(pl.program_id(0) == 0)
    def _():
        x = jnp.where(flag_ref[0] == 1, own_ref[...], arrived_ref[...])
        x_all[...] = x
        a, u = ranks_of(x, norm_ref, dn_ref)
        a_ref[...] = a
        u_ref[0] = (2.0 * u).astype(BF)

    q = dot(a_ref[...], w_ref[...]) + dot(u_ref[0], up_ref[...])
    q_ref[...] = (q * (INV_ROOT * LOG2E)).astype(BF)
    attend(heads, q_ref, kv_refs, bias_ref, o_ref, lse_ref)


def enter(tree, trees, own, arrived, flag, norm, dn, up, w, kv, bias, before, heads=8):
    rows = own.shape[0] // trees
    blocks = len(kv)
    wide = heads * HEAD_DIM
    steps = HEADS // heads
    whole = lambda i, f: (0, 0)
    mine = pl.BlockSpec((rows, D), lambda i, f: (tree, 0))
    part = pl.BlockSpec((rows, wide), lambda i, f: (tree, i))
    tall = jax.ShapeDtypeStruct((trees * rows, D), BF)
    return pl.pallas_call(
        functools.partial(enter_kernel, blocks, heads, len(before)),
        grid_spec=pltpu.PrefetchScalarGridSpec(
            num_scalar_prefetch=1,
            grid=(steps,),
            in_specs=[
                mine,
                pl.BlockSpec((rows, D), whole),
                pl.BlockSpec((2, D), whole),
                pl.BlockSpec((RANK, D), lambda i, f: (tree, 0)),
                pl.BlockSpec((RANK, wide), lambda i, f: (tree, i)),
                pl.BlockSpec((D, wide), lambda i, f: (0, i)),
            ]
            + [pl.BlockSpec((rows, 2 * HEAD_DIM), lambda i, f: (tree, 0))] * blocks
            + [pl.BlockSpec((rows, blocks * rows), whole)]
            + [pl.BlockSpec(memory_space=pl.ANY)] * len(before),
            out_specs=[
                part,
                pl.BlockSpec((1, heads, rows), lambda i, f: (tree * steps + i, 0, 0)),
                part,
                mine,
                mine,
                pl.BlockSpec((1, rows, RANK), lambda i, f: (tree, 0, 0)),
            ],
        ),
        out_shape=[
            tall,
            jax.ShapeDtypeStruct((trees * steps, heads, rows), F32),
            tall,
            tall,
            tall,
            jax.ShapeDtypeStruct((trees, rows, RANK), BF),
        ],
        input_output_aliases={8 + blocks + i: i for i in range(len(before))},
        compiler_params=params(),
        cost_estimate=pl.CostEstimate(
            flops=2 * rows * D * D + 8 * rows * rows * blocks * D,
            transcendentals=rows * rows * blocks * HEADS,
            bytes_accessed=2 * D * D + 16 * rows * D + 4 * rows * rows * blocks,
        ),
        name="enter",
    )(flag, own, arrived, norm, dn, up, w, *kv, bias, *before)


def queries_kernel(a_ref, u_ref, up_ref, w_ref, q_ref):
    q = dot(a_ref[...], w_ref[...]) + dot(u_ref[...], up_ref[...])
    q_ref[...] = (q * (INV_ROOT * LOG2E)).astype(BF)


def queries(tree, a, u, up, w, block=1024):
    rows = a.shape[0]
    return pl.pallas_call(
        queries_kernel,
        grid=(D // block,),
        in_specs=[
            pl.BlockSpec((rows, D), lambda i: (0, 0)),
            pl.BlockSpec((rows, RANK), lambda i: (0, 0)),
            pl.BlockSpec((RANK, block), lambda i: (tree, i)),
            pl.BlockSpec((D, block), lambda i: (0, i)),
        ],
        out_specs=pl.BlockSpec((rows, block), lambda i: (0, i)),
        out_shape=jax.ShapeDtypeStruct((rows, D), BF),
        compiler_params=params(),
        cost_estimate=pl.CostEstimate(
            flops=2 * rows * D * D, transcendentals=0, bytes_accessed=2 * D * D
        ),
        name="queries",
    )(a, u, up, w)


def mix(step, rows, o_ref, x_ref, dn_ref, up_ref, w_ref, u_ref, sum_ref):
    @pl.when(step == 0)
    def _():
        sum_ref[...] = x_ref[...].astype(F32)
        u_ref[...] = masked(dot(o_ref[...], dn_ref[...], NT), rows)

    block = w_ref.shape[2]
    cols = pl.ds(pl.multiple_of(step * block, block), block)
    sum_ref[:, cols] += dot(o_ref[...], w_ref[0]) + dot(u_ref[...], up_ref[...])


def normed(sum_ref, norm_ref):
    return layer_norm(sum_ref[...], norm_ref[0:1, :], norm_ref[1:2, :]).astype(BF)


def mixing_kernel(rows, o_ref, x_ref, norm_ref, dn_ref, up_ref, w_ref, x2_ref, b_ref, u_ref):
    step = pl.program_id(0)
    mix(step, rows, o_ref, x_ref, dn_ref, up_ref, w_ref, u_ref, x2_ref)

    @pl.when(step == pl.num_programs(0) - 1)
    def _():
        b_ref[...] = normed(x2_ref, norm_ref)


def mixing(o, x, norm, dn, up, held, part):
    total, wide = o.shape[0], dn.shape[0]
    shards = held.shape[0]
    block = D // shards
    at = part // block
    whole = lambda i: (0, 0)
    single = pl.Buffered(1)
    return pl.pallas_call(
        functools.partial(mixing_kernel, total * RANK // wide),
        grid=(shards,),
        in_specs=[pl.BlockSpec((total, D), whole, pipeline_mode=single)] * 2
        + [
            pl.BlockSpec((2, D), whole),
            pl.BlockSpec((wide, D), whole),
            pl.BlockSpec((wide, block), lambda i: (0, i)),
            pl.BlockSpec((1, D, block), lambda i: (i, 0, at)),
        ],
        out_specs=[pl.BlockSpec((total, D), whole), pl.BlockSpec((total, D), whole)],
        out_shape=[
            jax.ShapeDtypeStruct((total, D), F32),
            jax.ShapeDtypeStruct((total, D), BF),
        ],
        scratch_shapes=[pltpu.VMEM((total, wide), BF)],
        compiler_params=params(),
        cost_estimate=pl.CostEstimate(
            flops=2 * total * D * D, transcendentals=0, bytes_accessed=2 * D * D + 10 * total * D
        ),
        name="mixing",
    )(o, x, norm, dn, up, held)


def query_leaving_kernel(_, dq_ref, up_ref, w_ref, da_ref, du_ref):
    @pl.when(pl.program_id(0) == 0)
    def _():
        du_ref[...] = dot(dq_ref[...], up_ref[...], NT)

    da_ref[...] = dot(dq_ref[...], w_ref[...], NT)


def query_leaving(which, dq, up, w, block=1024):
    rows = dq.shape[0]
    whole = lambda i, w: (0, 0)
    return pl.pallas_call(
        query_leaving_kernel,
        grid_spec=pltpu.PrefetchScalarGridSpec(
            num_scalar_prefetch=1,
            grid=(D // block,),
            in_specs=[
                pl.BlockSpec((rows, D), whole),
                pl.BlockSpec((RANK, D), lambda i, w: (w[1], 0)),
                pl.BlockSpec((block, D), lambda i, w: (i, 0)),
            ],
            out_specs=[
                pl.BlockSpec((rows, block), lambda i, w: (0, i)),
                pl.BlockSpec((rows, RANK), whole),
            ],
        ),
        out_shape=[
            jax.ShapeDtypeStruct((rows, D), F32),
            jax.ShapeDtypeStruct((rows, RANK), F32),
        ],
        compiler_params=params(),
        cost_estimate=pl.CostEstimate(
            flops=2 * rows * D * D, transcendentals=0, bytes_accessed=2 * D * D
        ),
        name="query_leaving",
    )(which, dq, up, w)


def leaving_kernel(blocks, shards, _, dq_ref, da_ref, du_ref, *refs):
    dkv_refs = refs[:blocks]
    (a_ref, u_ref, x_ref, dr_ref, gain_ref, dn_ref, up_ref, w_ref,
     dx_ref, slab_ref, gdn_ref, gup_ref) = refs[blocks:]
    step = pl.program_id(0)

    @pl.when(step == 0)
    def _():
        gdn_ref[...] = jnp.zeros_like(gdn_ref)
        gup_ref[...] = jnp.zeros_like(gup_ref)

    total = dkv_refs[0][...].astype(F32)
    for ref in dkv_refs[1:]:
        total = total + ref[...].astype(F32)
    dkv = total.astype(BF)
    du = (2.0 * (du_ref[...] + dot(dkv, up_ref[...], NT))).astype(BF)
    gup_ref[:, :D] += dot(u_ref[0], dq_ref[...], TN)
    gup_ref[:, D:] += dot(u_ref[0], dkv, TN)
    gdn_ref[...] += dot(du, a_ref[...], TN)
    da = da_ref[...] + dot(dkv, w_ref[...], NT) + dot(du, dn_ref[...])
    back = layer_norm_back(
        x_ref[...].astype(F32), gain_ref[0:1, :], da.astype(BF).astype(F32)
    )
    dx_ref[...] = (dr_ref[...].astype(F32) + back).astype(BF)

    @pl.when(step == pl.num_programs(0) - 1)
    def _():
        small, large = D // shards, gup_ref.shape[1] // shards
        for z in range(shards):
            slab_ref[z] = jnp.concatenate(
                [
                    gdn_ref[:, z * small : (z + 1) * small],
                    gup_ref[...][:, z * large : (z + 1) * large],
                ],
                axis=1,
            ).astype(BF)


def leaving(which, dq, da, du, dkv, a, u, x, dr, gain, dn, up, w, shards, steps=2):
    rows = da.shape[0] // steps
    wide = 2 * HEAD_DIM
    last = D // wide
    columns = (D + D + wide) // shards
    whole = lambda i, w: (0, 0)
    here = pl.BlockSpec((rows, D), lambda i, w: (i, 0))
    mine = pl.BlockSpec((rows, D), lambda i, w: (w[1] * steps + i, 0))
    return pl.pallas_call(
        functools.partial(leaving_kernel, len(dkv), shards),
        grid_spec=pltpu.PrefetchScalarGridSpec(
            num_scalar_prefetch=1,
            grid=(steps,),
            in_specs=[here, here, pl.BlockSpec((rows, RANK), lambda i, w: (i, 0))]
            + [pl.BlockSpec((rows, wide), lambda i, w: (i, 0))] * len(dkv)
            + [
                mine,
                pl.BlockSpec((1, rows, RANK), lambda i, w: (w[1], i, 0)),
                mine,
                here,
                pl.BlockSpec((2, D), whole),
                pl.BlockSpec((RANK, D), lambda i, w: (w[1], 0)),
                pl.BlockSpec((RANK, wide), lambda i, w: (w[1], last)),
                pl.BlockSpec((D, wide), lambda i, w: (0, last)),
            ],
            out_specs=[here, pl.BlockSpec((shards, RANK, columns), lambda i, w: (0, 0, 0))],
            scratch_shapes=[pltpu.VMEM((RANK, D), F32), pltpu.VMEM((RANK, D + wide), F32)],
        ),
        out_shape=[
            jax.ShapeDtypeStruct(da.shape, BF),
            jax.ShapeDtypeStruct((shards, RANK, columns), BF),
        ],
        compiler_params=params(),
        cost_estimate=pl.CostEstimate(
            flops=8 * rows * D * wide, transcendentals=0, bytes_accessed=28 * rows * D
        ),
        name="leaving",
    )(which, dq, da, du, *dkv, a, u, x, dr, gain, dn, up, w)


def joined(ref):
    return jnp.concatenate([ref[i] for i in range(ref.shape[0])], axis=1)


def sliced(ref, value):
    for i in range(ref.shape[0]):
        ref[i] = value[:, i * SLICE : (i + 1) * SLICE]


def gelu_parts(f):
    square = f * f
    half = 0.5 + 0.5 * jnp.tanh(f * (GELU_C + (GELU_C * 0.044715) * square))
    return square, half


def mlp_up_kernel(per_tree, b_ref, wu_ref, upu_ref, dnu_ref, g_ref, u3_ref):
    @pl.when(pl.program_id(0) == 0)
    def _():
        u3_ref[...] = masked(dot(b_ref[...], dnu_ref[...], NT), per_tree)

    f = dot(b_ref[...], wu_ref[0]) + dot(u3_ref[...], upu_ref[...])
    sliced(g_ref, (f * gelu_parts(f)[1]).astype(BF))


def mlp_up(b, held, part, up_up, down_up, block=1024):
    rows = b.shape[0]
    shards = held.shape[0]
    hidden = shards * part
    wide = down_up.shape[0]
    block = min(block, part)
    per = part // block
    once = lambda j: (0, 0)
    return pl.pallas_call(
        functools.partial(mlp_up_kernel, rows * RANK // wide),
        grid=(hidden // block,),
        in_specs=[
            pl.BlockSpec((rows, D), once),
            pl.BlockSpec((1, D, block), lambda j: (j // per, 0, j % per)),
            pl.BlockSpec((wide, block), lambda j: (0, j)),
            pl.BlockSpec((wide, D), once),
        ],
        out_specs=pl.BlockSpec((block // SLICE, rows, SLICE), lambda j: (j, 0, 0)),
        out_shape=jax.ShapeDtypeStruct((hidden // SLICE, rows, SLICE), BF),
        scratch_shapes=[pltpu.VMEM((rows, wide), BF)],
        compiler_params=params(),
        cost_estimate=pl.CostEstimate(
            flops=2 * rows * D * hidden,
            transcendentals=rows * hidden,
            bytes_accessed=2 * D * hidden + 2 * rows * hidden,
        ),
        name="mlp_up",
    )(b, held, up_up, down_up)


def mlp_down_kernel(
    trees, g_ref, x2_ref, wd_ref, dnd_ref, upd_ref, norm_ref, dn_ref, up_ref, w_ref, *refs
):
    y_refs, (kv_ref, sum_ref, acc_ref) = refs[:trees], refs[trees:]
    step = pl.program_id(0)
    rows = g_ref.shape[1] // trees

    @pl.when(step == 0)
    def _():
        sum_ref[...] = x2_ref[...]
        acc_ref[...] = jnp.zeros_like(acc_ref)

    g = joined(g_ref)
    sum_ref[...] += dot(g, wd_ref[...])
    acc_ref[...] += dot(dnd_ref[...], g, NT)

    @pl.when(step == pl.num_programs(0) - 1)
    def _():
        u4 = masked(acc_ref[...].T, rows)
        y = (sum_ref[...] + dot(u4, upd_ref[...])).astype(BF)
        for m in range(trees):
            y_refs[m][...] = y[m * rows : (m + 1) * rows]
        a, u = ranks_of(y, norm_ref, dn_ref)
        kv_ref[...] = (dot(a, w_ref[...]) + dot(masked(u, rows), up_ref[...])).astype(BF)


def mlp_down(trees, g, x2, w_down, down_down, up_down, of_next, block=1024):
    total, hidden = g.shape[1], g.shape[0] * SLICE
    rows, wide = total // trees, trees * RANK
    pair = 2 * HEAD_DIM
    once = lambda j: (0, 0)
    return pl.pallas_call(
        functools.partial(mlp_down_kernel, trees),
        grid=(hidden // block,),
        in_specs=[
            pl.BlockSpec((block // SLICE, total, SLICE), lambda j: (j, 0, 0)),
            pl.BlockSpec((total, D), once, pipeline_mode=pl.Buffered(1)),
            pl.BlockSpec((block, D), lambda j: (j, 0)),
            pl.BlockSpec((wide, block), lambda j: (0, j)),
            pl.BlockSpec((wide, D), once),
            pl.BlockSpec((2, D), once),
            pl.BlockSpec((wide, D), once),
            pl.BlockSpec((wide, pair), once),
            pl.BlockSpec((D, pair), once),
        ],
        out_specs=[pl.BlockSpec((rows, D), once)] * trees + [pl.BlockSpec((total, pair), once)],
        out_shape=[jax.ShapeDtypeStruct((rows, D), BF)] * trees
        + [jax.ShapeDtypeStruct((total, pair), BF)],
        scratch_shapes=[pltpu.VMEM((total, D), F32), pltpu.VMEM((wide, total), F32)],
        compiler_params=params(),
        cost_estimate=pl.CostEstimate(
            flops=2 * total * D * hidden,
            transcendentals=0,
            bytes_accessed=2 * D * hidden + 2 * total * hidden,
        ),
        name="mlp_down",
    )(g, x2, w_down, down_down, up_down, *of_next)


def by_tree(u_ref, u, rows):
    for m in range(u_ref.shape[0]):
        u_ref[m] = u[m * rows : (m + 1) * rows, m * RANK : (m + 1) * RANK]


def forward_kernel(trees, first, *refs):
    (o_ref, x_ref, norm_ref, dno_ref, upo_ref, wo_ref, wu_ref, wd_ref, upu_ref, dnd_ref, dnu_ref,
     upd_ref, y_ref, x2_ref, b_ref, g_ref, gp_ref, u2_ref, u3_ref, u4_ref,
     sum_ref, acc_ref, mixed_ref, inner_ref) = refs
    step = pl.program_id(0)
    rows = o_ref.shape[0] // trees

    @pl.when(step < first)
    def _():
        mix(step, rows, o_ref, x_ref, dno_ref, upo_ref, wo_ref, mixed_ref, sum_ref)

    @pl.when(step == first - 1)
    def _():
        by_tree(u2_ref, mixed_ref[...], rows)
        x2_ref[...] = sum_ref[...].astype(BF)
        b = normed(sum_ref, norm_ref)
        b_ref[...] = b
        inner = masked(dot(b, dnu_ref[...], NT), rows)
        inner_ref[...] = inner
        by_tree(u3_ref, inner, rows)
        acc_ref[...] = jnp.zeros_like(acc_ref)

    @pl.when(step >= first)
    def _():
        f = dot(b_ref[...], wu_ref[0]) + dot(inner_ref[...], upu_ref[...])
        square, half = gelu_parts(f)
        g = (f * half).astype(BF)
        sliced(g_ref, g)
        slope = f * ((2 * GELU_C) + (6 * GELU_C * 0.044715) * square)
        sliced(gp_ref, (half + (half * (1.0 - half)) * slope).astype(BF))
        sum_ref[...] += dot(g, wd_ref[...])
        acc_ref[...] += dot(dnd_ref[...], g, NT)

    @pl.when(step == pl.num_programs(0) - 1)
    def _():
        u4 = masked(acc_ref[...].T, rows)
        by_tree(u4_ref, u4, rows)
        y_ref[...] = (sum_ref[...] + dot(u4, upd_ref[...])).astype(BF)


def forward_rest(trees, o, x, norm, held, part, w_down, maps, block=512):
    _, _, dn_out, up_out, dn_up, up_up, dn_down, up_down = maps
    total, wide = o.shape[0], trees * RANK
    rows = total // trees
    shards = held.shape[0]
    hidden = shards * part
    block = min(block, part)
    per = part // block
    at = part // (D // shards)
    once = lambda i: (0, 0)
    early = lambda i: jnp.minimum(i, shards - 1)
    late = lambda i: jnp.maximum(i - shards, 0)
    single = pl.Buffered(1)
    full = pl.BlockSpec((total, D), once)
    hid = pl.BlockSpec((block // SLICE, total, SLICE), lambda i: (late(i), 0, 0))
    ranks = pl.BlockSpec((trees, rows, RANK), lambda i: (0, 0, 0))
    return pl.pallas_call(
        functools.partial(forward_kernel, trees, shards),
        grid=(shards + hidden // block,),
        in_specs=[pl.BlockSpec((total, D), once, pipeline_mode=single)] * 2
        + [
            pl.BlockSpec((2, D), once),
            pl.BlockSpec((wide, D), once),
            pl.BlockSpec((wide, D // shards), lambda i: (0, early(i))),
            pl.BlockSpec((1, D, D // shards), lambda i: (early(i), 0, at)),
            pl.BlockSpec((1, D, block), lambda i: (late(i) // per, 0, late(i) % per)),
            pl.BlockSpec((block, D), lambda i: (late(i), 0)),
            pl.BlockSpec((wide, block), lambda i: (0, late(i))),
            pl.BlockSpec((wide, block), lambda i: (0, late(i))),
            pl.BlockSpec((wide, D), once),
            pl.BlockSpec((wide, D), once),
        ],
        out_specs=[
            full,
            full,
            full,
            hid,
            hid,
            ranks,
            ranks,
            ranks,
        ],
        out_shape=[jax.ShapeDtypeStruct((total, D), BF)] * 3
        + [jax.ShapeDtypeStruct((hidden // SLICE, total, SLICE), BF)] * 2
        + [jax.ShapeDtypeStruct((trees, rows, RANK), BF)] * 3,
        scratch_shapes=[
            pltpu.VMEM((total, D), F32),
            pltpu.VMEM((wide, total), F32),
            pltpu.VMEM((total, wide), BF),
            pltpu.VMEM((total, wide), BF),
        ],
        compiler_params=params(),
        cost_estimate=pl.CostEstimate(
            flops=4 * total * D * hidden + 2 * total * D * D,
            transcendentals=total * hidden,
            bytes_accessed=4 * D * hidden + 4 * total * hidden + 2 * D * D,
        ),
        name="forward_rest",
    )(o, x, norm, dn_out, up_out, held, held, w_down, up_up, dn_down, dn_up, up_down)


def backward_kernel(given, first, *refs):
    flag_ref, own_ref, *refs = refs
    if given == 2:
        arrived_ref, *refs = refs
    (b_ref, x2_ref, gain_ref, wu_ref, wd_ref, g_ref, gp_ref, u3_ref, u4_ref, upu_ref, dnd_ref,
     dnu_ref, upd_ref, o_ref, u2_ref, dno_ref, upo_ref, wo_ref,
     dr_ref, do_ref, slab_ref,
     dy_ref, sum_ref, du4_ref, du3_ref, du2_ref) = refs
    shards = slab_ref.shape[0]
    small = D // shards
    large = (slab_ref.shape[2] - 4 * small) // 2
    at = [0, small, 2 * small, 3 * small, 3 * small + large, 3 * small + 2 * large]

    def put(which, grad):
        for z in range(shards):
            part = grad[:, z * small : (z + 1) * small].astype(BF)
            slab_ref[z, :, at[which] : at[which] + small] = part

    def put_block(which, index, grad):
        block = grad.shape[1]
        per = large // block
        cols = pl.ds(pl.multiple_of(at[which] + lax.rem(index, per) * block, 128), block)
        slab_ref[index // per, :, cols] = grad.astype(BF)

    step = pl.program_id(0)

    @pl.when(step == 0)
    def _():
        dy = own_ref[...]
        if given == 2:
            dy = jnp.where(flag_ref[0] == 1, dy, arrived_ref[...])
        dy_ref[...] = dy
        du4_ref[...] = (2.0 * dot(dy, upd_ref[...], NT)).astype(BF)
        put(5, dot(u4_ref[0], dy, TN))
        sum_ref[...] = jnp.zeros_like(sum_ref)
        du3_ref[...] = jnp.zeros_like(du3_ref)

    @pl.when(step < first)
    def _():
        du4 = du4_ref[...]
        dg = dot(dy_ref[...], wd_ref[...], NT) + dot(du4, dnd_ref[...])
        df = (joined(gp_ref).astype(F32) * dg).astype(BF)
        put_block(4, step, dot(du4, joined(g_ref), TN))
        put_block(3, step, dot(u3_ref[0], df, TN))
        du3_ref[...] += dot(upu_ref[...], df, NT)
        sum_ref[...] += dot(df, wu_ref[0], NT)

    @pl.when(step == first - 1)
    def _():
        du3 = (2.0 * du3_ref[...].T).astype(BF)
        put(2, dot(du3, b_ref[...], TN))
        db = (sum_ref[...] + dot(du3, dnu_ref[...])).astype(BF).astype(F32)
        back = layer_norm_back(x2_ref[...].astype(F32), gain_ref[0:1, :], db)
        dr = (dy_ref[...].astype(F32) + back).astype(BF)
        dr_ref[...] = dr
        du2_ref[...] = (2.0 * dot(dr, upo_ref[...], NT)).astype(BF)
        put(1, dot(u2_ref[0], dr, TN))

    @pl.when(step >= first)
    def _():
        wide = wo_ref.shape[2]
        du2 = du2_ref[...]
        do = dot(du2, dno_ref[...])
        for z in range(wo_ref.shape[0]):
            do = do + dot(dr_ref[:, z * wide : (z + 1) * wide], wo_ref[z], NT)
        do_ref[...] = do.astype(BF)
        grad = dot(du2, o_ref[...], TN).astype(BF)
        deep = grad.shape[1]
        for z in range(deep // small):
            slab_ref[(step - first) * (deep // small) + z, :, :small] = grad[:, z * small : (z + 1) * small]


def backward_rest(
    which, own, b, x2, gain, held, part, w_down, g, gp, u2, u3, u4, o, maps, arrived=None,
    block=1024,
):
    _, _, dn_out, up_out, dn_up, up_up, dn_down, up_down = maps
    rows = u2.shape[1]
    shards = held.shape[0]
    hidden = shards * part
    block = min(block, part)
    per = part // block
    at = part // (D // shards)
    first = hidden // block
    deep = 512
    once = lambda i, w: (0, 0)
    mine = lambda i, w: (w[1], 0)
    early = lambda i: jnp.minimum(i, first - 1)
    late = lambda i: jnp.maximum(i - first, 0)
    single = pl.Buffered(1)
    row = pl.BlockSpec((rows, D), mine, pipeline_mode=single)
    given = 1 if arrived is None else 2
    hid = pl.BlockSpec((block // SLICE, rows, SLICE), lambda i, w: (early(i), w[1], 0))
    thin = pl.BlockSpec((RANK, block), lambda i, w: (w[1], early(i)))
    ranks = pl.BlockSpec((1, rows, RANK), lambda i, w: (w[1], 0, 0))
    across = pl.BlockSpec((RANK, D), mine)
    shape = jax.ShapeDtypeStruct
    columns = 4 * (D // shards) + 2 * part
    return pl.pallas_call(
        functools.partial(backward_kernel, given, first),
        grid_spec=pltpu.PrefetchScalarGridSpec(
            num_scalar_prefetch=1,
            grid=(first + D // deep,),
            in_specs=[row]
            + [pl.BlockSpec((rows, D), once, pipeline_mode=single)] * (given - 1)
            + [
                row,
                row,
                pl.BlockSpec((2, D), once),
                pl.BlockSpec((1, D, block), lambda i, w: (early(i) // per, 0, early(i) % per)),
                pl.BlockSpec((block, D), lambda i, w: (early(i), 0)),
                hid,
                hid,
                ranks,
                ranks,
                thin,
                thin,
                across,
                across,
                pl.BlockSpec((rows, deep), lambda i, w: (w[1], late(i))),
                ranks,
                pl.BlockSpec((RANK, deep), lambda i, w: (w[1], late(i))),
                across,
                pl.BlockSpec((shards, deep, D // shards), lambda i, w: (0, late(i), at)),
            ],
            out_specs=[
                pl.BlockSpec((rows, D), once),
                pl.BlockSpec((rows, deep), lambda i, w: (0, late(i))),
                pl.BlockSpec((shards, RANK, columns), lambda i, w: (0, 0, 0)),
            ],
            scratch_shapes=[
                pltpu.VMEM((rows, D), BF),
                pltpu.VMEM((rows, D), F32),
                pltpu.VMEM((rows, RANK), BF),
                pltpu.VMEM((RANK, rows), F32),
                pltpu.VMEM((rows, RANK), BF),
            ],
        ),
        out_shape=[shape((rows, D), BF)] * 2 + [shape((shards, RANK, columns), BF)],
        compiler_params=params(),
        cost_estimate=pl.CostEstimate(
            flops=4 * rows * D * hidden + 2 * rows * D * D,
            transcendentals=0,
            bytes_accessed=4 * D * hidden + 4 * rows * hidden + 2 * D * D,
        ),
        name="backward_rest",
    )(
        which, own, *([] if arrived is None else [arrived]),
        b, x2, gain, held, w_down, g, gp, u3, u4, up_up, dn_down, dn_up, up_down,
        o, u2, dn_out, up_out, held,
    )


def place_kernel(groups, trees, ids_ref, *refs):
    count = sum(members for _, members, _ in groups)
    slab_refs, grad_refs = refs[:count], refs[count:]
    for ref in grad_refs:
        ref[...] = jnp.zeros_like(ref)
    at = 0
    for tree, members, parts in groups:
        for r in range(members):
            name = ids_ref[r * trees + tree]
            for which, start, width in parts:
                grad_refs[which][name] += slab_refs[at][:, start : start + width].astype(F32)
            at += 1


def place(ids, groups, trees, widths, adapters):
    slabs = [slab for _, slabs, _ in groups for slab in slabs]
    every = lambda i, ids: (0, 0, 0)
    return pl.pallas_call(
        functools.partial(
            place_kernel, [(tree, len(held), parts) for tree, held, parts in groups], trees
        ),
        grid_spec=pltpu.PrefetchScalarGridSpec(
            num_scalar_prefetch=1,
            grid=(1,),
            in_specs=[pl.BlockSpec(slab.shape, lambda i, ids: (0, 0)) for slab in slabs],
            out_specs=[pl.BlockSpec((adapters, RANK, width), every) for width in widths],
        ),
        out_shape=[jax.ShapeDtypeStruct((adapters, RANK, width), F32) for width in widths],
        compiler_params=params(),
        cost_estimate=pl.CostEstimate(
            flops=0, transcendentals=0, bytes_accessed=6 * sum(slab.size for slab in slabs)
        ),
        name="place",
    )(ids, *slabs)


def segment_of(places, lengths):
    order = jnp.arange(lengths.shape[0], dtype=jnp.int32)
    ends = jnp.sum(
        jnp.where(order[None, :] <= order[:, None], lengths[None, :], 0), axis=1, dtype=jnp.int32
    )
    return jnp.sum((places[:, None] >= ends[None, :]).astype(jnp.int32), axis=1, dtype=jnp.int32)


def ancestry(parents):
    seg_ids = jnp.arange(parents.shape[0], dtype=jnp.int32)
    current = seg_ids
    reach = current[:, None] == seg_ids[None, :]
    for sweep in range(parents.shape[0] - 1):
        current = jnp.sum(
            jnp.where(current[:, None] == seg_ids[None, :], parents[None, :], 0),
            axis=1,
            dtype=jnp.int32,
        )
        reach = reach | (current[:, None] == seg_ids[None, :])
    return reach.astype(BF)


def key_bias(lengths, parents, query_places, key_places):
    seg_ids = jnp.arange(parents.shape[0], dtype=jnp.int32)
    of_query = (segment_of(query_places, lengths)[:, None] == seg_ids[None, :]).astype(BF)
    of_key = (segment_of(key_places, lengths)[:, None] == seg_ids[None, :]).astype(BF)
    known = ancestry(parents)

    def bias(rows_in, rows_out, place_query, place_key):
        reach = dot(rows_in, rows_out, NT)
        allowed = (reach > 0.5) & (place_key <= place_query) & (place_key >= 0)
        return jnp.where(allowed, 0.0, MASKED).astype(F32)

    anc = dot(of_query, known).astype(BF)
    return (
        bias(anc, of_key, query_places[:, None], key_places[None, :]),
        bias(of_key, anc, query_places[None, :], key_places[:, None]),
    )


def shifted(value, axis, steps):
    count = lax.axis_size(axis)
    return lax.ppermute(value, axis, [(i, (i + steps) % count) for i in range(count)])


def local(
    inputs, cotangent, norm_gains, norm_biases, w_attn, w_out, w_up, w_down,
    down_attn, up_attn, down_out, up_out, down_up, up_up, down_down, up_down,
    seg_lengths, parent_ids, adapter_ids,
):
    section = lax.axis_index("section")
    shard = lax.axis_index("fsdp")
    member = lax.axis_index("replica")
    shards = lax.axis_size("fsdp")
    members = lax.axis_size("replica")
    trees, per_tree = inputs.shape[0], inputs.shape[1]
    gain = norm_gains[0].astype(F32)
    shift = norm_biases[0].astype(F32)
    norms = [jnp.stack([gain[i], shift[i]]) for i in range(2)]
    is_first = (section == 0).astype(jnp.int32).reshape(1)

    def quarter(weight):
        part = weight.shape[0] // members
        return lax.dynamic_slice_in_dim(weight, member * part, part, 0)

    def gathered(own):
        return lax.all_gather(own[None], ("fsdp", "replica"), axis=1, tiled=True)[0]

    part, out_wide, attn_wide = w_up.shape[2], w_out.shape[2], w_attn.shape[2]
    padded = -(-attn_wide // 128) * 128
    attn_at = -(-(part + out_wide) // padded) * padded
    each = D // members
    own = pack(member, each, w_up[0], w_out[0], w_attn[0].T, attn_at, attn_at + padded)
    held = gathered(own).reshape(shards, D, own.shape[1])
    down_full = gathered(quarter(w_down[0]))
    attn_full = assemble(held, attn_at, attn_wide)

    stacks = (down_attn, up_attn, down_out, up_out, down_up, up_up, down_down, up_down)
    widths = [stack.shape[3] for stack in stacks]
    starts = [sum(widths[:i]) for i in range(len(widths))]
    chosen = adapter_ids[:, 0, 0]
    picked = jnp.concatenate(
        [
            jnp.concatenate(
                [lax.dynamic_index_in_dim(stack[0], chosen[m], 0, keepdims=False) for m in range(trees)],
                axis=0,
            )
            for stack in stacks
        ],
        axis=1,
    )
    owners = lax.all_gather(chosen, "replica", axis=0, tiled=True)
    owners, picked = lax.optimization_barrier((owners, picked))
    ups, downs = [picked], [picked]
    for k in range(1, shards):
        ups.append(lax.ppermute(ups[-1], "fsdp", [(i, i + 1) for i in range(shards - 1)]))
        downs.append(lax.ppermute(downs[-1], "fsdp", [(i + 1, i) for i in range(shards - 1)]))
    behind = jnp.stack(
        [picked] + [jnp.where(shard >= k, ups[k], downs[shards - k]) for k in range(1, shards)]
    )
    ordered = [
        lax.dynamic_index_in_dim(behind, lax.rem(shard - z + shards, shards), 0, keepdims=False)
        for z in range(shards)
    ]
    maps = [
        jnp.concatenate([piece[:, at : at + width] for piece in ordered], axis=1)
        for at, width in zip(starts, widths)
    ]
    dn_attn, up_attn_, dn_out, up_out_, dn_up, up_up_, dn_down, up_down_ = maps

    query_places = shard * per_tree + jnp.arange(per_tree, dtype=jnp.int32)
    key_places = jnp.concatenate(
        [(shard - s) * per_tree + jnp.arange(per_tree, dtype=jnp.int32) for s in range(shards)]
    )
    biases = [
        key_bias(seg_lengths[m, 0], parent_ids[m, 0], query_places, key_places)
        for m in range(trees)
    ]

    def to_higher(value, steps):
        return lax.ppermute(value, "fsdp", [(i, i + steps) for i in range(shards - steps)])

    def to_lower(value, steps):
        return lax.ppermute(value, "fsdp", [(i + steps, i) for i in range(shards - steps)])

    def with_lower(kv):
        return [kv] + [to_higher(kv, s) for s in range(1, shards)]

    own_rows = inputs.reshape(trees * per_tree, D)
    entered = [
        entry(m, trees, own_rows, norms[0], dn_attn, up_attn_, attn_full) for m in range(trees)
    ]
    own_kv = jnp.concatenate([part[2] for part in entered], axis=0)
    blocks = with_lower(own_kv)
    attended = ()
    for m, (a, u1, _) in enumerate(entered):
        q = queries(m, a, u1, up_attn_, attn_full)
        attended = attention_forward(m, trees, q, blocks, biases[m][0], attended)
    x2, b = mixing(attended[0], own_rows, norms[1], dn_out, up_out_, held, part)
    g = mlp_up(b, held, part, up_up_, dn_up)
    of_last = [
        lax.ppermute(value, "section", [(1, 0)])
        for value in (norms[0], dn_attn, up_attn_[:, D:], attn_full[:, D:])
    ]
    bias = jnp.concatenate([pair[1] for pair in biases], axis=0)
    g, of_last = lax.optimization_barrier((g, of_last))
    *sent, sent_kv = mlp_down(trees, g, x2, down_full, dn_down, up_down_, of_last)
    arrived_kv = lax.ppermute(sent_kv, "section", [(0, 1)])
    sent, arrived_kv = lax.optimization_barrier((sent, arrived_kv))
    arrived = [lax.ppermute(rows, "section", [(0, 1)]) for rows in sent]
    blocks = with_lower(jnp.where(section == 0, own_kv, arrived_kv))
    entered = ()
    for m in range(trees):
        rows = arrived[m]
        if m:
            rows, entered = lax.optimization_barrier((rows, entered))
        entered = enter(
            m, trees, own_rows, rows, is_first, norms[0], dn_attn, up_attn_, attn_full, blocks,
            biases[m][0], entered,
        )
    o, lse, q, x, a, u1 = entered
    layer_out, x2, b, g, gp, u2, u3, u4 = forward_rest(
        trees, o, x, norms[1], held, part, down_full, maps
    )
    def scattered(slabs):
        return lax.psum_scatter(slabs, "fsdp", scatter_dimension=0)

    def permuted(slabs):
        total = lax.dynamic_index_in_dim(slabs, shard, 0, keepdims=False).astype(F32)
        for k in range(1, shards):
            part = lax.dynamic_index_in_dim(slabs, lax.rem(shard + k, shards), 0, keepdims=False)
            total = total + shifted(part, "fsdp", k).astype(F32)
        return total.astype(BF)

    def all_replicas(total):
        return [total] + [shifted(total, "replica", i) for i in range(1, members)]

    own_grads = cotangent.reshape(trees * per_tree, D)
    order = lax.rem(member - jnp.arange(members, dtype=jnp.int32) + members, members)
    cyclic = owners.reshape(members, trees)[order].reshape(-1)
    early_ones, late_ones = tuple(range(2, len(stacks))), (0, 1)

    def columns(order):
        return [(i, sum(widths[j] for j in order[:at]), widths[i]) for at, i in enumerate(order)]

    in_grads, sums, arrived, before, total, ready = [], [], None, None, None, None
    for step in range(trees + 1):
        tree = jnp.clip(step - 1 + section, 0, trees - 1)
        which = jnp.stack([section, tree]).astype(jnp.int32)
        if arrived is None:
            which = jnp.array([1, 0], jnp.int32)
        total = None
        if ready is not None:
            arrived, ready = lax.optimization_barrier((arrived, ready))
            in_grads.append(ready[0])
            total = scattered(ready[1])
        dr, do, slab = backward_rest(
            which, own_grads, b, x2, norms[1], held, part, down_full, g, gp, u2, u3, u4,
            o, maps, arrived,
        )
        if total is not None:
            do, total = lax.optimization_barrier((do, total))
            total = all_replicas(total)
        early_sum = scattered(slab) if step == trees else None
        dq, dkv = attention_backward(which, q, do, o, blocks, bias, lse)
        dkv = [dkv[0]] + [to_lower(dkv[s], s) for s in range(1, shards)]
        if total is not None:
            dq, total = lax.optimization_barrier((dq, total))
            sums.append((step - 2, total, columns(early_ones + late_ones)))
        da, du = query_leaving(which, dq, up_attn_, attn_full)
        if early_sum is not None:
            da, early_sum = lax.optimization_barrier((da, early_sum))
        dx, late = leaving(
            which, dq, da, du, dkv, a, u1, x, dr, norms[0], dn_attn, up_attn_, attn_full, shards
        )
        if step < trees:
            arrived = lax.ppermute(dx, "section", [(1, 0)])
        now = (dx, slab, late)
        ready = None
        if 0 < step < trees:
            dx_ready, *grads = (
                jnp.where(section == 1, was, new) for was, new in zip(before, now)
            )
            ready = (dx_ready, jnp.concatenate(grads, axis=2))
        before = now
    in_grads.append(dx)
    early_sums, late = lax.optimization_barrier((all_replicas(early_sum), late))
    sums.append((trees - 1, early_sums, columns(early_ones)))
    sums.append((trees - 1, all_replicas(permuted(late)), columns(late_ones)))
    placed = place(cyclic, sums, trees, widths, down_attn.shape[1])
    finals = [grad[None] for grad in placed]
    return (
        layer_out.reshape(1, trees, per_tree, D),
        jnp.stack(in_grads)[None],
        *finals,
    )


def solution(mesh):
    rows = P(None, ("replica", "fsdp"), None)
    stack = P("section", None, None, "fsdp")
    placed = (
        (rows, rows)
        + (P("section", None, None),) * 2
        + (P("section", None, "fsdp"),) * 3
        + (P("section", "fsdp", None),)
        + (stack,) * 8
        + (P(None, "replica", None),) * 3
    )
    return jax.shard_map(
        local,
        mesh=mesh,
        in_specs=placed,
        out_specs=(P("section", None, ("replica", "fsdp"), None),) * 2 + (stack,) * 8,
        check_vma=False,
    )
```

```python
import functools
import math

import jax
import jax.numpy as jnp
from jax import lax
from jax.experimental import pallas as pl
from jax.experimental.pallas import tpu as pltpu
from jax.sharding import PartitionSpec as P

D = 2048
HEADS = 16
HEAD_DIM = 128
RANK = 16

NORM_EPS = 1e-05
MASKED = -1e30
BF = jnp.bfloat16
F32 = jnp.float32
INV_ROOT = HEAD_DIM ** (-0.5)
LOG2E = math.log2(math.e)
LN2 = math.log(2.0)
GELU_C = math.sqrt(2.0 / math.pi)
VMEM_LIMIT = 53 * 1024 * 1024
SLICE = 512

NN = (((1,), (0,)), ((), ()))
NT = (((1,), (1,)), ((), ()))
TN = (((0,), (0,)), ((), ()))


def dot(left, right, dims=NN):
    return lax.dot_general(left, right, dims, preferred_element_type=F32)


def params(steps=1):
    return pltpu.CompilerParams(
        dimension_semantics=("arbitrary",) * steps, vmem_limit_bytes=VMEM_LIMIT
    )


def layer_norm(rows, gain, shift):
    centre = rows - jnp.mean(rows, axis=-1, keepdims=True)
    spread = jnp.mean(centre * centre, axis=-1, keepdims=True)
    return centre * lax.rsqrt(spread + NORM_EPS) * gain + shift


def layer_norm_back(rows, gain, grad):
    centre = rows - jnp.mean(rows, axis=-1, keepdims=True)
    spread = jnp.mean(centre * centre, axis=-1, keepdims=True)
    scale = lax.rsqrt(spread + NORM_EPS)
    unit = centre * scale
    inner = grad * gain
    return scale * (
        inner
        - jnp.mean(inner, axis=-1, keepdims=True)
        - unit * jnp.mean(inner * unit, axis=-1, keepdims=True)
    )


def tree_mask(rows, per_tree):
    row = lax.broadcasted_iota(jnp.int32, (rows, (rows // per_tree) * RANK), 0)
    col = lax.broadcasted_iota(jnp.int32, (rows, (rows // per_tree) * RANK), 1)
    return (row // per_tree) == (col // RANK)


def masked(value, per_tree):
    return jnp.where(tree_mask(value.shape[0], per_tree), 2.0 * value, 0.0).astype(BF)


def attend(heads, q_ref, kv_refs, bias_ref, o_ref, lse_ref):
    keys = jnp.concatenate([r[:, :HEAD_DIM] for r in kv_refs], axis=0)
    vals = jnp.concatenate([r[:, HEAD_DIM:] for r in kv_refs], axis=0)
    vals = jnp.concatenate([vals, jnp.ones_like(vals)], axis=1)
    for h in range(heads):
        cols = slice(h * HEAD_DIM, (h + 1) * HEAD_DIM)
        scores = dot(q_ref[:, cols], keys, NT) + bias_ref[...]
        top = jnp.max(scores, axis=1, keepdims=True)
        probs = jnp.exp2(scores - top)
        mixed = dot(probs.astype(BF), vals)
        total = mixed[:, HEAD_DIM:]
        o_ref[:, cols] = (mixed[:, :HEAD_DIM] / total).astype(BF)
        lse_ref[0, h : h + 1, :] = (top + jnp.log2(total)).T[0:1, :]


def attention_forward_kernel(blocks, heads, before, q_ref, *refs):
    kv_refs, (bias_ref, *refs) = refs[:blocks], refs[blocks:]
    attend(heads, q_ref, kv_refs, bias_ref, *refs[before:])


def attention_forward(tree, trees, q, kv, bias, before, heads=8):
    rows = q.shape[0]
    blocks = len(kv)
    wide = heads * HEAD_DIM
    steps = HEADS // heads
    return pl.pallas_call(
        functools.partial(attention_forward_kernel, blocks, heads, len(before)),
        grid=(steps,),
        in_specs=[pl.BlockSpec((rows, wide), lambda i: (0, i))]
        + [pl.BlockSpec((rows, 2 * HEAD_DIM), lambda i: (tree, 0))] * blocks
        + [pl.BlockSpec((rows, blocks * rows), lambda i: (0, 0))]
        + [pl.BlockSpec(memory_space=pl.ANY)] * len(before),
        out_specs=[
            pl.BlockSpec((rows, wide), lambda i: (tree, i)),
            pl.BlockSpec((1, heads, rows), lambda i: (tree * steps + i, 0, 0)),
        ],
        out_shape=[
            jax.ShapeDtypeStruct((trees * rows, D), BF),
            jax.ShapeDtypeStruct((trees * steps, heads, rows), F32),
        ],
        input_output_aliases={blocks + 2 + i: i for i in range(len(before))},
        compiler_params=params(),
        cost_estimate=pl.CostEstimate(
            flops=8 * rows * rows * blocks * D,
            transcendentals=rows * rows * blocks * HEADS,
            bytes_accessed=4 * rows * D + 4 * rows * rows * blocks,
        ),
        name="attention_forward",
    )(q, *kv, bias, *before)


def attention_backward_kernel(blocks, heads, _, q_ref, do_ref, o_ref, *refs):
    kv_refs = refs[:blocks]
    bias_ref, lse_ref, dq_ref, *dkv_refs, acc_ref = refs[blocks:]
    rows = q_ref.shape[0]
    step = pl.program_id(0)

    @pl.when(step == 0)
    def _():
        acc_ref[...] = jnp.zeros_like(acc_ref)

    keys = jnp.concatenate([r[:, :HEAD_DIM] for r in kv_refs], axis=0)
    vals = jnp.concatenate([r[:, HEAD_DIM:] for r in kv_refs], axis=0)
    keys_t = keys.T
    for h in range(heads):
        cols = slice(h * HEAD_DIM, (h + 1) * HEAD_DIM)
        q, do = q_ref[:, cols], do_ref[:, cols]
        delta = jnp.sum(
            (do.astype(F32) * o_ref[:, cols].astype(F32)).T, axis=0, keepdims=True
        )
        scores = dot(keys, q, NT) + bias_ref[...]
        probs = jnp.exp2(scores - lse_ref[0, h : h + 1, :])
        dprobs = dot(vals, do, NT)
        dscores = (probs * (dprobs - delta)).astype(BF)
        acc_ref[:, :HEAD_DIM] += dot(dscores, q)
        acc_ref[:, HEAD_DIM:] += dot(probs.astype(BF), do)
        dq_ref[:, cols] = (dot(keys_t, dscores) * INV_ROOT).T.astype(BF)

    @pl.when(step == pl.num_programs(0) - 1)
    def _():
        for s in range(blocks):
            part = slice(s * rows, (s + 1) * rows)
            dkv_refs[s][:, :HEAD_DIM] = (acc_ref[part, :HEAD_DIM] * LN2).astype(BF)
            dkv_refs[s][:, HEAD_DIM:] = acc_ref[part, HEAD_DIM:].astype(BF)


def attention_backward(which, q, do, o, kv, bias, lse):
    rows = do.shape[0]
    blocks = len(kv)
    trees = q.shape[0] // rows
    heads = lse.shape[1]
    steps = lse.shape[0] // trees
    wide = heads * HEAD_DIM
    mine = lambda i, w: (w[1], i)
    pair = pl.BlockSpec((rows, 2 * HEAD_DIM), lambda i, w: (0, 0))
    dq, *dkv = pl.pallas_call(
        functools.partial(attention_backward_kernel, blocks, heads),
        grid_spec=pltpu.PrefetchScalarGridSpec(
            num_scalar_prefetch=1,
            grid=(steps,),
            in_specs=[
                pl.BlockSpec((rows, wide), mine),
                pl.BlockSpec((rows, wide), lambda i, w: (0, i)),
                pl.BlockSpec((rows, wide), mine),
            ]
            + [pl.BlockSpec((rows, 2 * HEAD_DIM), lambda i, w: (w[1], 0))] * blocks
            + [
                pl.BlockSpec((blocks * rows, rows), lambda i, w: (w[1], 0)),
                pl.BlockSpec((1, heads, rows), lambda i, w: (w[1] * steps + i, 0, 0)),
            ],
            out_specs=[pl.BlockSpec((rows, wide), lambda i, w: (0, i))] + [pair] * blocks,
            scratch_shapes=[pltpu.VMEM((blocks * rows, 2 * HEAD_DIM), F32)],
        ),
        out_shape=[jax.ShapeDtypeStruct((rows, D), BF)]
        + [jax.ShapeDtypeStruct((rows, 2 * HEAD_DIM), BF)] * blocks,
        compiler_params=params(),
        cost_estimate=pl.CostEstimate(
            flops=20 * rows * rows * blocks * D,
            transcendentals=rows * rows * blocks * HEADS,
            bytes_accessed=8 * rows * D + 4 * rows * rows * blocks,
        ),
        name="attention_backward",
    )(which, q, do, o, *kv, bias, lse)
    return dq, dkv


def pack_kernel(at, _, up_ref, out_ref, attn_ref, all_ref):
    part, wide = up_ref.shape[1], attn_ref.shape[0]
    after = part + out_ref.shape[1]
    all_ref[:, :part] = up_ref[...]
    all_ref[:, part:after] = out_ref[...]
    if at > after:
        all_ref[:, after:at] = jnp.zeros((all_ref.shape[0], at - after), BF)
    attn = attn_ref[...].T
    spare = all_ref.shape[1] - at - wide
    if spare:
        attn = jnp.concatenate([attn, jnp.zeros((attn.shape[0], spare), BF)], axis=1)
    all_ref[:, at:] = attn


def pack(member, each, up, out, attn_t, at, total):
    return pl.pallas_call(
        functools.partial(pack_kernel, at),
        grid_spec=pltpu.PrefetchScalarGridSpec(
            num_scalar_prefetch=1,
            grid=(1,),
            in_specs=[
                pl.BlockSpec((each, up.shape[1]), lambda i, w: (w[0], 0)),
                pl.BlockSpec((each, out.shape[1]), lambda i, w: (w[0], 0)),
                pl.BlockSpec((attn_t.shape[0], each), lambda i, w: (0, w[0])),
            ],
            out_specs=pl.BlockSpec((each, total), lambda i, w: (0, 0)),
        ),
        out_shape=jax.ShapeDtypeStruct((each, total), BF),
        compiler_params=params(),
        cost_estimate=pl.CostEstimate(
            flops=0, transcendentals=0, bytes_accessed=4 * each * total
        ),
        name="pack",
    )(member.astype(jnp.int32).reshape(1), up, out, attn_t)


def assemble_kernel(wide, held_ref, full_ref):
    full_ref[...] = jnp.concatenate(
        [held_ref[z][:, :wide] for z in range(held_ref.shape[0])], axis=1
    )


def assemble(held, start, wide, block=256):
    shards, depth, _ = held.shape
    padded = -(-wide // 128) * 128
    return pl.pallas_call(
        functools.partial(assemble_kernel, wide),
        grid=(depth // block,),
        in_specs=[pl.BlockSpec((shards, block, padded), lambda i: (0, i, start // padded))],
        out_specs=pl.BlockSpec((block, shards * wide), lambda i: (i, 0)),
        out_shape=jax.ShapeDtypeStruct((depth, shards * wide), BF),
        compiler_params=params(),
        cost_estimate=pl.CostEstimate(
            flops=0, transcendentals=0, bytes_accessed=4 * shards * depth * padded
        ),
        name="assemble",
    )(held)


def ranks_of(rows, norm_ref, dn_ref):
    a = layer_norm(rows.astype(F32), norm_ref[0:1, :], norm_ref[1:2, :]).astype(BF)
    return a, dot(a, dn_ref[...], NT)


def entry_kernel(x_ref, norm_ref, dn_ref, up_ref, w_ref, a_ref, u_ref, kv_ref):
    a, u = ranks_of(x_ref[...], norm_ref, dn_ref)
    a_ref[...] = a
    u = (2.0 * u).astype(BF)
    u_ref[...] = u
    kv_ref[...] = (dot(a, w_ref[...]) + dot(u, up_ref[...])).astype(BF)


def entry(tree, trees, x, norm, dn, up, w):
    rows = x.shape[0] // trees
    wide = 2 * HEAD_DIM
    last = D // wide
    whole = lambda i: (0, 0)
    return pl.pallas_call(
        entry_kernel,
        grid=(1,),
        in_specs=[
            pl.BlockSpec((rows, D), lambda i: (tree, 0)),
            pl.BlockSpec((2, D), whole),
            pl.BlockSpec((RANK, D), lambda i: (tree, 0)),
            pl.BlockSpec((RANK, wide), lambda i: (tree, last)),
            pl.BlockSpec((D, wide), lambda i: (0, last)),
        ],
        out_specs=[
            pl.BlockSpec((rows, D), whole),
            pl.BlockSpec((rows, RANK), whole),
            pl.BlockSpec((rows, wide), whole),
        ],
        out_shape=[
            jax.ShapeDtypeStruct((rows, D), BF),
            jax.ShapeDtypeStruct((rows, RANK), BF),
            jax.ShapeDtypeStruct((rows, wide), BF),
        ],
        compiler_params=params(),
        cost_estimate=pl.CostEstimate(
            flops=3 * rows * D * wide, transcendentals=0, bytes_accessed=8 * rows * D
        ),
        name="entry",
    )(x, norm, dn, up, w)


def enter_kernel(
    blocks, heads, before, flag_ref, own_ref, arrived_ref, norm_ref, dn_ref, up_ref, w_ref, *refs
):
    kv_refs, (bias_ref, *refs) = refs[:blocks], refs[blocks:]
    o_ref, lse_ref, q_ref, x_all, a_ref, u_ref = refs[before:]

    @pl.when(pl.program_id(0) == 0)
    def _():
        x = jnp.where(flag_ref[0] == 1, own_ref[...], arrived_ref[...])
        x_all[...] = x
        a, u = ranks_of(x, norm_ref, dn_ref)
        a_ref[...] = a
        u_ref[0] = (2.0 * u).astype(BF)

    q = dot(a_ref[...], w_ref[...]) + dot(u_ref[0], up_ref[...])
    q_ref[...] = (q * (INV_ROOT * LOG2E)).astype(BF)
    attend(heads, q_ref, kv_refs, bias_ref, o_ref, lse_ref)


def enter(tree, trees, own, arrived, flag, norm, dn, up, w, kv, bias, before, heads=8):
    rows = own.shape[0] // trees
    blocks = len(kv)
    wide = heads * HEAD_DIM
    steps = HEADS // heads
    whole = lambda i, f: (0, 0)
    mine = pl.BlockSpec((rows, D), lambda i, f: (tree, 0))
    part = pl.BlockSpec((rows, wide), lambda i, f: (tree, i))
    tall = jax.ShapeDtypeStruct((trees * rows, D), BF)
    return pl.pallas_call(
        functools.partial(enter_kernel, blocks, heads, len(before)),
        grid_spec=pltpu.PrefetchScalarGridSpec(
            num_scalar_prefetch=1,
            grid=(steps,),
            in_specs=[
                mine,
                pl.BlockSpec((rows, D), whole),
                pl.BlockSpec((2, D), whole),
                pl.BlockSpec((RANK, D), lambda i, f: (tree, 0)),
                pl.BlockSpec((RANK, wide), lambda i, f: (tree, i)),
                pl.BlockSpec((D, wide), lambda i, f: (0, i)),
            ]
            + [pl.BlockSpec((rows, 2 * HEAD_DIM), lambda i, f: (tree, 0))] * blocks
            + [pl.BlockSpec((rows, blocks * rows), whole)]
            + [pl.BlockSpec(memory_space=pl.ANY)] * len(before),
            out_specs=[
                part,
                pl.BlockSpec((1, heads, rows), lambda i, f: (tree * steps + i, 0, 0)),
                part,
                mine,
                mine,
                pl.BlockSpec((1, rows, RANK), lambda i, f: (tree, 0, 0)),
            ],
        ),
        out_shape=[
            tall,
            jax.ShapeDtypeStruct((trees * steps, heads, rows), F32),
            tall,
            tall,
            tall,
            jax.ShapeDtypeStruct((trees, rows, RANK), BF),
        ],
        input_output_aliases={8 + blocks + i: i for i in range(len(before))},
        compiler_params=params(),
        cost_estimate=pl.CostEstimate(
            flops=2 * rows * D * D + 8 * rows * rows * blocks * D,
            transcendentals=rows * rows * blocks * HEADS,
            bytes_accessed=2 * D * D + 16 * rows * D + 4 * rows * rows * blocks,
        ),
        name="enter",
    )(flag, own, arrived, norm, dn, up, w, *kv, bias, *before)


def queries_kernel(a_ref, u_ref, up_ref, w_ref, q_ref):
    q = dot(a_ref[...], w_ref[...]) + dot(u_ref[...], up_ref[...])
    q_ref[...] = (q * (INV_ROOT * LOG2E)).astype(BF)


def queries(tree, a, u, up, w, block=1024):
    rows = a.shape[0]
    return pl.pallas_call(
        queries_kernel,
        grid=(D // block,),
        in_specs=[
            pl.BlockSpec((rows, D), lambda i: (0, 0)),
            pl.BlockSpec((rows, RANK), lambda i: (0, 0)),
            pl.BlockSpec((RANK, block), lambda i: (tree, i)),
            pl.BlockSpec((D, block), lambda i: (0, i)),
        ],
        out_specs=pl.BlockSpec((rows, block), lambda i: (0, i)),
        out_shape=jax.ShapeDtypeStruct((rows, D), BF),
        compiler_params=params(),
        cost_estimate=pl.CostEstimate(
            flops=2 * rows * D * D, transcendentals=0, bytes_accessed=2 * D * D
        ),
        name="queries",
    )(a, u, up, w)


def mix(step, rows, o_ref, x_ref, dn_ref, up_ref, w_ref, u_ref, sum_ref):
    @pl.when(step == 0)
    def _():
        sum_ref[...] = x_ref[...].astype(F32)
        u_ref[...] = masked(dot(o_ref[...], dn_ref[...], NT), rows)

    block = w_ref.shape[2]
    cols = pl.ds(pl.multiple_of(step * block, block), block)
    sum_ref[:, cols] += dot(o_ref[...], w_ref[0]) + dot(u_ref[...], up_ref[...])


def normed(sum_ref, norm_ref):
    return layer_norm(sum_ref[...], norm_ref[0:1, :], norm_ref[1:2, :]).astype(BF)


def mixing_kernel(rows, o_ref, x_ref, norm_ref, dn_ref, up_ref, w_ref, x2_ref, b_ref, u_ref):
    step = pl.program_id(0)
    mix(step, rows, o_ref, x_ref, dn_ref, up_ref, w_ref, u_ref, x2_ref)

    @pl.when(step == pl.num_programs(0) - 1)
    def _():
        b_ref[...] = normed(x2_ref, norm_ref)


def mixing(o, x, norm, dn, up, held, part):
    total, wide = o.shape[0], dn.shape[0]
    shards = held.shape[0]
    block = D // shards
    at = part // block
    whole = lambda i: (0, 0)
    single = pl.Buffered(1)
    return pl.pallas_call(
        functools.partial(mixing_kernel, total * RANK // wide),
        grid=(shards,),
        in_specs=[pl.BlockSpec((total, D), whole, pipeline_mode=single)] * 2
        + [
            pl.BlockSpec((2, D), whole),
            pl.BlockSpec((wide, D), whole),
            pl.BlockSpec((wide, block), lambda i: (0, i)),
            pl.BlockSpec((1, D, block), lambda i: (i, 0, at)),
        ],
        out_specs=[pl.BlockSpec((total, D), whole), pl.BlockSpec((total, D), whole)],
        out_shape=[
            jax.ShapeDtypeStruct((total, D), F32),
            jax.ShapeDtypeStruct((total, D), BF),
        ],
        scratch_shapes=[pltpu.VMEM((total, wide), BF)],
        compiler_params=params(),
        cost_estimate=pl.CostEstimate(
            flops=2 * total * D * D, transcendentals=0, bytes_accessed=2 * D * D + 10 * total * D
        ),
        name="mixing",
    )(o, x, norm, dn, up, held)


def query_leaving_kernel(_, dq_ref, up_ref, w_ref, da_ref, du_ref):
    @pl.when(pl.program_id(0) == 0)
    def _():
        du_ref[...] = dot(dq_ref[...], up_ref[...], NT)

    da_ref[...] = dot(dq_ref[...], w_ref[...], NT)


def query_leaving(which, dq, up, w, block=1024):
    rows = dq.shape[0]
    whole = lambda i, w: (0, 0)
    return pl.pallas_call(
        query_leaving_kernel,
        grid_spec=pltpu.PrefetchScalarGridSpec(
            num_scalar_prefetch=1,
            grid=(D // block,),
            in_specs=[
                pl.BlockSpec((rows, D), whole),
                pl.BlockSpec((RANK, D), lambda i, w: (w[1], 0)),
                pl.BlockSpec((block, D), lambda i, w: (i, 0)),
            ],
            out_specs=[
                pl.BlockSpec((rows, block), lambda i, w: (0, i)),
                pl.BlockSpec((rows, RANK), whole),
            ],
        ),
        out_shape=[
            jax.ShapeDtypeStruct((rows, D), F32),
            jax.ShapeDtypeStruct((rows, RANK), F32),
        ],
        compiler_params=params(),
        cost_estimate=pl.CostEstimate(
            flops=2 * rows * D * D, transcendentals=0, bytes_accessed=2 * D * D
        ),
        name="query_leaving",
    )(which, dq, up, w)


def leaving_kernel(blocks, shards, _, dq_ref, da_ref, du_ref, *refs):
    dkv_refs = refs[:blocks]
    (a_ref, u_ref, x_ref, dr_ref, gain_ref, dn_ref, up_ref, w_ref,
     dx_ref, slab_ref, gdn_ref, gup_ref) = refs[blocks:]
    step = pl.program_id(0)

    @pl.when(step == 0)
    def _():
        gdn_ref[...] = jnp.zeros_like(gdn_ref)
        gup_ref[...] = jnp.zeros_like(gup_ref)

    total = dkv_refs[0][...].astype(F32)
    for ref in dkv_refs[1:]:
        total = total + ref[...].astype(F32)
    dkv = total.astype(BF)
    du = (2.0 * (du_ref[...] + dot(dkv, up_ref[...], NT))).astype(BF)
    gup_ref[:, :D] += dot(u_ref[0], dq_ref[...], TN)
    gup_ref[:, D:] += dot(u_ref[0], dkv, TN)
    gdn_ref[...] += dot(du, a_ref[...], TN)
    da = da_ref[...] + dot(dkv, w_ref[...], NT) + dot(du, dn_ref[...])
    back = layer_norm_back(
        x_ref[...].astype(F32), gain_ref[0:1, :], da.astype(BF).astype(F32)
    )
    dx_ref[...] = (dr_ref[...].astype(F32) + back).astype(BF)

    @pl.when(step == pl.num_programs(0) - 1)
    def _():
        small, large = D // shards, gup_ref.shape[1] // shards
        for z in range(shards):
            slab_ref[z] = jnp.concatenate(
                [
                    gdn_ref[:, z * small : (z + 1) * small],
                    gup_ref[...][:, z * large : (z + 1) * large],
                ],
                axis=1,
            ).astype(BF)


def leaving(which, dq, da, du, dkv, a, u, x, dr, gain, dn, up, w, shards, steps=2):
    rows = da.shape[0] // steps
    wide = 2 * HEAD_DIM
    last = D // wide
    columns = (D + D + wide) // shards
    whole = lambda i, w: (0, 0)
    here = pl.BlockSpec((rows, D), lambda i, w: (i, 0))
    mine = pl.BlockSpec((rows, D), lambda i, w: (w[1] * steps + i, 0))
    return pl.pallas_call(
        functools.partial(leaving_kernel, len(dkv), shards),
        grid_spec=pltpu.PrefetchScalarGridSpec(
            num_scalar_prefetch=1,
            grid=(steps,),
            in_specs=[here, here, pl.BlockSpec((rows, RANK), lambda i, w: (i, 0))]
            + [pl.BlockSpec((rows, wide), lambda i, w: (i, 0))] * len(dkv)
            + [
                mine,
                pl.BlockSpec((1, rows, RANK), lambda i, w: (w[1], i, 0)),
                mine,
                here,
                pl.BlockSpec((2, D), whole),
                pl.BlockSpec((RANK, D), lambda i, w: (w[1], 0)),
                pl.BlockSpec((RANK, wide), lambda i, w: (w[1], last)),
                pl.BlockSpec((D, wide), lambda i, w: (0, last)),
            ],
            out_specs=[here, pl.BlockSpec((shards, RANK, columns), lambda i, w: (0, 0, 0))],
            scratch_shapes=[pltpu.VMEM((RANK, D), F32), pltpu.VMEM((RANK, D + wide), F32)],
        ),
        out_shape=[
            jax.ShapeDtypeStruct(da.shape, BF),
            jax.ShapeDtypeStruct((shards, RANK, columns), BF),
        ],
        compiler_params=params(),
        cost_estimate=pl.CostEstimate(
            flops=8 * rows * D * wide, transcendentals=0, bytes_accessed=28 * rows * D
        ),
        name="leaving",
    )(which, dq, da, du, *dkv, a, u, x, dr, gain, dn, up, w)


def joined(ref):
    return jnp.concatenate([ref[i] for i in range(ref.shape[0])], axis=1)


def sliced(ref, value):
    for i in range(ref.shape[0]):
        ref[i] = value[:, i * SLICE : (i + 1) * SLICE]


def gelu_parts(f):
    square = f * f
    half = 0.5 + 0.5 * jnp.tanh(f * (GELU_C + (GELU_C * 0.044715) * square))
    return square, half


def mlp_up_kernel(per_tree, b_ref, wu_ref, upu_ref, dnu_ref, g_ref, u3_ref):
    @pl.when(pl.program_id(0) == 0)
    def _():
        u3_ref[...] = masked(dot(b_ref[...], dnu_ref[...], NT), per_tree)

    f = dot(b_ref[...], wu_ref[0]) + dot(u3_ref[...], upu_ref[...])
    sliced(g_ref, (f * gelu_parts(f)[1]).astype(BF))


def mlp_up(b, held, part, up_up, down_up, block=1024):
    rows = b.shape[0]
    shards = held.shape[0]
    hidden = shards * part
    wide = down_up.shape[0]
    block = min(block, part)
    per = part // block
    once = lambda j: (0, 0)
    return pl.pallas_call(
        functools.partial(mlp_up_kernel, rows * RANK // wide),
        grid=(hidden // block,),
        in_specs=[
            pl.BlockSpec((rows, D), once),
            pl.BlockSpec((1, D, block), lambda j: (j // per, 0, j % per)),
            pl.BlockSpec((wide, block), lambda j: (0, j)),
            pl.BlockSpec((wide, D), once),
        ],
        out_specs=pl.BlockSpec((block // SLICE, rows, SLICE), lambda j: (j, 0, 0)),
        out_shape=jax.ShapeDtypeStruct((hidden // SLICE, rows, SLICE), BF),
        scratch_shapes=[pltpu.VMEM((rows, wide), BF)],
        compiler_params=params(),
        cost_estimate=pl.CostEstimate(
            flops=2 * rows * D * hidden,
            transcendentals=rows * hidden,
            bytes_accessed=2 * D * hidden + 2 * rows * hidden,
        ),
        name="mlp_up",
    )(b, held, up_up, down_up)


def mlp_down_kernel(
    trees, g_ref, x2_ref, wd_ref, dnd_ref, upd_ref, norm_ref, dn_ref, up_ref, w_ref, *refs
):
    y_refs, (kv_ref, sum_ref, acc_ref) = refs[:trees], refs[trees:]
    step = pl.program_id(0)
    rows = g_ref.shape[1] // trees

    @pl.when(step == 0)
    def _():
        sum_ref[...] = x2_ref[...]
        acc_ref[...] = jnp.zeros_like(acc_ref)

    g = joined(g_ref)
    sum_ref[...] += dot(g, wd_ref[...])
    acc_ref[...] += dot(dnd_ref[...], g, NT)

    @pl.when(step == pl.num_programs(0) - 1)
    def _():
        u4 = masked(acc_ref[...].T, rows)
        y = (sum_ref[...] + dot(u4, upd_ref[...])).astype(BF)
        for m in range(trees):
            y_refs[m][...] = y[m * rows : (m + 1) * rows]
        a, u = ranks_of(y, norm_ref, dn_ref)
        kv_ref[...] = (dot(a, w_ref[...]) + dot(masked(u, rows), up_ref[...])).astype(BF)


def mlp_down(trees, g, x2, w_down, down_down, up_down, of_next, block=1024):
    total, hidden = g.shape[1], g.shape[0] * SLICE
    rows, wide = total // trees, trees * RANK
    pair = 2 * HEAD_DIM
    once = lambda j: (0, 0)
    return pl.pallas_call(
        functools.partial(mlp_down_kernel, trees),
        grid=(hidden // block,),
        in_specs=[
            pl.BlockSpec((block // SLICE, total, SLICE), lambda j: (j, 0, 0)),
            pl.BlockSpec((total, D), once, pipeline_mode=pl.Buffered(1)),
            pl.BlockSpec((block, D), lambda j: (j, 0)),
            pl.BlockSpec((wide, block), lambda j: (0, j)),
            pl.BlockSpec((wide, D), once),
            pl.BlockSpec((2, D), once),
            pl.BlockSpec((wide, D), once),
            pl.BlockSpec((wide, pair), once),
            pl.BlockSpec((D, pair), once),
        ],
        out_specs=[pl.BlockSpec((rows, D), once)] * trees + [pl.BlockSpec((total, pair), once)],
        out_shape=[jax.ShapeDtypeStruct((rows, D), BF)] * trees
        + [jax.ShapeDtypeStruct((total, pair), BF)],
        scratch_shapes=[pltpu.VMEM((total, D), F32), pltpu.VMEM((wide, total), F32)],
        compiler_params=params(),
        cost_estimate=pl.CostEstimate(
            flops=2 * total * D * hidden,
            transcendentals=0,
            bytes_accessed=2 * D * hidden + 2 * total * hidden,
        ),
        name="mlp_down",
    )(g, x2, w_down, down_down, up_down, *of_next)


def by_tree(u_ref, u, rows):
    for m in range(u_ref.shape[0]):
        u_ref[m] = u[m * rows : (m + 1) * rows, m * RANK : (m + 1) * RANK]


def forward_kernel(trees, first, *refs):
    (o_ref, x_ref, norm_ref, dno_ref, upo_ref, wo_ref, wu_ref, wd_ref, upu_ref, dnd_ref, dnu_ref,
     upd_ref, y_ref, x2_ref, b_ref, g_ref, gp_ref, u2_ref, u3_ref, u4_ref,
     sum_ref, acc_ref, mixed_ref, inner_ref) = refs
    step = pl.program_id(0)
    rows = o_ref.shape[0] // trees

    @pl.when(step < first)
    def _():
        mix(step, rows, o_ref, x_ref, dno_ref, upo_ref, wo_ref, mixed_ref, sum_ref)

    @pl.when(step == first - 1)
    def _():
        by_tree(u2_ref, mixed_ref[...], rows)
        x2_ref[...] = sum_ref[...].astype(BF)
        b = normed(sum_ref, norm_ref)
        b_ref[...] = b
        inner = masked(dot(b, dnu_ref[...], NT), rows)
        inner_ref[...] = inner
        by_tree(u3_ref, inner, rows)
        acc_ref[...] = jnp.zeros_like(acc_ref)

    @pl.when(step >= first)
    def _():
        f = dot(b_ref[...], wu_ref[0]) + dot(inner_ref[...], upu_ref[...])
        square, half = gelu_parts(f)
        g = (f * half).astype(BF)
        sliced(g_ref, g)
        slope = f * ((2 * GELU_C) + (6 * GELU_C * 0.044715) * square)
        sliced(gp_ref, (half + (half * (1.0 - half)) * slope).astype(BF))
        sum_ref[...] += dot(g, wd_ref[...])
        acc_ref[...] += dot(dnd_ref[...], g, NT)

    @pl.when(step == pl.num_programs(0) - 1)
    def _():
        u4 = masked(acc_ref[...].T, rows)
        by_tree(u4_ref, u4, rows)
        y_ref[...] = (sum_ref[...] + dot(u4, upd_ref[...])).astype(BF)


def forward_rest(trees, o, x, norm, held, part, w_down, maps, block=512):
    _, _, dn_out, up_out, dn_up, up_up, dn_down, up_down = maps
    total, wide = o.shape[0], trees * RANK
    rows = total // trees
    shards = held.shape[0]
    hidden = shards * part
    block = min(block, part)
    per = part // block
    at = part // (D // shards)
    once = lambda i: (0, 0)
    early = lambda i: jnp.minimum(i, shards - 1)
    late = lambda i: jnp.maximum(i - shards, 0)
    single = pl.Buffered(1)
    full = pl.BlockSpec((total, D), once)
    hid = pl.BlockSpec((block // SLICE, total, SLICE), lambda i: (late(i), 0, 0))
    ranks = pl.BlockSpec((trees, rows, RANK), lambda i: (0, 0, 0))
    return pl.pallas_call(
        functools.partial(forward_kernel, trees, shards),
        grid=(shards + hidden // block,),
        in_specs=[pl.BlockSpec((total, D), once, pipeline_mode=single)] * 2
        + [
            pl.BlockSpec((2, D), once),
            pl.BlockSpec((wide, D), once),
            pl.BlockSpec((wide, D // shards), lambda i: (0, early(i))),
            pl.BlockSpec((1, D, D // shards), lambda i: (early(i), 0, at)),
            pl.BlockSpec((1, D, block), lambda i: (late(i) // per, 0, late(i) % per)),
            pl.BlockSpec((block, D), lambda i: (late(i), 0)),
            pl.BlockSpec((wide, block), lambda i: (0, late(i))),
            pl.BlockSpec((wide, block), lambda i: (0, late(i))),
            pl.BlockSpec((wide, D), once),
            pl.BlockSpec((wide, D), once),
        ],
        out_specs=[
            full,
            full,
            full,
            hid,
            hid,
            ranks,
            ranks,
            ranks,
        ],
        out_shape=[jax.ShapeDtypeStruct((total, D), BF)] * 3
        + [jax.ShapeDtypeStruct((hidden // SLICE, total, SLICE), BF)] * 2
        + [jax.ShapeDtypeStruct((trees, rows, RANK), BF)] * 3,
        scratch_shapes=[
            pltpu.VMEM((total, D), F32),
            pltpu.VMEM((wide, total), F32),
            pltpu.VMEM((total, wide), BF),
            pltpu.VMEM((total, wide), BF),
        ],
        compiler_params=params(),
        cost_estimate=pl.CostEstimate(
            flops=4 * total * D * hidden + 2 * total * D * D,
            transcendentals=total * hidden,
            bytes_accessed=4 * D * hidden + 4 * total * hidden + 2 * D * D,
        ),
        name="forward_rest",
    )(o, x, norm, dn_out, up_out, held, held, w_down, up_up, dn_down, dn_up, up_down)


def backward_kernel(given, first, *refs):
    flag_ref, own_ref, *refs = refs
    if given == 2:
        arrived_ref, *refs = refs
    (b_ref, x2_ref, gain_ref, wu_ref, wd_ref, g_ref, gp_ref, u3_ref, u4_ref, upu_ref, dnd_ref,
     dnu_ref, upd_ref, o_ref, u2_ref, dno_ref, upo_ref, wo_ref,
     dr_ref, do_ref, slab_ref,
     dy_ref, sum_ref, du4_ref, du3_ref, du2_ref) = refs
    shards = slab_ref.shape[0]
    small = D // shards
    large = (slab_ref.shape[2] - 4 * small) // 2
    at = [0, small, 2 * small, 3 * small, 3 * small + large, 3 * small + 2 * large]

    def put(which, grad):
        for z in range(shards):
            part = grad[:, z * small : (z + 1) * small].astype(BF)
            slab_ref[z, :, at[which] : at[which] + small] = part

    def put_block(which, index, grad):
        block = grad.shape[1]
        per = large // block
        cols = pl.ds(pl.multiple_of(at[which] + lax.rem(index, per) * block, 128), block)
        slab_ref[index // per, :, cols] = grad.astype(BF)

    step = pl.program_id(0)

    @pl.when(step == 0)
    def _():
        dy = own_ref[...]
        if given == 2:
            dy = jnp.where(flag_ref[0] == 1, dy, arrived_ref[...])
        dy_ref[...] = dy
        du4_ref[...] = (2.0 * dot(dy, upd_ref[...], NT)).astype(BF)
        put(5, dot(u4_ref[0], dy, TN))
        sum_ref[...] = jnp.zeros_like(sum_ref)
        du3_ref[...] = jnp.zeros_like(du3_ref)

    @pl.when(step < first)
    def _():
        du4 = du4_ref[...]
        dg = dot(dy_ref[...], wd_ref[...], NT) + dot(du4, dnd_ref[...])
        df = (joined(gp_ref).astype(F32) * dg).astype(BF)
        put_block(4, step, dot(du4, joined(g_ref), TN))
        put_block(3, step, dot(u3_ref[0], df, TN))
        du3_ref[...] += dot(upu_ref[...], df, NT)
        sum_ref[...] += dot(df, wu_ref[0], NT)

    @pl.when(step == first - 1)
    def _():
        du3 = (2.0 * du3_ref[...].T).astype(BF)
        put(2, dot(du3, b_ref[...], TN))
        db = (sum_ref[...] + dot(du3, dnu_ref[...])).astype(BF).astype(F32)
        back = layer_norm_back(x2_ref[...].astype(F32), gain_ref[0:1, :], db)
        dr = (dy_ref[...].astype(F32) + back).astype(BF)
        dr_ref[...] = dr
        du2_ref[...] = (2.0 * dot(dr, upo_ref[...], NT)).astype(BF)
        put(1, dot(u2_ref[0], dr, TN))

    @pl.when(step >= first)
    def _():
        wide = wo_ref.shape[2]
        du2 = du2_ref[...]
        do = dot(du2, dno_ref[...])
        for z in range(wo_ref.shape[0]):
            do = do + dot(dr_ref[:, z * wide : (z + 1) * wide], wo_ref[z], NT)
        do_ref[...] = do.astype(BF)
        grad = dot(du2, o_ref[...], TN).astype(BF)
        deep = grad.shape[1]
        for z in range(deep // small):
            slab_ref[(step - first) * (deep // small) + z, :, :small] = grad[:, z * small : (z + 1) * small]


def backward_rest(
    which, own, b, x2, gain, held, part, w_down, g, gp, u2, u3, u4, o, maps, arrived=None,
    block=1024,
):
    _, _, dn_out, up_out, dn_up, up_up, dn_down, up_down = maps
    rows = u2.shape[1]
    shards = held.shape[0]
    hidden = shards * part
    block = min(block, part)
    per = part // block
    at = part // (D // shards)
    first = hidden // block
    deep = 512
    once = lambda i, w: (0, 0)
    mine = lambda i, w: (w[1], 0)
    early = lambda i: jnp.minimum(i, first - 1)
    late = lambda i: jnp.maximum(i - first, 0)
    single = pl.Buffered(1)
    row = pl.BlockSpec((rows, D), mine, pipeline_mode=single)
    given = 1 if arrived is None else 2
    hid = pl.BlockSpec((block // SLICE, rows, SLICE), lambda i, w: (early(i), w[1], 0))
    thin = pl.BlockSpec((RANK, block), lambda i, w: (w[1], early(i)))
    ranks = pl.BlockSpec((1, rows, RANK), lambda i, w: (w[1], 0, 0))
    across = pl.BlockSpec((RANK, D), mine)
    shape = jax.ShapeDtypeStruct
    columns = 4 * (D // shards) + 2 * part
    return pl.pallas_call(
        functools.partial(backward_kernel, given, first),
        grid_spec=pltpu.PrefetchScalarGridSpec(
            num_scalar_prefetch=1,
            grid=(first + D // deep,),
            in_specs=[row]
            + [pl.BlockSpec((rows, D), once, pipeline_mode=single)] * (given - 1)
            + [
                row,
                row,
                pl.BlockSpec((2, D), once),
                pl.BlockSpec((1, D, block), lambda i, w: (early(i) // per, 0, early(i) % per)),
                pl.BlockSpec((block, D), lambda i, w: (early(i), 0)),
                hid,
                hid,
                ranks,
                ranks,
                thin,
                thin,
                across,
                across,
                pl.BlockSpec((rows, deep), lambda i, w: (w[1], late(i))),
                ranks,
                pl.BlockSpec((RANK, deep), lambda i, w: (w[1], late(i))),
                across,
                pl.BlockSpec((shards, deep, D // shards), lambda i, w: (0, late(i), at)),
            ],
            out_specs=[
                pl.BlockSpec((rows, D), once),
                pl.BlockSpec((rows, deep), lambda i, w: (0, late(i))),
                pl.BlockSpec((shards, RANK, columns), lambda i, w: (0, 0, 0)),
            ],
            scratch_shapes=[
                pltpu.VMEM((rows, D), BF),
                pltpu.VMEM((rows, D), F32),
                pltpu.VMEM((rows, RANK), BF),
                pltpu.VMEM((RANK, rows), F32),
                pltpu.VMEM((rows, RANK), BF),
            ],
        ),
        out_shape=[shape((rows, D), BF)] * 2 + [shape((shards, RANK, columns), BF)],
        compiler_params=params(),
        cost_estimate=pl.CostEstimate(
            flops=4 * rows * D * hidden + 2 * rows * D * D,
            transcendentals=0,
            bytes_accessed=4 * D * hidden + 4 * rows * hidden + 2 * D * D,
        ),
        name="backward_rest",
    )(
        which, own, *([] if arrived is None else [arrived]),
        b, x2, gain, held, w_down, g, gp, u3, u4, up_up, dn_down, dn_up, up_down,
        o, u2, dn_out, up_out, held,
    )


def place_kernel(groups, trees, ids_ref, *refs):
    count = sum(members for _, members, _ in groups)
    slab_refs, grad_refs = refs[:count], refs[count:]
    for ref in grad_refs:
        ref[...] = jnp.zeros_like(ref)
    at = 0
    for tree, members, parts in groups:
        for r in range(members):
            name = ids_ref[r * trees + tree]
            for which, start, width in parts:
                grad_refs[which][name] += slab_refs[at][:, start : start + width].astype(F32)
            at += 1


def place(ids, groups, trees, widths, adapters):
    slabs = [slab for _, slabs, _ in groups for slab in slabs]
    every = lambda i, ids: (0, 0, 0)
    return pl.pallas_call(
        functools.partial(
            place_kernel, [(tree, len(held), parts) for tree, held, parts in groups], trees
        ),
        grid_spec=pltpu.PrefetchScalarGridSpec(
            num_scalar_prefetch=1,
            grid=(1,),
            in_specs=[pl.BlockSpec(slab.shape, lambda i, ids: (0, 0)) for slab in slabs],
            out_specs=[pl.BlockSpec((adapters, RANK, width), every) for width in widths],
        ),
        out_shape=[jax.ShapeDtypeStruct((adapters, RANK, width), F32) for width in widths],
        compiler_params=params(),
        cost_estimate=pl.CostEstimate(
            flops=0, transcendentals=0, bytes_accessed=6 * sum(slab.size for slab in slabs)
        ),
        name="place",
    )(ids, *slabs)


def segment_of(places, lengths):
    order = jnp.arange(lengths.shape[0], dtype=jnp.int32)
    ends = jnp.sum(
        jnp.where(order[None, :] <= order[:, None], lengths[None, :], 0), axis=1, dtype=jnp.int32
    )
    return jnp.sum((places[:, None] >= ends[None, :]).astype(jnp.int32), axis=1, dtype=jnp.int32)


def ancestry(parents):
    seg_ids = jnp.arange(parents.shape[0], dtype=jnp.int32)
    current = seg_ids
    reach = current[:, None] == seg_ids[None, :]
    for sweep in range(parents.shape[0] - 1):
        current = jnp.sum(
            jnp.where(current[:, None] == seg_ids[None, :], parents[None, :], 0),
            axis=1,
            dtype=jnp.int32,
        )
        reach = reach | (current[:, None] == seg_ids[None, :])
    return reach.astype(BF)


def key_bias(lengths, parents, query_places, key_places):
    seg_ids = jnp.arange(parents.shape[0], dtype=jnp.int32)
    of_query = (segment_of(query_places, lengths)[:, None] == seg_ids[None, :]).astype(BF)
    of_key = (segment_of(key_places, lengths)[:, None] == seg_ids[None, :]).astype(BF)
    known = ancestry(parents)

    def bias(rows_in, rows_out, place_query, place_key):
        reach = dot(rows_in, rows_out, NT)
        allowed = (reach > 0.5) & (place_key <= place_query) & (place_key >= 0)
        return jnp.where(allowed, 0.0, MASKED).astype(F32)

    anc = dot(of_query, known).astype(BF)
    return (
        bias(anc, of_key, query_places[:, None], key_places[None, :]),
        bias(of_key, anc, query_places[None, :], key_places[:, None]),
    )


def shifted(value, axis, steps):
    count = lax.axis_size(axis)
    return lax.ppermute(value, axis, [(i, (i + steps) % count) for i in range(count)])


def local(
    inputs, cotangent, norm_gains, norm_biases, w_attn, w_out, w_up, w_down,
    down_attn, up_attn, down_out, up_out, down_up, up_up, down_down, up_down,
    seg_lengths, parent_ids, adapter_ids,
):
    section = lax.axis_index("section")
    shard = lax.axis_index("fsdp")
    member = lax.axis_index("replica")
    shards = lax.axis_size("fsdp")
    members = lax.axis_size("replica")
    trees, per_tree = inputs.shape[0], inputs.shape[1]
    gain = norm_gains[0].astype(F32)
    shift = norm_biases[0].astype(F32)
    norms = [jnp.stack([gain[i], shift[i]]) for i in range(2)]
    is_first = (section == 0).astype(jnp.int32).reshape(1)

    def quarter(weight):
        part = weight.shape[0] // members
        return lax.dynamic_slice_in_dim(weight, member * part, part, 0)

    def gathered(own):
        return lax.all_gather(own[None], ("fsdp", "replica"), axis=1, tiled=True)[0]

    part, out_wide, attn_wide = w_up.shape[2], w_out.shape[2], w_attn.shape[2]
    padded = -(-attn_wide // 128) * 128
    attn_at = -(-(part + out_wide) // padded) * padded
    each = D // members
    own = pack(member, each, w_up[0], w_out[0], w_attn[0].T, attn_at, attn_at + padded)
    held = gathered(own).reshape(shards, D, own.shape[1])
    down_full = gathered(quarter(w_down[0]))
    attn_full = assemble(held, attn_at, attn_wide)

    stacks = (down_attn, up_attn, down_out, up_out, down_up, up_up, down_down, up_down)
    widths = [stack.shape[3] for stack in stacks]
    starts = [sum(widths[:i]) for i in range(len(widths))]
    chosen = adapter_ids[:, 0, 0]
    picked = jnp.concatenate(
        [
            jnp.concatenate(
                [lax.dynamic_index_in_dim(stack[0], chosen[m], 0, keepdims=False) for m in range(trees)],
                axis=0,
            )
            for stack in stacks
        ],
        axis=1,
    )
    owners = lax.all_gather(chosen, "replica", axis=0, tiled=True)
    owners, picked = lax.optimization_barrier((owners, picked))
    ups, downs = [picked], [picked]
    for k in range(1, shards):
        ups.append(lax.ppermute(ups[-1], "fsdp", [(i, i + 1) for i in range(shards - 1)]))
        downs.append(lax.ppermute(downs[-1], "fsdp", [(i + 1, i) for i in range(shards - 1)]))
    behind = jnp.stack(
        [picked] + [jnp.where(shard >= k, ups[k], downs[shards - k]) for k in range(1, shards)]
    )
    ordered = [
        lax.dynamic_index_in_dim(behind, lax.rem(shard - z + shards, shards), 0, keepdims=False)
        for z in range(shards)
    ]
    maps = [
        jnp.concatenate([piece[:, at : at + width] for piece in ordered], axis=1)
        for at, width in zip(starts, widths)
    ]
    dn_attn, up_attn_, dn_out, up_out_, dn_up, up_up_, dn_down, up_down_ = maps

    query_places = shard * per_tree + jnp.arange(per_tree, dtype=jnp.int32)
    key_places = jnp.concatenate(
        [(shard - s) * per_tree + jnp.arange(per_tree, dtype=jnp.int32) for s in range(shards)]
    )
    biases = [
        key_bias(seg_lengths[m, 0], parent_ids[m, 0], query_places, key_places)
        for m in range(trees)
    ]

    def to_higher(value, steps):
        return lax.ppermute(value, "fsdp", [(i, i + steps) for i in range(shards - steps)])

    def to_lower(value, steps):
        return lax.ppermute(value, "fsdp", [(i + steps, i) for i in range(shards - steps)])

    def with_lower(kv):
        return [kv] + [to_higher(kv, s) for s in range(1, shards)]

    own_rows = inputs.reshape(trees * per_tree, D)
    entered = [
        entry(m, trees, own_rows, norms[0], dn_attn, up_attn_, attn_full) for m in range(trees)
    ]
    own_kv = jnp.concatenate([part[2] for part in entered], axis=0)
    blocks = with_lower(own_kv)
    attended = ()
    for m, (a, u1, _) in enumerate(entered):
        q = queries(m, a, u1, up_attn_, attn_full)
        attended = attention_forward(m, trees, q, blocks, biases[m][0], attended)
    x2, b = mixing(attended[0], own_rows, norms[1], dn_out, up_out_, held, part)
    g = mlp_up(b, held, part, up_up_, dn_up)
    of_last = [
        lax.ppermute(value, "section", [(1, 0)])
        for value in (norms[0], dn_attn, up_attn_[:, D:], attn_full[:, D:])
    ]
    bias = jnp.concatenate([pair[1] for pair in biases], axis=0)
    g, of_last = lax.optimization_barrier((g, of_last))
    *sent, sent_kv = mlp_down(trees, g, x2, down_full, dn_down, up_down_, of_last)
    arrived_kv = lax.ppermute(sent_kv, "section", [(0, 1)])
    sent, arrived_kv = lax.optimization_barrier((sent, arrived_kv))
    arrived = [lax.ppermute(rows, "section", [(0, 1)]) for rows in sent]
    blocks = with_lower(jnp.where(section == 0, own_kv, arrived_kv))
    entered = ()
    for m in range(trees):
        rows = arrived[m]
        if m:
            rows, entered = lax.optimization_barrier((rows, entered))
        entered = enter(
            m, trees, own_rows, rows, is_first, norms[0], dn_attn, up_attn_, attn_full, blocks,
            biases[m][0], entered,
        )
    o, lse, q, x, a, u1 = entered
    layer_out, x2, b, g, gp, u2, u3, u4 = forward_rest(
        trees, o, x, norms[1], held, part, down_full, maps
    )
    def scattered(slabs):
        return lax.psum_scatter(slabs, "fsdp", scatter_dimension=0)

    def permuted(slabs):
        total = lax.dynamic_index_in_dim(slabs, shard, 0, keepdims=False).astype(F32)
        for k in range(1, shards):
            part = lax.dynamic_index_in_dim(slabs, lax.rem(shard + k, shards), 0, keepdims=False)
            total = total + shifted(part, "fsdp", k).astype(F32)
        return total.astype(BF)

    def all_replicas(total):
        return [total] + [shifted(total, "replica", i) for i in range(1, members)]

    own_grads = cotangent.reshape(trees * per_tree, D)
    order = lax.rem(member - jnp.arange(members, dtype=jnp.int32) + members, members)
    cyclic = owners.reshape(members, trees)[order].reshape(-1)
    early_ones, late_ones = tuple(range(2, len(stacks))), (0, 1)

    def columns(order):
        return [(i, sum(widths[j] for j in order[:at]), widths[i]) for at, i in enumerate(order)]

    in_grads, sums, arrived, before, total, ready = [], [], None, None, None, None
    for step in range(trees + 1):
        tree = jnp.clip(step - 1 + section, 0, trees - 1)
        which = jnp.stack([section, tree]).astype(jnp.int32)
        if arrived is None:
            which = jnp.array([1, 0], jnp.int32)
        total = None
        if ready is not None:
            arrived, ready = lax.optimization_barrier((arrived, ready))
            in_grads.append(ready[0])
            total = scattered(ready[1])
        dr, do, slab = backward_rest(
            which, own_grads, b, x2, norms[1], held, part, down_full, g, gp, u2, u3, u4,
            o, maps, arrived,
        )
        if total is not None:
            do, total = lax.optimization_barrier((do, total))
            total = all_replicas(total)
        early_sum = scattered(slab) if step == trees else None
        dq, dkv = attention_backward(which, q, do, o, blocks, bias, lse)
        dkv = [dkv[0]] + [to_lower(dkv[s], s) for s in range(1, shards)]
        if total is not None:
            dq, total = lax.optimization_barrier((dq, total))
            sums.append((step - 2, total, columns(early_ones + late_ones)))
        da, du = query_leaving(which, dq, up_attn_, attn_full)
        if early_sum is not None:
            da, early_sum = lax.optimization_barrier((da, early_sum))
        dx, late = leaving(
            which, dq, da, du, dkv, a, u1, x, dr, norms[0], dn_attn, up_attn_, attn_full, shards
        )
        if step < trees:
            arrived = lax.ppermute(dx, "section", [(1, 0)])
        now = (dx, slab, late)
        ready = None
        if 0 < step < trees:
            dx_ready, *grads = (
                jnp.where(section == 1, was, new) for was, new in zip(before, now)
            )
            ready = (dx_ready, jnp.concatenate(grads, axis=2))
        before = now
    in_grads.append(dx)
    early_sums, late = lax.optimization_barrier((all_replicas(early_sum), late))
    sums.append((trees - 1, early_sums, columns(early_ones)))
    sums.append((trees - 1, all_replicas(permuted(late)), columns(late_ones)))
    placed = place(cyclic, sums, trees, widths, down_attn.shape[1])
    finals = [grad[None] for grad in placed]
    return (
        layer_out.reshape(1, trees, per_tree, D),
        jnp.stack(in_grads)[None],
        *finals,
    )


def solution(mesh):
    rows = P(None, ("replica", "fsdp"), None)
    stack = P("section", None, None, "fsdp")
    placed = (
        (rows, rows)
        + (P("section", None, None),) * 2
        + (P("section", None, "fsdp"),) * 3
        + (P("section", "fsdp", None),)
        + (stack,) * 8
        + (P(None, "replica", None),) * 3
    )
    return jax.shard_map(
        local,
        mesh=mesh,
        in_specs=placed,
        out_specs=(P("section", None, ("replica", "fsdp"), None),) * 2 + (stack,) * 8,
        check_vma=False,
    )
```
